256 devices in a mesh: dp: 8 (over x, core), vocab: 32 (over z, y).
Axes of the slice: x: 4, y: 4, z: 8, core: 2. Of those that a mesh axis runs over, the one named last changes fastest.
Arguments:
- hidden: bfloat16 [1024, 8192], P('dp', 'vocab'), may hold values from -500 to 500, as said below
- norm_gain: float32 [8192], replicated, may hold values from 0.5 to 1.5
- head_weight: bfloat16 [65536, 8192], P('vocab', 'dp'), may hold values from -1 to 1
- target_logits: bfloat16 [1024, 65536], P('dp', 'vocab'), may hold values from -20 to 400
- valid_rows: int32 [1024], P('dp'), may hold values from 0 to 1, as said below
- parents: int32 [1024], P('dp'), may hold values from 0 to 62, as said below
- features: bfloat16 [1024, 24576], P('dp', 'vocab'), may hold values from -0.29882812 to 0.29882812
Outputs:
- grad_hidden: bfloat16 [1024, 8192], P('vocab', 'dp')
- grad_joining: float32 [8192, 24576], P('dp', 'vocab')
The draws below stay inside these ranges and needn't reach their ends.
Inputs may be any that keep to these rules, and one draw needn't show every extreme that they name: hidden is finite; in some draws a few rows are far from the others. `valid_rows`: row 0 is always valid. `parents`: rows form trees of 64 rows aligned on multiples of 64; a tree's first row has parent 0, every other row a parent before it in its tree, and the last row of each tree has parent 64 - 2.
All inputs are finite; a program needn't handle non-finite values.
Results may differ from the reference program's by a relative error of at most 0.007.
Values may be sent and summed in bfloat16 or wider, within the bound.
A program may use at most 64 MiB of HBM per device.

```python
import math
import jax
import jax.numpy as jnp
from jax import lax

D = 8192
TREE = 64
ROWS_DEV = 128
VOCAB = 65536
ROWS = 1024
JOINED = 24576


def draw_hidden(key, part):
    base_key = jax.random.fold_in(key, 1)
    key_noise, key_rows, key_cols = jax.random.split(base_key, 3)
    col_scale = jnp.exp(jax.random.uniform(key_cols, (1, D), jnp.float32) * math.log(10.0))
    row_scale = jnp.exp(jax.random.uniform(key_rows, (ROWS, 1), jnp.float32) * math.log(10.0))
    values = jax.random.normal(key_noise, (ROWS, D), jnp.float32) * col_scale * row_scale
    return jnp.clip(values, -500.0, 500.0).astype(jnp.bfloat16)


def draw_head_weight(key, part):
    key_noise = jax.random.fold_in(key, 2)
    spread = 3.0 / math.sqrt(D)
    values = jnp.clip(jax.random.normal(key_noise, (VOCAB, D), jnp.float32), -6.0, 6.0) * spread
    return jnp.clip(values, -0.3, 0.3).astype(jnp.bfloat16)


def draw_target_logits(key, part):
    key_noise = jax.random.fold_in(key, 3)
    values = jnp.clip(jax.random.normal(key_noise, (ROWS, VOCAB), jnp.float32) * 3.0, -18.0, 18.0)
    return values.astype(jnp.bfloat16)


def draw_valid_rows(key, part):
    picks = jax.random.randint(jax.random.fold_in(key, 4), (ROWS,), 0, 1000)
    positions = jnp.arange(ROWS, dtype=jnp.int32)
    threshold = 250 + 700 * positions // ROWS
    chosen = (picks < threshold).astype(jnp.int32)
    return jnp.where(positions == 0, 1, chosen).astype(jnp.int32)


def draw_parents(key, part):
    position = jnp.arange(ROWS, dtype=jnp.int32) % TREE
    upper = jnp.maximum(position, 1)
    picks = jax.random.randint(jax.random.fold_in(key, 5), (ROWS,), 0, upper)
    picks = jnp.where(position == TREE - 1, TREE - 2, picks)
    picks = jnp.where(position == 0, 0, picks)
    return picks.astype(jnp.int32)


def shard_levels(key, extent, cuts, smallest, high):
    gain = 1.0
    for dim, parts in cuts:
        steps = jax.random.uniform(jax.random.fold_in(jax.random.fold_in(key, 6), dim), (parts,), jnp.float32, smallest / len(cuts), high / len(cuts))
        gain = gain * jnp.repeat(jnp.exp(steps), extent[dim] // parts).reshape((-1,) + (1,) * (len(extent) - 1 - dim))
    return gain


def scatter_about(own_key, extent, scale, bound, shards=(), kind=jnp.bfloat16):
    gain = shard_levels(own_key, extent, shards, -0.22, 0.18) if shards else 1.0
    result = jax.random.normal(own_key, extent, jnp.float32) * scale * gain
    return jnp.minimum(jnp.maximum(result, -bound), bound).astype(kind)


def setup_inputs(seed: int = 0) -> dict:
    splits = jax.random.split(jax.random.key(seed), 8)
    hidden = draw_hidden(jax.random.fold_in(splits[7], 71), 0)
    norm_gain = jnp.clip(1.0 + 0.1 * jax.random.normal(splits[1], (D,), jnp.float32), 0.5, 1.5)
    head_weight = draw_head_weight(jax.random.fold_in(splits[7], 71), 0)
    target_logits = draw_target_logits(jax.random.fold_in(splits[7], 71), 0)
    valid_rows = draw_valid_rows(jax.random.fold_in(splits[7], 71), 0)
    parents = draw_parents(jax.random.fold_in(splits[7], 71), 0)
    features = scatter_about(splits[6], (ROWS, JOINED), 0.05, 0.29882812, ((0, 8), (1, 32)))
    return dict(hidden=hidden, norm_gain=norm_gain, head_weight=head_weight, target_logits=target_logits, valid_rows=valid_rows, parents=parents, features=features)


def reference(hidden, norm_gain, head_weight, target_logits, valid_rows, parents, features):
    values = hidden.astype(jnp.float32)
    row_factor = lax.rsqrt(lax.optimization_barrier(jnp.mean(values * values, axis=1)) + 1e-05)
    normed = (values * row_factor[:, None] * norm_gain).astype(jnp.bfloat16)
    live_rows = (valid_rows == 1).astype(jnp.float32)
    valid_count = jnp.sum(live_rows)
    row_weight = 1048576.0 * live_rows / valid_count
    block_count = ROWS // ROWS_DEV

    def one_block(inputs):
        normed_block, target_block, weight_block = inputs
        logits = lax.dot_general(normed_block, head_weight, (((1,), (1,)), ((), ())), preferred_element_type=jnp.float32)
        draft_max = lax.optimization_barrier(jnp.max(logits, axis=1, keepdims=True))
        draft_exp = jnp.exp(logits - draft_max)
        draft_probs = draft_exp / lax.optimization_barrier(jnp.sum(draft_exp, axis=1, keepdims=True))
        targets = target_block.astype(jnp.float32)
        target_max = lax.optimization_barrier(jnp.max(targets, axis=1, keepdims=True))
        target_exp = jnp.exp(targets - target_max)
        target_probs = target_exp / lax.optimization_barrier(jnp.sum(target_exp, axis=1, keepdims=True))
        logit_grad = (weight_block[:, None] * (draft_probs - target_probs)).astype(jnp.bfloat16)
        return jnp.dot(logit_grad, head_weight, preferred_element_type=jnp.float32)
    normed_grad = lax.map(one_block, (normed.reshape(block_count, ROWS_DEV, D), target_logits.reshape(block_count, ROWS_DEV, VOCAB), row_weight.reshape(block_count, ROWS_DEV)))
    normed_grad = normed_grad.reshape(ROWS, D)
    row_dot = lax.optimization_barrier(jnp.sum(norm_gain * values * normed_grad, axis=1))
    grad_hidden = (row_factor[:, None] * norm_gain * normed_grad - values * (row_factor ** 3 * row_dot / D)[:, None]).astype(jnp.bfloat16)
    source_rows = jnp.arange(ROWS, dtype=jnp.int32) // TREE * TREE + parents.astype(jnp.int32)
    chosen = jnp.take(features, source_rows, axis=0)
    grad_joining = jnp.dot(grad_hidden.T, chosen, preferred_element_type=jnp.float32)
    return (grad_hidden, grad_joining)
```

```python
import functools

import jax
import jax.numpy as jnp
from jax import lax
from jax.experimental import pallas as pl
from jax.experimental.pallas import tpu as pltpu
from jax.sharding import PartitionSpec as P

TREE = 64
NX, NC, NY, NZ = 4, 2, 4, 8
F32, BF16 = jnp.float32, jnp.bfloat16
DMA = pltpu.SemaphoreType.DMA


def remote(src, dst, send_sem, recv_sem, device):
    return pltpu.make_async_remote_copy(
        src_ref=src,
        dst_ref=dst,
        send_sem=send_sem,
        recv_sem=recv_sem,
        device_id=device,
        device_id_type=pl.DeviceIdType.MESH,
    )


class Place:
    def __init__(self):
        self.g = lax.axis_index("dp")
        self.v = lax.axis_index("vocab")
        self.x, self.c = self.g // NC, self.g % NC
        self.z, self.y = self.v // NY, self.v % NY

    def dp(self, i):
        return (i, self.v)

    def at_x(self, x):
        return (x * NC + self.c, self.v)

    def partner(self):
        return (self.x * NC + 1 - self.c, self.v)

    def at_y(self, y):
        return (self.g, self.z * NY + y)

    def at_z(self, z):
        return (self.g, z * NY + self.y)


def greet(peers):
    barrier = pltpu.get_barrier_semaphore()
    for peer in peers:
        pl.semaphore_signal(
            barrier, inc=1, device_id=peer, device_id_type=pl.DeviceIdType.MESH
        )
    pl.semaphore_wait(barrier, len(peers))


class Sender:
    def __init__(self, sems):
        self.sems, self.used, self.copies = sems, 0, []

    def __call__(self, src, dst, recv_sem, device):
        copy = remote(src, dst, self.sems.at[self.used], recv_sem, device)
        self.used += 1
        copy.start()
        self.copies.append(copy)

    def drain(self):
        for copy in self.copies:
            copy.wait_send()


def arrived(dst, recv_sem, device, any_sem):
    remote(dst, dst, any_sem, recv_sem, device).wait_recv()


class Gather:
    def __init__(self, at, buf, send, near, far, pair):
        self.at, self.buf, self.send = at, buf, send
        self.near, self.far, self.pair = near, far, pair

    def slot(self, step, core):
        return ((self.at.x + step) % NX) * NC + core

    def start(self, half):
        at, buf = self.at, self.buf
        mine = buf.at[at.g, half]
        self.send(mine, mine, self.near.at[0, half], at.at_x((at.x + 1) % NX))
        self.send(mine, mine, self.near.at[1, half], at.at_x((at.x + 3) % NX))
        self.send(mine, mine, self.pair.at[0, half], at.partner())

    def middle(self):
        at, buf = self.at, self.buf
        for half in range(2):
            for side, step in ((0, 3), (1, 1)):
                block = buf.at[self.slot(step, at.c), half]
                arrived(block, self.near.at[side, half], at.partner(), self.near.at[side, half])
                if half == side:
                    onward = at.at_x((at.x + (1 if side == 0 else 3)) % NX)
                    self.send(block, block, self.far.at[half], onward)
                self.send(block, block, self.pair.at[step, half], at.partner())

    def last(self):
        at, buf = self.at, self.buf
        for half in range(2):
            block = buf.at[self.slot(2, at.c), half]
            arrived(block, self.far.at[half], at.partner(), self.far.at[half])
            self.send(block, block, self.pair.at[2, half], at.partner())

    def paired(self, step):
        at = self.at
        for half in range(2):
            block = self.buf.at[self.slot(step, 1 - at.c), half]
            arrived(block, self.pair.at[step, half], at.partner(), self.pair.at[step, half])


GATHER_SENDS = 14


def row_tile(column):
    return jnp.transpose(jnp.broadcast_to(column, (128, 128)))[0:8]


def column_tile(row):
    return jnp.transpose(jnp.broadcast_to(row, (128, 128)))


def stack_rows(*rows):
    index = lax.broadcasted_iota(jnp.int32, (8, 128), 0)
    tile = jnp.zeros((8, 128), F32)
    for k, row in enumerate(rows):
        tile = jnp.where(index == k, row, tile)
    return tile


def spread_kernel(
    hid, live, gain, feat,
    n_out, vals_out, rf_out, f_out,
    zbuf, xall, stat, cols,
    send_sems, f_sems, zr, xs, xr, yr, y2, sr, fr, own_sems,
    f_near, f_far, f_pair,
):
    at = Place()
    x, c, y, z, g = at.x, at.c, at.y, at.z, at.g
    up_z, down_z = at.at_z((z + 1) % NZ), at.at_z((z + NZ - 1) % NZ)
    up_y, down_y = at.at_y((y + 1) % NY), at.at_y((y + 3) % NY)
    greet(
        [at.dp((g + k) % 8) for k in range(1, 8)]
        + [up_z, down_z]
        + [at.at_y((y + k) % NY) for k in range(1, NY)]
    )
    send = Sender(send_sems)
    spread = Gather(at, f_out, Sender(f_sems), f_near, f_far, f_pair)
    own_feat = pltpu.make_async_copy(feat, f_out.at[g], own_sems.at[0])
    own_feat.start()

    def to_slice(src, j):
        @pl.when(j != g)
        def _():
            remote(src, xall.at[y, g], xs.at[j], xr.at[g], at.dp(j)).start()

        @pl.when(j == g)
        def _():
            pltpu.make_async_copy(src, xall.at[y, g], xs.at[j]).start()

    for step in range(5):
        low, high = (z + NZ - step) % NZ, (z + step) % NZ
        if step > 0:
            arrived(zbuf.at[low], zr.at[low], up_z, zr.at[low])
        src = hid if step == 0 else zbuf.at[low]
        if step < 4:
            send(src, zbuf.at[low], zr.at[low], up_z)
        to_slice(src, low)
        if step == 0:
            send(hid, zbuf.at[high], zr.at[high], down_z)
        elif step < 4:
            arrived(zbuf.at[high], zr.at[high], up_z, zr.at[high])
            if step < 3:
                send(zbuf.at[high], zbuf.at[high], zr.at[high], down_z)
            to_slice(zbuf.at[high], high)

    own_feat.wait()
    for half in range(2):
        spread.start(half)
    squares = jnp.square(hid[...].astype(F32))
    for k in range(1, NZ):
        squares = squares + jnp.square(zbuf[(z + k) % NZ].astype(F32))
    stat[y] = row_tile(jnp.sum(squares, axis=1, keepdims=True))
    for k in range(1, NY):
        send(stat.at[y], stat.at[y], sr.at[y], at.at_y((y + k) % NY))

    for i in range(8):
        block = xall.at[y, i]

        @pl.when(g != i)
        def _():
            arrived(block, xr.at[i], up_y, xr.at[i])

        @pl.when(g == i)
        def _():
            pltpu.make_async_copy(hid, block, xs.at[i]).wait()

        send(block, block, yr.at[0, i], up_y)
        send(block, block, yr.at[1, i], down_y)

    total = stat[y]
    for k in range(1, NY):
        other = (y + k) % NY
        arrived(stat.at[other], sr.at[other], up_y, sr.at[other])
        total = total + stat[other]
    factor = lax.rsqrt(total / (1024.0 * 8) + 1e-05)
    rf_out[g] = stack_rows(factor[0:1], live[...])
    for k in range(1, 8):
        other = (g + k) % 8
        send(rf_out.at[g], rf_out.at[g], fr.at[g], at.dp(other))

    spread.middle()
    for i in range(8):
        for side, step in ((0, 3), (1, 1)):
            block = xall.at[(y + step) % NY, i]
            arrived(block, yr.at[side, i], up_y, yr.at[side, i])
            if (i < 4) == (side == 0):
                send(block, block, y2.at[i], up_y if side == 0 else down_y)
    spread.last()
    for k in range(1, 8):
        other = (g + k) % 8
        arrived(rf_out.at[other], fr.at[other], up_y, fr.at[other])
    for i in range(8):
        cols[i] = column_tile(rf_out[i, 0:1])
    for i in range(8):
        block = xall.at[(y + 2) % NY, i]
        arrived(block, y2.at[i], up_y, y2.at[i])

    @pl.loop(0, 8)
    def _(i):
        scale = cols[i]
        scale = jnp.concatenate([scale, scale], axis=1)
        rows = pl.ds(pl.multiple_of(i * 128, 128), 128)
        for part in range(NY):
            columns = slice(part * 256, part * 256 + 256)
            values = xall[part, i].astype(F32)
            n_out[rows, columns] = (values * scale * gain[:, columns]).astype(BF16)

    for part in range(NY):
        vals_out[:, part * 256 : part * 256 + 256] = xall[
            part, z, pl.ds(pl.multiple_of(y * 32, 32), 32), :
        ]
    for step in range(4):
        spread.paired(step)
    send.drain()
    spread.send.drain()
    for j in range(8):

        @pl.when(g != j)
        def _():
            remote(hid, xall.at[y, g], xs.at[j], xr.at[g], at.dp(j)).wait_send()


def main_kernel(
    normed, weight, targets, rf, vals, gain,
    share_out, grad_out,
    pk, pr, sb, rl, fin, lg, tst, stat_y, stat_z, gbuf, pf, ysb, yrl, yfin,
    qown, qs, zrs, rds, rdr, rfcol,
    pair_s, pair_r, sb_s, rl_r, fin_r,
    send_sems, sty, stz, g_sems, g_near, g_far, g_pair,
    yrl_r, yfin_r, zs_s, zs_r, rd_r, a_z, a_y, a_y2,
):
    at = Place()
    x, c, y, z, g = at.x, at.c, at.y, at.z, at.g
    up_z, down_z = at.at_z((z + 1) % NZ), at.at_z((z + NZ - 1) % NZ)
    up_y, down_y = at.at_y((y + 1) % NY), at.at_y((y + 3) % NY)
    greet(
        [at.dp((g + k) % 8) for k in range(1, 8)]
        + [at.at_z((z + k) % NZ) for k in range(1, NZ)]
        + [at.at_y((y + k) % NY) for k in range(1, NY)]
    )
    send = Sender(send_sems)

    def multiply(t):
        tile = pl.ds(pl.multiple_of(t * 256, 256), 256)
        for d in range(NX):
            part = lax.dot_general(
                normed[d * 256 : d * 256 + 256, :],
                weight[tile, :],
                (((1,), (1,)), ((), ())),
                preferred_element_type=F32,
            )
            pk[t, 0, d] = part[:128]
            pk[t, 1, d] = part[128:]
        remote(
            pk.at[t, 1 - c], pr.at[t], pair_s.at[t], pair_r.at[t], at.partner()
        ).start()

    def hops(t):
        way = 1 + 2 * (t % 2)
        return (x + way) % NX, (x + 4 - way) % NX

    def direct(t, started):
        ahead, back = hops(t)
        return (
            remote(sb.at[t, 0], rl.at[t], sb_s.at[t, 0], rl_r.at[t], at.at_x(ahead)),
            remote(sb.at[t, 1], fin.at[t, 0], sb_s.at[t, 1], fin_r.at[t, 0], at.at_x(back)),
        )

    def onward(t):
        ahead, _ = hops(t)
        return remote(sb.at[t, 2], fin.at[t, 1], sb_s.at[t, 2], fin_r.at[t, 1], at.at_x(ahead))

    def encode(t, k, value):
        top = jnp.max(jnp.abs(value), axis=0, keepdims=True)
        step = (120.0 / jnp.maximum(top, 1e-30)).astype(BF16)
        sb[t, k, 128:] = jnp.broadcast_to(step, (16, 256))
        step = sb[t, k, 128:].astype(F32)[0:1]
        sb[t, k, :128] = jnp.exp2(value * step).astype(BF16)

    def decode(block):
        step = block[128:].astype(F32)[0:1]
        return jnp.log2(block[:128].astype(F32)) * (1.0 / step)

    def pair_sum(t):
        ahead, back = hops(t)
        far = (x + 2) % NX
        arrived(pr.at[t], pair_r.at[t], at.partner(), pair_r.at[t])
        encode(t, 0, pk[t, c, far] + pr[t, far])
        encode(t, 1, pk[t, c, back] + pr[t, back])
        for copy in direct(t, True):
            copy.start()

    def relay(t):
        ahead, _ = hops(t)
        arrived(rl.at[t], rl_r.at[t], at.partner(), rl_r.at[t])
        encode(t, 2, pk[t, c, ahead] + pr[t, ahead] + decode(rl.at[t]))
        onward(t).start()

    def finish(t):
        for k in range(2):
            arrived(fin.at[t, k], fin_r.at[t, k], at.partner(), fin_r.at[t, k])
        lg[t] = pk[t, c, x] + pr[t, x] + decode(fin.at[t, 0]) + decode(fin.at[t, 1])

    @pl.loop(0, 11)
    def _(t):
        @pl.when(t < 8)
        def _():
            multiply(t)

        @pl.when((t >= 1) & (t < 9))
        def _():
            pair_sum(t - 1)

        @pl.when((t >= 2) & (t < 10))
        def _():
            relay(t - 2)

        @pl.when(t >= 3)
        def _():
            finish(t - 3)

        @pl.when(t == 8)
        def _():
            top = jnp.max(targets[...].astype(F32), axis=1, keepdims=True)
            part = jnp.zeros((128, 256), F32)
            for k in range(8):
                part = part + jnp.exp(targets[:, k * 256 : k * 256 + 256].astype(F32) - top)
            tst[...] = stack_rows(
                jnp.zeros((1, 128), F32),
                jnp.zeros((1, 128), F32),
                row_tile(top)[0:1],
                row_tile(jnp.sum(part, axis=1, keepdims=True))[0:1],
            )

    top = lg[0]
    for t in range(1, 8):
        top = jnp.maximum(top, lg[t])
    top = jnp.max(top, axis=1, keepdims=True)
    part = jnp.zeros((128, 256), F32)
    for t in range(8):
        part = part + jnp.exp(lg[t] - top)
    stat_y[y] = stack_rows(
        row_tile(top)[0:1],
        row_tile(jnp.sum(part, axis=1, keepdims=True))[0:1],
        tst[2:3],
        tst[3:4],
    )
    for k in range(1, NY):
        send(stat_y.at[y], stat_y.at[y], sty.at[y], at.at_y((y + k) % NY))

    def combine(tiles):
        out = []
        for k in (0, 2):
            m = tiles[0][k : k + 1]
            for tile in tiles[1:]:
                m = jnp.maximum(m, tile[k : k + 1])
            s = jnp.zeros((1, 128), F32)
            for tile in tiles:
                s = s + tile[k + 1 : k + 2] * jnp.exp(tile[k : k + 1] - m)
            out += [m, s]
        return out

    tiles = [stat_y[y]]
    for k in range(1, NY):
        other = (y + k) % NY
        arrived(stat_y.at[other], sty.at[other], up_y, sty.at[other])
        tiles.append(stat_y[other])
    stat_z[z] = stack_rows(*combine(tiles))
    for k in range(1, NZ):
        send(stat_z.at[z], stat_z.at[z], stz.at[z], at.at_z((z + k) % NZ))
    tiles = [stat_z[z]]
    for k in range(1, NZ):
        other = (z + k) % NZ
        arrived(stat_z.at[other], stz.at[other], up_y, stz.at[other])
        tiles.append(stat_z[other])
    draft_max, draft_sum, target_max, target_sum = combine(tiles)
    live = jnp.zeros((1, 128), F32)
    for i in range(8):
        live = live + rf[i, 1:2]
    count = jnp.sum(live, axis=1, keepdims=True)
    scale = 1048576.0 * rf[g][1:2] / count
    wide = lambda row: jnp.concatenate([column_tile(row)] * 2, axis=1)
    draft_top, target_top = wide(draft_max), wide(target_max)
    draft_scale, target_scale = wide(1.0 / draft_sum), wide(1.0 / target_sum)
    scale = wide(scale)

    gather = Gather(at, gbuf, Sender(g_sems), g_near, g_far, g_pair)
    for t in range(8):
        draft = jnp.exp(lg[t] - draft_top) * draft_scale
        target = (
            jnp.exp(targets[:, t * 256 : t * 256 + 256].astype(F32) - target_top)
            * target_scale
        )
        column = (t % 4) * 256
        gbuf[g, t // 4, :, column : column + 256] = (scale * (draft - target)).astype(BF16)
        if t % 4 == 3:
            gather.start(t // 4)

    def backward(k, step):
        block = pl.ds(((x + step) % NX) * NC, 2)

        @pl.loop(0, 4)
        def _(n):
            columns = pl.ds(pl.multiple_of(n * 256, 256), 256)
            part = jnp.zeros((256, 256), F32)
            for half in range(2):
                part = part + jnp.dot(
                    gbuf[block, half].reshape(256, 1024),
                    weight[half * 1024 : half * 1024 + 1024, columns],
                    preferred_element_type=F32,
                )
            for which in range(2):
                for dest in range(NY):
                    row = which * 128 + dest * 32
                    pf[k, dest, which, :, columns] = part[row : row + 32]

    def y_first(k):
        way = 1 if k % 2 == 0 else 3
        ysb[k, 0] = pf[k, (y + 2) % NY].astype(BF16)
        send(ysb.at[k, 0], yrl.at[k], yrl_r.at[k], at.at_y((y + way) % NY))
        ysb[k, 1] = pf[k, (y + 4 - way) % NY].astype(BF16)
        send(ysb.at[k, 1], yfin.at[k, 0], yfin_r.at[k, 0], at.at_y((y + 4 - way) % NY))

    def y_second(k):
        way = 1 if k % 2 == 0 else 3
        arrived(yrl.at[k], yrl_r.at[k], up_y, yrl_r.at[k])
        ysb[k, 2] = (pf[k, (y + way) % NY] + yrl[k].astype(F32)).astype(BF16)
        send(ysb.at[k, 2], yfin.at[k, 1], yfin_r.at[k, 1], at.at_y((y + way) % NY))

    def z_send(dest):
        return remote(qs.at[dest], zrs.at[z], zs_s.at[dest], zs_r.at[z], at.at_z(dest))

    def y_third(k, step):
        for j in range(2):
            arrived(yfin.at[k, j], yfin_r.at[k, j], up_y, yfin_r.at[k, j])
        for which in range(2):
            dest = ((x + step) % NX) * 2 + which
            value = (
                pf[k, y, which]
                + yfin[k, 0, which].astype(F32)
                + yfin[k, 1, which].astype(F32)
            )

            @pl.when(dest == z)
            def _():
                qown[...] = value

            @pl.when(dest != z)
            def _():
                qs[dest] = value.astype(BF16)
                z_send(dest).start()

    gather.paired(0)
    backward(0, 0)
    y_first(0)
    gather.middle()
    gather.paired(3)
    backward(1, 3)
    y_first(1)
    y_second(0)
    gather.paired(1)
    backward(2, 1)
    y_first(2)
    y_second(1)
    y_third(0, 0)
    gather.last()
    gather.paired(2)
    backward(3, 2)
    y_first(3)
    y_second(2)
    y_third(1, 3)
    y_second(3)
    y_third(2, 1)
    y_third(3, 2)

    values = vals[...].astype(F32)
    rfcol[...] = column_tile(rf[z][0:1])
    factor = rfcol[pl.ds(pl.multiple_of(y * 32, 32), 32), :]
    total = qown[...]
    for k in range(1, NZ):
        other = (z + k) % NZ
        arrived(zrs.at[other], zs_r.at[other], up_y, zs_r.at[other])
        total = total + zrs[other].astype(F32)
    dot = jnp.sum(gain[...] * values * total, axis=1, keepdims=True)
    dot = jnp.broadcast_to(dot, (32, 128))
    rds[...] = dot
    for k in range(1, 8):
        send(rds, rdr.at[g], rd_r.at[g], at.dp((g + k) % 8))
    for k in range(1, 8):
        other = (g + k) % 8
        arrived(rdr.at[other], rd_r.at[other], up_y, rd_r.at[other])
        dot = dot + rdr[other]
    pull = factor * factor * factor * dot / (1024.0 * 8)
    broad = lambda tile: jnp.concatenate([tile] * 8, axis=1)
    grad = (broad(factor) * gain[...] * total - values * broad(pull)).astype(BF16)
    share_out[...] = grad
    grad_out[z, y] = grad

    order = []

    def to_y(block_z):
        k = len(order)
        block = grad_out.at[block_z, y]
        send(block, block, a_y.at[0, k], up_y)
        send(block, block, a_y.at[1, k], down_y)
        order.append(block_z)

    done = [0]

    def pass_y(count):
        while done[0] < count:
            k = done[0]
            for side, step in ((0, 3), (1, 1)):
                block = grad_out.at[order[k], (y + step) % NY]
                arrived(block, a_y.at[side, k], up_y, a_y.at[side, k])
                if k % 2 == side:
                    send(block, block, a_y2.at[k], up_y if side == 0 else down_y)
            done[0] += 1

    for step in range(5):
        low, high = (z + NZ - step) % NZ, (z + step) % NZ
        block = grad_out.at[low, y]
        if step > 0:
            arrived(block, a_z.at[low], up_z, a_z.at[low])
        if step < 4:
            send(block, block, a_z.at[low], up_z)
        if step == 0:
            send(block, block, a_z.at[high], down_z)
        to_y(low)
        if 0 < step < 4:
            block = grad_out.at[high, y]
            arrived(block, a_z.at[high], up_z, a_z.at[high])
            if step < 3:
                send(block, block, a_z.at[high], down_z)
            to_y(high)
        if step > 0:
            pass_y(max(0, 2 * step - 1))
    pass_y(8)
    for k in range(8):
        block = grad_out.at[order[k], (y + 2) % NY]
        arrived(block, a_y2.at[k], up_y, a_y2.at[k])

    @pl.loop(0, 8)
    def _(t):
        remote(
            pk.at[t, 1 - c], pr.at[t], pair_s.at[t], pair_r.at[t], at.partner()
        ).wait_send()
        for copy in direct(t, False):
            copy.wait_send()
        onward(t).wait_send()

    send.drain()
    gather.send.drain()
    for k in range(1, NZ):
        z_send((z + k) % NZ).wait_send()


VMEM = pl.BlockSpec(memory_space=pltpu.VMEM)
LIMIT = 60 * 1024 * 1024


def spread_call(hidden, live, gain, feat):
    return pl.pallas_call(
        spread_kernel,
        out_shape=(
            jax.ShapeDtypeStruct((1024, 1024), BF16),
            jax.ShapeDtypeStruct((32, 1024), BF16),
            jax.ShapeDtypeStruct((8, 8, 128), F32),
            jax.ShapeDtypeStruct((8, 2, 64, 768), BF16),
        ),
        in_specs=[VMEM] * 4,
        out_specs=[VMEM] * 4,
        scratch_shapes=[
            pltpu.VMEM((NZ, 128, 256), BF16),
            pltpu.VMEM((NY, 8, 128, 256), BF16),
            pltpu.VMEM((NY, 8, 128), F32),
            pltpu.VMEM((8, 128, 128), F32),
            DMA((41,)),
            DMA((GATHER_SENDS,)),
            DMA((NZ,)),
            DMA((8,)),
            DMA((8,)),
            DMA((2, 8)),
            DMA((8,)),
            DMA((NY,)),
            DMA((8,)),
            DMA((1,)),
            DMA((2, 2)),
            DMA((2,)),
            DMA((4, 2)),
        ],
        compiler_params=pltpu.CompilerParams(
            collective_id=0, has_side_effects=True, vmem_limit_bytes=LIMIT
        ),
    )(hidden, live, gain, feat)


def main_call(normed, weight, targets, rf, vals, gain):
    return pl.pallas_call(
        main_kernel,
        out_shape=(
            jax.ShapeDtypeStruct((32, 1024), BF16),
            jax.ShapeDtypeStruct((NZ, NY, 32, 1024), BF16),
        ),
        in_specs=[VMEM] * 6,
        out_specs=[VMEM] * 2,
        scratch_shapes=[
            pltpu.VMEM((8, 2, NX, 128, 256), F32),
            pltpu.VMEM((8, NX, 128, 256), F32),
            pltpu.VMEM((8, 3, 144, 256), BF16),
            pltpu.VMEM((8, 144, 256), BF16),
            pltpu.VMEM((8, 2, 144, 256), BF16),
            pltpu.VMEM((8, 128, 256), F32),
            pltpu.VMEM((8, 128), F32),
            pltpu.VMEM((NY, 8, 128), F32),
            pltpu.VMEM((NZ, 8, 128), F32),
            pltpu.VMEM((8, 2, 128, 1024), BF16),
            pltpu.VMEM((4, NY, 2, 32, 1024), F32),
            pltpu.VMEM((4, 3, 2, 32, 1024), BF16),
            pltpu.VMEM((4, 2, 32, 1024), BF16),
            pltpu.VMEM((4, 2, 2, 32, 1024), BF16),
            pltpu.VMEM((32, 1024), F32),
            pltpu.VMEM((NZ, 32, 1024), BF16),
            pltpu.VMEM((NZ, 32, 1024), BF16),
            pltpu.VMEM((32, 128), F32),
            pltpu.VMEM((8, 32, 128), F32),
            pltpu.VMEM((128, 128), F32),
            DMA((8,)),
            DMA((8,)),
            DMA((8, 3)),
            DMA((8,)),
            DMA((8, 2)),
            DMA((60,)),
            DMA((NY,)),
            DMA((NZ,)),
            DMA((GATHER_SENDS,)),
            DMA((2, 2)),
            DMA((2,)),
            DMA((4, 2)),
            DMA((4,)),
            DMA((4, 2)),
            DMA((NZ,)),
            DMA((NZ,)),
            DMA((8,)),
            DMA((NZ,)),
            DMA((2, 8)),
            DMA((8,)),
        ],
        compiler_params=pltpu.CompilerParams(
            collective_id=1, has_side_effects=True, vmem_limit_bytes=LIMIT
        ),
    )(normed, weight, targets, rf, vals, gain)


def body(hidden, norm_gain, head_weight, target_logits, valid_rows, parents, features):
    group_index = lax.axis_index("dp")
    group_rows = hidden.shape[0]
    gain = lax.dynamic_slice_in_dim(norm_gain, group_index * 1024, 1024).reshape(1, 1024)
    live = (valid_rows == 1).astype(F32).reshape(1, 128)
    tree_rows = jnp.arange(group_rows, dtype=jnp.int32) // TREE * TREE + parents
    chosen = jnp.take(features, tree_rows, axis=0).reshape(2, 64, 768)
    normed, vals, rf, parent_features = spread_call(hidden, live, gain, chosen)
    share, grad = main_call(normed, head_weight, target_logits, rf, vals, gain)
    grad_joining = lax.dot_general(
        grad.reshape(1024, 1024),
        parent_features.reshape(1024, 768),
        (((0,), (0,)), ((), ())),
        preferred_element_type=F32,
    )
    return (share, grad_joining)


def solution(mesh):
    placed = (
        P("dp", "vocab"),
        P(),
        P("vocab", "dp"),
        P("dp", "vocab"),
        P("dp"),
        P("dp"),
        P("dp", "vocab"),
    )
    return jax.shard_map(
        body,
        mesh=mesh,
        in_specs=placed,
        out_specs=(P("vocab", "dp"), P("dp", "vocab")),
        check_vma=False,
    )
```

```python
import contextlib

import jax
import jax.numpy as jnp
from jax import lax
from jax.experimental import pallas as pl
from jax.experimental.pallas import tpu as pltpu
from jax.sharding import PartitionSpec as P

TREE = 64
NX, NC, NY, NZ = 4, 2, 4, 8
F32, BF16 = jnp.float32, jnp.bfloat16
DMA = pltpu.SemaphoreType.DMA


def remote(src, dst, send_sem, recv_sem, device):
    return pltpu.make_async_remote_copy(
        src_ref=src,
        dst_ref=dst,
        send_sem=send_sem,
        recv_sem=recv_sem,
        device_id=device,
        device_id_type=pl.DeviceIdType.MESH,
    )


def phase(name):
    return contextlib.nullcontext()


class Place:
    def __init__(self):
        self.g = lax.axis_index("dp")
        self.v = lax.axis_index("vocab")
        self.x, self.c = self.g // NC, self.g % NC
        self.z, self.y = self.v // NY, self.v % NY

    def dp(self, i):
        return (i, self.v)

    def at_x(self, x):
        return (x * NC + self.c, self.v)

    def partner(self):
        return (self.x * NC + 1 - self.c, self.v)

    def at_y(self, y):
        return (self.g, self.z * NY + y)

    def at_z(self, z):
        return (self.g, z * NY + self.y)


def greet(peers):
    barrier = pltpu.get_barrier_semaphore()
    for peer in peers:
        pl.semaphore_signal(
            barrier, inc=1, device_id=peer, device_id_type=pl.DeviceIdType.MESH
        )
    pl.semaphore_wait(barrier, len(peers))


class Sender:
    def __init__(self, sems):
        self.sems, self.used, self.copies = sems, 0, []

    def __call__(self, src, dst, recv_sem, device):
        assert self.used < self.sems.shape[0]
        copy = remote(src, dst, self.sems.at[self.used], recv_sem, device)
        self.used += 1
        copy.start()
        self.copies.append(copy)

    def drain(self):
        for copy in self.copies:
            copy.wait_send()


def arrived(dst, recv_sem, device, any_sem):
    remote(dst, dst, any_sem, recv_sem, device).wait_recv()


class Gather:
    def __init__(self, at, buf, send, near, far, pair):
        self.at, self.buf, self.send = at, buf, send
        self.near, self.far, self.pair = near, far, pair

    def slot(self, step, core):
        return ((self.at.x + step) % NX) * NC + core

    def start(self, half):
        at, buf = self.at, self.buf
        mine = buf.at[at.g, half]
        self.send(mine, mine, self.near.at[0, half], at.at_x((at.x + 1) % NX))
        self.send(mine, mine, self.near.at[1, half], at.at_x((at.x + 3) % NX))
        self.send(mine, mine, self.pair.at[0, half], at.partner())

    def middle(self):
        at, buf = self.at, self.buf
        for half in range(2):
            for side, step in ((0, 3), (1, 1)):
                block = buf.at[self.slot(step, at.c), half]
                arrived(block, self.near.at[side, half], at.partner(), self.near.at[side, half])
                if half == side:
                    onward = at.at_x((at.x + (1 if side == 0 else 3)) % NX)
                    self.send(block, block, self.far.at[half], onward)
                self.send(block, block, self.pair.at[step, half], at.partner())

    def last(self):
        at, buf = self.at, self.buf
        for half in range(2):
            block = buf.at[self.slot(2, at.c), half]
            arrived(block, self.far.at[half], at.partner(), self.far.at[half])
            self.send(block, block, self.pair.at[2, half], at.partner())

    def paired(self, step):
        at = self.at
        for half in range(2):
            block = self.buf.at[self.slot(step, 1 - at.c), half]
            arrived(block, self.pair.at[step, half], at.partner(), self.pair.at[step, half])


GATHER_SENDS = 14


def row_tile(column):
    return jnp.transpose(jnp.broadcast_to(column, (128, 128)))[0:8]


def column_tile(row):
    return jnp.transpose(jnp.broadcast_to(row, (128, 128)))


def stack_rows(*rows):
    index = lax.broadcasted_iota(jnp.int32, (8, 128), 0)
    tile = jnp.zeros((8, 128), F32)
    for k, row in enumerate(rows):
        tile = jnp.where(index == k, row, tile)
    return tile


def kernel(
    hid, valid, parents, feat, gains, weight_hbm, targets_hbm,
    share_out, grad_out, feat_out,
    weight, targets, zbuf, xall, normed, stat, cols, rf, fall, gain,
    pk, pr, sb, rl, fin, lg, tst, stat_y, stat_z, gbuf, pf, ysb, yrl, yfin,
    qs, zrs, tot, vscr, rds, rdr, sscr,
    local_sems, send_sems, f_sems, zr, xs, xr, yr, y2, sr, fr,
    f_near, f_far, f_pair,
    pair_s, pair_r, sb_s, rl_r, fin_r,
    sty, stz, g_sems, g_near, g_far, g_pair,
    yrl_r, yfin_r, zs_s, zs_r, rd_r, a_z, a_y, a_y2, b_y, b_z,
):
    at = Place()
    x, c, y, z, g = at.x, at.c, at.y, at.z, at.g
    up_z, down_z = at.at_z((z + 1) % NZ), at.at_z((z + NZ - 1) % NZ)
    up_y, down_y = at.at_y((y + 1) % NY), at.at_y((y + 3) % NY)
    zz, zr_ = z // 4, z % 4

    load_weight = pltpu.make_async_copy(weight_hbm, weight, local_sems.at[0])
    load_targets = pltpu.make_async_copy(targets_hbm, targets, local_sems.at[1])
    load_weight.start()
    load_targets.start()

    with phase("A_feat"):
        live = (valid[...] == 1).astype(F32)
        row = lax.broadcasted_iota(jnp.int32, (128, 128), 0)
        lane = lax.broadcasted_iota(jnp.int32, (128, 128), 1)
        wanted = column_tile(parents[...].astype(F32)).astype(jnp.int32) + row // TREE * TREE
        pick = (lane == wanted).astype(BF16)
        chosen = jnp.dot(pick, feat[...], preferred_element_type=F32).astype(BF16)
        source = 32 * (row // 8 % 4) + 8 * (row // 32) + row % 8
        shuffle = (lane == source).astype(BF16)
        chosen = jnp.dot(shuffle, chosen, preferred_element_type=F32).astype(BF16)
        fall[g, 0] = chosen[:64]
        fall[g, 1] = chosen[64:]
        own_gain = gains[g]
        gain[...] = jnp.concatenate([own_gain[k : k + 1] for k in range(8)], axis=1)

    with phase("A_greet"):
        greet(
            [at.dp((g + k) % 8) for k in range(1, 8)]
            + [at.at_z((z + k) % NZ) for k in range(1, NZ)]
            + [at.at_y((y + k) % NY) for k in range(1, NY)]
        )
    send = Sender(send_sems)
    spread = Gather(at, fall, Sender(f_sems), f_near, f_far, f_pair)

    def to_slice(src, j):
        @pl.when(j != g)
        def _():
            remote(src, xall.at[y, g], xs.at[j], xr.at[g], at.dp(j)).start()

        @pl.when(j == g)
        def _():
            pltpu.make_async_copy(src, xall.at[y, g], xs.at[j]).start()

    with phase("A_z"):
        for step in range(5):
            low, high = (z + NZ - step) % NZ, (z + step) % NZ
            if step > 0:
                arrived(zbuf.at[low], zr.at[low], up_z, zr.at[low])
            src = hid if step == 0 else zbuf.at[low]
            if step < 4:
                send(src, zbuf.at[low], zr.at[low], up_z)
            if step == 0:
                send(hid, zbuf.at[high], zr.at[high], down_z)
            to_slice(src, low)
            if 0 < step < 4:
                arrived(zbuf.at[high], zr.at[high], up_z, zr.at[high])
                if step < 3:
                    send(zbuf.at[high], zbuf.at[high], zr.at[high], down_z)
                to_slice(zbuf.at[high], high)

    with phase("A_stat"):
        squares = jnp.square(hid[...].astype(F32))
        for k in range(1, NZ):
            squares = squares + jnp.square(zbuf[(z + k) % NZ].astype(F32))
        stat[y] = row_tile(jnp.sum(squares, axis=1, keepdims=True))
        for k in range(1, NY):
            send(stat.at[y], stat.at[y], sr.at[y], at.at_y((y + k) % NY))

    with phase("A_ysend"):
        for i in range(8):
            block = xall.at[y, i]

            @pl.when(g != i)
            def _():
                arrived(block, xr.at[i], up_y, xr.at[i])

            @pl.when(g == i)
            def _():
                pltpu.make_async_copy(hid, block, xs.at[i]).wait()

            send(block, block, yr.at[0, i], up_y)
            send(block, block, yr.at[1, i], down_y)
        for half in range(2):
            spread.start(half)

    with phase("A_rf"):
        total = stat[y]
        for k in range(1, NY):
            other = (y + k) % NY
            arrived(stat.at[other], sr.at[other], up_y, sr.at[other])
            total = total + stat[other]
        factor = lax.rsqrt(total / (1024.0 * 8) + 1e-05)
        rf[g] = stack_rows(factor[0:1], live)
        for k in range(1, 8):
            send(rf.at[g], rf.at[g], fr.at[g], at.dp((g + k) % 8))

    with phase("A_yrelay"):
        for i in range(8):
            for side, step in ((0, 3), (1, 1)):
                block = xall.at[(y + step) % NY, i]
                arrived(block, yr.at[side, i], up_y, yr.at[side, i])
                if (i < 4) == (side == 0):
                    send(block, block, y2.at[i], up_y if side == 0 else down_y)
    with phase("A_featmid"):
        spread.middle()
        for k in range(1, 8):
            other = (g + k) % 8
            arrived(rf.at[other], fr.at[other], up_y, fr.at[other])
        for i in range(8):
            cols[i] = column_tile(rf[i, 0:1])
    with phase("A_yfar"):
        for i in range(8):
            block = xall.at[(y + 2) % NY, i]
            arrived(block, y2.at[i], up_y, y2.at[i])

    with phase("A_norm"):

        @pl.loop(0, 8)
        def _(i):
            scale = cols[i]
            scale = jnp.concatenate([scale, scale], axis=1)
            rows = pl.ds(pl.multiple_of(i * 128, 128), 128)
            for part in range(NY):
                columns = slice(part * 256, part * 256 + 256)
                values = xall[part, i].astype(F32)
                normed[rows, columns] = (values * scale * gain[:, columns]).astype(BF16)

        load_weight.wait()
        load_targets.wait()

    def multiply(t):
        tile = pl.ds(pl.multiple_of(t * 256, 256), 256)
        for d in range(NX):
            part = lax.dot_general(
                normed[d * 256 : d * 256 + 256, :],
                weight[tile, :],
                (((1,), (1,)), ((), ())),
                preferred_element_type=F32,
            )
            pk[t, 0, d] = part[:128]
            pk[t, 1, d] = part[128:]
        remote(
            pk.at[t, 1 - c], pr.at[t], pair_s.at[t], pair_r.at[t], at.partner()
        ).start()

    def hops(t):
        way = 1 + 2 * (t % 2)
        return (x + way) % NX, (x + 4 - way) % NX

    def direct(t):
        ahead, back = hops(t)
        return (
            remote(sb.at[t, 0], rl.at[t], sb_s.at[t, 0], rl_r.at[t], at.at_x(ahead)),
            remote(sb.at[t, 1], fin.at[t, 0], sb_s.at[t, 1], fin_r.at[t, 0], at.at_x(back)),
        )

    def onward(t):
        ahead, _ = hops(t)
        return remote(sb.at[t, 2], fin.at[t, 1], sb_s.at[t, 2], fin_r.at[t, 1], at.at_x(ahead))

    def encode(t, k, value):
        top = jnp.max(jnp.abs(value), axis=0, keepdims=True)
        step = (120.0 / jnp.maximum(top, 1e-30)).astype(BF16)
        sb[t, k, 128:] = jnp.broadcast_to(step, (16, 256))
        step = sb[t, k, 128:].astype(F32)[0:1]
        sb[t, k, :128] = jnp.exp2(value * step).astype(BF16)

    def decode(block):
        step = block[128:].astype(F32)[0:1]
        return jnp.log2(block[:128].astype(F32)) * (1.0 / step)

    def pair_sum(t):
        ahead, back = hops(t)
        far = (x + 2) % NX
        arrived(pr.at[t], pair_r.at[t], at.partner(), pair_r.at[t])
        encode(t, 0, pk[t, c, far] + pr[t, far])
        encode(t, 1, pk[t, c, back] + pr[t, back])
        for copy in direct(t):
            copy.start()

    def relay(t):
        ahead, _ = hops(t)
        arrived(rl.at[t], rl_r.at[t], at.partner(), rl_r.at[t])
        encode(t, 2, pk[t, c, ahead] + pr[t, ahead] + decode(rl.at[t]))
        onward(t).start()

    def finish(t):
        for k in range(2):
            arrived(fin.at[t, k], fin_r.at[t, k], at.partner(), fin_r.at[t, k])
        lg[t] = pk[t, c, x] + pr[t, x] + decode(fin.at[t, 0]) + decode(fin.at[t, 1])

    with phase("B_fwd"):

        @pl.loop(0, 12)
        def _(t):
            @pl.when(t < 8)
            def _():
                multiply(t)

            @pl.when((t >= 1) & (t < 9))
            def _():
                pair_sum(t - 1)

            @pl.when(t >= 4)
            def _():
                relay(t - 4)

    with phase("B_target"):
        top = jnp.max(targets[...].astype(F32), axis=1, keepdims=True)
        part = jnp.zeros((128, 256), F32)
        for k in range(8):
            part = part + jnp.exp(targets[:, k * 256 : k * 256 + 256].astype(F32) - top)
        tst[...] = stack_rows(
            jnp.zeros((1, 128), F32),
            jnp.zeros((1, 128), F32),
            row_tile(top)[0:1],
            row_tile(jnp.sum(part, axis=1, keepdims=True))[0:1],
        )

    with phase("B_fin"):

        @pl.loop(0, 8)
        def _(t):
            finish(t)

    with phase("B_stat"):
        top = lg[0]
        for t in range(1, 8):
            top = jnp.maximum(top, lg[t])
        top = jnp.max(top, axis=1, keepdims=True)
        part = jnp.zeros((128, 256), F32)
        for t in range(8):
            part = part + jnp.exp(lg[t] - top)
        stat_y[y] = stack_rows(
            row_tile(top)[0:1],
            row_tile(jnp.sum(part, axis=1, keepdims=True))[0:1],
            tst[2:3],
            tst[3:4],
        )
        for k in range(1, NY):
            send(stat_y.at[y], stat_y.at[y], sty.at[y], at.at_y((y + k) % NY))

    def combine(tiles):
        out = []
        for k in (0, 2):
            m = tiles[0][k : k + 1]
            for tile in tiles[1:]:
                m = jnp.maximum(m, tile[k : k + 1])
            s = jnp.zeros((1, 128), F32)
            for tile in tiles:
                s = s + tile[k + 1 : k + 2] * jnp.exp(tile[k : k + 1] - m)
            out += [m, s]
        return out

    with phase("B_staty"):
        tiles = [stat_y[y]]
        for k in range(1, NY):
            other = (y + k) % NY
            arrived(stat_y.at[other], sty.at[other], up_y, sty.at[other])
            tiles.append(stat_y[other])
        stat_z[z] = stack_rows(*combine(tiles))
        for k in range(1, NZ):
            send(stat_z.at[z], stat_z.at[z], stz.at[z], at.at_z((z + k) % NZ))
    with phase("B_statz"):
        tiles = [stat_z[z]]
        for k in range(1, NZ):
            other = (z + k) % NZ
            arrived(stat_z.at[other], stz.at[other], up_y, stz.at[other])
            tiles.append(stat_z[other])
        draft_max, draft_sum, target_max, target_sum = combine(tiles)
        count = jnp.zeros((1, 128), F32)
        for i in range(8):
            count = count + rf[i, 1:2]
        count = jnp.sum(count, axis=1, keepdims=True)
        scale = 1048576.0 * rf[g][1:2] / count
        wide = lambda row: jnp.concatenate([column_tile(row)] * 2, axis=1)
        draft_top, target_top = wide(draft_max), wide(target_max)
        draft_scale, target_scale = wide(1.0 / draft_sum), wide(1.0 / target_sum)
        scale = wide(scale)

    gather = Gather(at, gbuf, Sender(g_sems), g_near, g_far, g_pair)
    with phase("B_G"):
        for t in range(8):
            draft = jnp.exp(lg[t] - draft_top) * draft_scale
            target = (
                jnp.exp(targets[:, t * 256 : t * 256 + 256].astype(F32) - target_top)
                * target_scale
            )
            column = (t % 4) * 256
            gbuf[g, t // 4, :, column : column + 256] = (scale * (draft - target)).astype(BF16)
            if t % 4 == 3:
                gather.start(t // 4)

    with phase("B_featlast"):
        spread.last()
        for step in range(4):
            spread.paired(step)

        @pl.loop(0, NZ)
        def _(owner):
            high, low = owner // 4, owner % 4
            rows = pl.ds(pl.multiple_of((low % 2) * 32, 32), 32)
            blocks = [fall[2 * b + high, low // 2, rows, :].astype(F32) for b in range(4)]
            for k in range(NY):
                group = [block[8 * k : 8 * k + 8] for block in blocks]
                feat_out[owner, k] = jnp.concatenate(group, axis=0).astype(BF16)

    def backward(k, step):
        block = pl.ds(((x + step) % NX) * NC, 2)

        @pl.loop(0, 4)
        def _(n):
            columns = pl.ds(pl.multiple_of(n * 256, 256), 256)
            part = jnp.zeros((256, 256), F32)
            for half in range(2):
                part = part + jnp.dot(
                    gbuf[block, half].reshape(256, 1024),
                    weight[half * 1024 : half * 1024 + 1024, columns],
                    preferred_element_type=F32,
                )
            for which in range(2):
                for dest in range(NY):
                    row = which * 128 + dest * 32
                    pf[k, dest, which, :, columns] = part[row : row + 32]

    def y_first(k):
        way = 1 if k % 2 == 0 else 3
        ysb[k, 0] = pf[k, (y + 2) % NY].astype(BF16)
        send(ysb.at[k, 0], yrl.at[k], yrl_r.at[k], at.at_y((y + way) % NY))
        ysb[k, 1] = pf[k, (y + 4 - way) % NY].astype(BF16)
        send(ysb.at[k, 1], yfin.at[k, 0], yfin_r.at[k, 0], at.at_y((y + 4 - way) % NY))

    def y_second(k):
        way = 1 if k % 2 == 0 else 3
        arrived(yrl.at[k], yrl_r.at[k], up_y, yrl_r.at[k])
        ysb[k, 2] = (pf[k, (y + way) % NY] + yrl[k].astype(F32)).astype(BF16)
        send(ysb.at[k, 2], yfin.at[k, 1], yfin_r.at[k, 1], at.at_y((y + way) % NY))

    steps = (0, 3, 1, 2)

    def z_send(k, dest):
        return remote(
            qs.at[k, dest], zrs.at[k, z], zs_s.at[k, dest], zs_r.at[k, z], at.at_z(dest)
        )

    def y_third(k):
        for j in range(2):
            arrived(yfin.at[k, j], yfin_r.at[k, j], up_y, yfin_r.at[k, j])
        value = pf[k, y] + yfin[k, 0].astype(F32) + yfin[k, 1].astype(F32)
        for owner in range(NZ):
            row = 8 * (owner % 4)
            qs[k, owner] = value[owner // 4, row : row + 8]
        for shift in (4, 3, 5, 2, 6, 1, 7):
            z_send(k, (z + shift) % NZ).start()

    with phase("B_p0"):
        gather.paired(0)
    with phase("B_bw0"):
        backward(0, 0)
        y_first(0)
    with phase("B_mid"):
        gather.middle()
        gather.paired(3)
    with phase("B_bw1"):
        backward(1, 3)
        y_first(1)
        y_second(0)
    with phase("B_bw2"):
        gather.paired(1)
        backward(2, 1)
        y_first(2)
        y_second(1)
        y_third(0)
    with phase("B_last"):
        gather.last()
        gather.paired(2)
    with phase("B_bw3"):
        backward(3, 2)
        y_first(3)
        y_second(2)
        y_third(1)
    with phase("B_ytail"):
        y_second(3)
        y_third(2)
        y_third(3)

    with phase("C_sum"):
        for b in range(4):
            for part in range(NY):
                vscr[b, :, part * 256 : part * 256 + 256] = xall[
                    part, 2 * b + zz, pl.ds(pl.multiple_of(y * 32, 32), 32), :
                ].astype(F32)
        eight = pl.ds(pl.multiple_of(zr_ * 8, 8), 8)
        values = jnp.concatenate([vscr[b, eight, :] for b in range(4)], axis=0)
        eight = pl.ds(pl.multiple_of(y * 32 + zr_ * 8, 8), 8)
        factor = jnp.concatenate([cols[2 * b + zz, eight, :] for b in range(4)], axis=0)
        for k in range(4):
            total = qs[k, z]
            for j in range(1, NZ):
                other = (z + j) % NZ
                arrived(zrs.at[k, other], zs_r.at[k, other], up_y, zs_r.at[k, other])
                total = total + zrs[k, other]
            tot[(x + steps[k]) % NX] = total
    with phase("C_dot"):
        total = tot[...].reshape(32, 1024)
        dot = jnp.sum(gain[...] * values * total, axis=1, keepdims=True)
        dot = jnp.broadcast_to(dot, (32, 128))
        rds[...] = dot
        for k in range(1, 8):
            send(rds, rdr.at[g], rd_r.at[g], at.dp((g + k) % 8))
        for k in range(1, 8):
            other = (g + k) % 8
            arrived(rdr.at[other], rd_r.at[other], up_y, rd_r.at[other])
            dot = dot + rdr[other]
        pull = factor * factor * factor * dot / (1024.0 * 8)
        broad = lambda tile: jnp.concatenate([tile] * 8, axis=1)
        grad = (broad(factor) * gain[...] * total - values * broad(pull)).astype(BF16)
        grad_out[z, y] = grad

    left, right = slice(0, SPLIT), slice(SPLIT, 1024)
    order = []

    def to_y(block_z):
        k = len(order)
        block = grad_out.at[block_z, y, :, left]
        send(block, block, a_y.at[0, k], up_y)
        send(block, block, a_y.at[1, k], down_y)
        order.append(block_z)

    done = [0]

    def pass_y(count):
        while done[0] < count:
            k = done[0]
            for side, step in ((0, 3), (1, 1)):
                block = grad_out.at[order[k], (y + step) % NY, :, left]
                arrived(block, a_y.at[side, k], up_y, a_y.at[side, k])
                if k % 2 == side:
                    send(block, block, a_y2.at[k], up_y if side == 0 else down_y)
            done[0] += 1

    with phase("C_ag"):
        mine = grad_out.at[z, y, :, left]
        send(mine, mine, a_z.at[z], up_z)
        send(mine, mine, a_z.at[z], down_z)
        mine = grad_out.at[z, y, :, right]
        for k in range(1, NY):
            send(mine, mine, b_y.at[y], at.at_y((y + k) % NY))
        to_y(z)
        for k in range(1, NY):
            other = (y + k) % NY
            block = grad_out.at[z, other, :, right]
            arrived(block, b_y.at[other], up_y, b_y.at[other])
        mine = grad_out.at[z, :, :, right]
        send(mine, mine, b_z.at[z], up_z)
        send(mine, mine, b_z.at[z], down_z)
        for step in range(1, 5):
            low, high = (z + NZ - step) % NZ, (z + step) % NZ
            for sems, pick in ((a_z, lambda i: grad_out.at[i, y, :, left]), (b_z, lambda i: grad_out.at[i, :, :, right])):
                arrived(pick(low), sems.at[low], up_z, sems.at[low])
                if step < 4:
                    send(pick(low), pick(low), sems.at[low], up_z)
                if step < 4:
                    arrived(pick(high), sems.at[high], up_z, sems.at[high])
                    if step < 3:
                        send(pick(high), pick(high), sems.at[high], down_z)
                if sems is a_z:
                    to_y(low)
                    if step < 4:
                        to_y(high)
                    pass_y(max(0, 2 * step - 1))
        pass_y(8)
    with phase("C_agfar"):
        for k in range(8):
            block = grad_out.at[order[k], (y + 2) % NY, :, left]
            arrived(block, a_y2.at[k], up_y, a_y2.at[k])

    with phase("C_share"):
        for k in range(4):
            sscr[k] = grad_out[4 * (z % 2) + k, y].astype(F32)
        eight = pl.ds(pl.multiple_of((z // 2) * 8, 8), 8)
        share_out[...] = jnp.concatenate([sscr[k, eight, :] for k in range(4)], axis=0).astype(BF16)

    with phase("C_drain"):

        @pl.loop(0, 8)
        def _(t):
            remote(
                pk.at[t, 1 - c], pr.at[t], pair_s.at[t], pair_r.at[t], at.partner()
            ).wait_send()
            for copy in direct(t):
                copy.wait_send()
            onward(t).wait_send()

        send.drain()
        spread.send.drain()
        gather.send.drain()
        for k in range(4):
            for j in range(1, NZ):
                z_send(k, (z + j) % NZ).wait_send()
        for j in range(8):

            @pl.when(g != j)
            def _():
                remote(hid, xall.at[y, g], xs.at[j], xr.at[g], at.dp(j)).wait_send()


SPLIT = 640
VMEM = pl.BlockSpec(memory_space=pltpu.VMEM)
HBM = pl.BlockSpec(memory_space=pl.ANY)
LIMIT = 60 * 1024 * 1024


def call(*operands):
    return pl.pallas_call(
        kernel,
        out_shape=(
            jax.ShapeDtypeStruct((32, 1024), BF16),
            jax.ShapeDtypeStruct((NZ, NY, 32, 1024), BF16),
            jax.ShapeDtypeStruct((NZ, NY, 32, 768), BF16),
        ),
        in_specs=[VMEM] * 5 + [HBM] * 2,
        out_specs=[VMEM] * 3,
        scratch_shapes=[
            pltpu.VMEM((2048, 1024), BF16),
            pltpu.VMEM((128, 2048), BF16),
            pltpu.VMEM((NZ, 128, 256), BF16),
            pltpu.VMEM((NY, 8, 128, 256), BF16),
            pltpu.VMEM((1024, 1024), BF16),
            pltpu.VMEM((NY, 8, 128), F32),
            pltpu.VMEM((8, 128, 128), F32),
            pltpu.VMEM((8, 8, 128), F32),
            pltpu.VMEM((8, 2, 64, 768), BF16),
            pltpu.VMEM((1, 1024), F32),
            pltpu.VMEM((8, 2, NX, 128, 256), F32),
            pltpu.VMEM((8, NX, 128, 256), F32),
            pltpu.VMEM((8, 3, 144, 256), BF16),
            pltpu.VMEM((8, 144, 256), BF16),
            pltpu.VMEM((8, 2, 144, 256), BF16),
            pltpu.VMEM((8, 128, 256), F32),
            pltpu.VMEM((8, 128), F32),
            pltpu.VMEM((NY, 8, 128), F32),
            pltpu.VMEM((NZ, 8, 128), F32),
            pltpu.VMEM((8, 2, 128, 1024), BF16),
            pltpu.VMEM((4, NY, 2, 32, 1024), F32),
            pltpu.VMEM((4, 3, 2, 32, 1024), BF16),
            pltpu.VMEM((4, 2, 32, 1024), BF16),
            pltpu.VMEM((4, 2, 2, 32, 1024), BF16),
            pltpu.VMEM((4, NZ, 8, 1024), F32),
            pltpu.VMEM((4, NZ, 8, 1024), F32),
            pltpu.VMEM((4, 8, 1024), F32),
            pltpu.VMEM((4, 32, 1024), F32),
            pltpu.VMEM((32, 128), F32),
            pltpu.VMEM((8, 32, 128), F32),
            pltpu.VMEM((4, 32, 1024), F32),
            DMA((2,)),
            DMA((112,)),
            DMA((GATHER_SENDS,)),
            DMA((NZ,)),
            DMA((8,)),
            DMA((8,)),
            DMA((2, 8)),
            DMA((8,)),
            DMA((NY,)),
            DMA((8,)),
            DMA((2, 2)),
            DMA((2,)),
            DMA((4, 2)),
            DMA((8,)),
            DMA((8,)),
            DMA((8, 3)),
            DMA((8,)),
            DMA((8, 2)),
            DMA((NY,)),
            DMA((NZ,)),
            DMA((GATHER_SENDS,)),
            DMA((2, 2)),
            DMA((2,)),
            DMA((4, 2)),
            DMA((4,)),
            DMA((4, 2)),
            DMA((4, NZ)),
            DMA((4, NZ)),
            DMA((8,)),
            DMA((NZ,)),
            DMA((2, 8)),
            DMA((8,)),
            DMA((NY,)),
            DMA((NZ,)),
        ],
        compiler_params=pltpu.CompilerParams(
            collective_id=0, has_side_effects=True, vmem_limit_bytes=LIMIT
        ),
    )(*operands)


def body(hidden, norm_gain, head_weight, target_logits, valid_rows, parents, features):
    share, grad, parent_features = call(
        hidden,
        valid_rows.reshape(1, 128),
        parents.reshape(1, 128),
        features,
        norm_gain.reshape(8, 8, 128),
        head_weight,
        target_logits,
    )
    grad_joining = lax.dot_general(
        grad.reshape(1024, 1024),
        parent_features.reshape(1024, 768),
        (((0,), (0,)), ((), ())),
        preferred_element_type=F32,
    )
    return (share, grad_joining)


def solution(mesh):
    placed = (
        P("dp", "vocab"),
        P(),
        P("vocab", "dp"),
        P("dp", "vocab"),
        P("dp"),
        P("dp"),
        P("dp", "vocab"),
    )
    return jax.shard_map(
        body,
        mesh=mesh,
        in_specs=placed,
        out_specs=(P("vocab", "dp"), P("dp", "vocab")),
        check_vma=False,
    )
```

```python
import contextlib

import jax
import jax.numpy as jnp
from jax import lax
from jax.experimental import pallas as pl
from jax.experimental.pallas import tpu as pltpu
from jax.sharding import PartitionSpec as P

TREE = 64
NX, NC, NY, NZ = 4, 2, 4, 8
F32, BF16 = jnp.float32, jnp.bfloat16
DMA = pltpu.SemaphoreType.DMA


def remote(src, dst, send_sem, recv_sem, device):
    return pltpu.make_async_remote_copy(
        src_ref=src,
        dst_ref=dst,
        send_sem=send_sem,
        recv_sem=recv_sem,
        device_id=device,
        device_id_type=pl.DeviceIdType.MESH,
    )


def phase(name):
    return contextlib.nullcontext()


class Place:
    def __init__(self):
        self.g = lax.axis_index("dp")
        self.v = lax.axis_index("vocab")
        self.x, self.c = self.g // NC, self.g % NC
        self.z, self.y = self.v // NY, self.v % NY

    def dp(self, i):
        return (i, self.v)

    def at_x(self, x):
        return (x * NC + self.c, self.v)

    def partner(self):
        return (self.x * NC + 1 - self.c, self.v)

    def at_y(self, y):
        return (self.g, self.z * NY + y)

    def at_z(self, z):
        return (self.g, z * NY + self.y)


class Sender:
    def __init__(self, sems):
        self.sems, self.used, self.copies = sems, 0, []

    def __call__(self, src, dst, recv_sem, device):
        assert self.used < self.sems.shape[0]
        copy = remote(src, dst, self.sems.at[self.used], recv_sem, device)
        self.used += 1
        copy.start()
        self.copies.append(copy)

    def drain(self):
        for copy in self.copies:
            copy.wait_send()


def arrived(dst, recv_sem, device, any_sem):
    remote(dst, dst, any_sem, recv_sem, device).wait_recv()


class Gather:
    def __init__(self, at, buf, send, near, far, pair):
        self.at, self.buf, self.send = at, buf, send
        self.near, self.far, self.pair = near, far, pair

    def slot(self, step, core):
        return ((self.at.x + step) % NX) * NC + core

    def start(self):
        at, buf = self.at, self.buf
        up, down = at.at_x((at.x + 1) % NX), at.at_x((at.x + 3) % NX)
        for k in range(2):
            for side, half, device in ((0, k, up), (1, 1 - k, down)):
                mine = buf.at[at.g, half]
                self.send(mine, mine, self.near.at[side, half], device)
            mine = buf.at[at.g, k]
            self.send(mine, mine, self.pair.at[0, k], at.partner())

    def middle(self, first):
        at, buf = self.at, self.buf
        for side, step in ((0, 3), (1, 1)):
            half = side if first else 1 - side
            block = buf.at[self.slot(step, at.c), half]
            arrived(block, self.near.at[side, half], at.partner(), self.near.at[side, half])
            if first:
                onward = at.at_x((at.x + (1 if side == 0 else 3)) % NX)
                self.send(block, block, self.far.at[half], onward)
            self.send(block, block, self.pair.at[step, half], at.partner())

    def last(self):
        at, buf = self.at, self.buf
        for half in range(2):
            block = buf.at[self.slot(2, at.c), half]
            arrived(block, self.far.at[half], at.partner(), self.far.at[half])
            self.send(block, block, self.pair.at[2, half], at.partner())

    def paired(self, step):
        at = self.at
        for half in range(2):
            block = self.buf.at[self.slot(step, 1 - at.c), half]
            arrived(block, self.pair.at[step, half], at.partner(), self.pair.at[step, half])


GATHER_SENDS = 14


def row_tile(column):
    return jnp.transpose(jnp.broadcast_to(column, (128, 128)))[0:8]


def column_tile(row):
    return jnp.transpose(jnp.broadcast_to(row, (128, 128)))


def stack_rows(*rows):
    index = lax.broadcasted_iota(jnp.int32, (8, 128), 0)
    tile = jnp.zeros((8, 128), F32)
    for k, row in enumerate(rows):
        tile = jnp.where(index == k, row, tile)
    return tile


def kernel(
    hid, valid, parents, feat, gains, weight_hbm, targets_hbm,
    share_out, grad_out, fall,
    weight, targets, zbuf, xall, normed, stat, cols, scols, rf, srow, gain,
    pk, pr, sb, rl, fin, lg, tst, stat_v, dot_v, gbuf, pf, ysb, yrl, yfin,
    qf, qs, zrs,
    local_sems, send_sems, f_sems, zr, xs, xr, yr, y2, sr, fr,
    f_near, f_far, f_pair,
    pair_s, pair_r, sb_s, rl_r, fin_r,
    sv_s, sv_r, dv_s, dv_r, sd_r, g_sems, g_near, g_far, g_pair,
    yrl_r, yfin_r, zs_s, zs_r, a_z, a_y, a_y2,
):
    at = Place()
    x, c, y, z, g, v = at.x, at.c, at.y, at.z, at.g, at.v
    up_z, down_z = at.at_z((z + 1) % NZ), at.at_z((z + NZ - 1) % NZ)
    up_y, down_y = at.at_y((y + 1) % NY), at.at_y((y + 3) % NY)

    load_weight = pltpu.make_async_copy(weight_hbm, weight, local_sems.at[0])
    load_targets = pltpu.make_async_copy(targets_hbm, targets, local_sems.at[1])
    load_weight.start()
    load_targets.start()

    with phase("A_feat"):
        live = (valid[...] == 1).astype(F32)
        row = lax.broadcasted_iota(jnp.int32, (128, 128), 0)
        lane = lax.broadcasted_iota(jnp.int32, (128, 128), 1)
        wanted = column_tile(parents[...].astype(F32)).astype(jnp.int32) + row // TREE * TREE
        pick = (lane == wanted).astype(BF16)
        chosen = jnp.dot(pick, feat[...], preferred_element_type=F32).astype(BF16)
        fall[g, 0] = chosen[:64]
        fall[g, 1] = chosen[64:]
        own_gain = gains[g]
        gain[...] = jnp.concatenate([own_gain[k : k + 1] for k in range(8)], axis=1)

    with phase("A_greet"):
        barrier = pltpu.get_barrier_semaphore()

        @pl.loop(1, 32)
        def _(k):
            pl.semaphore_signal(
                barrier,
                inc=1,
                device_id=(g, (v + k) % 32),
                device_id_type=pl.DeviceIdType.MESH,
            )

        @pl.loop(1, 8)
        def _(k):
            pl.semaphore_signal(
                barrier,
                inc=1,
                device_id=((g + k) % 8, v),
                device_id_type=pl.DeviceIdType.MESH,
            )

        pl.semaphore_wait(barrier, 38)
    send = Sender(send_sems)
    spread = Gather(at, fall, Sender(f_sems), f_near, f_far, f_pair)

    def to_slice(src, j):
        @pl.when(j != g)
        def _():
            remote(src, xall.at[y, g], xs.at[j], xr.at[g], at.dp(j)).start()

        @pl.when(j == g)
        def _():
            pltpu.make_async_copy(src, xall.at[y, g], xs.at[j]).start()

    with phase("A_z"):
        for step in range(5):
            low, high = (z + NZ - step) % NZ, (z + step) % NZ
            if step > 0:
                arrived(zbuf.at[low], zr.at[low], up_z, zr.at[low])
            src = hid if step == 0 else zbuf.at[low]
            if step < 4:
                send(src, zbuf.at[low], zr.at[low], up_z)
            if step == 0:
                send(hid, zbuf.at[high], zr.at[high], down_z)
            to_slice(src, low)
            if step == 0:
                spread.start()
            if 0 < step < 4:
                arrived(zbuf.at[high], zr.at[high], up_z, zr.at[high])
                if step < 3:
                    send(zbuf.at[high], zbuf.at[high], zr.at[high], down_z)
                to_slice(zbuf.at[high], high)

    with phase("A_stat"):
        squares = jnp.square(hid[...].astype(F32))
        for k in range(1, NZ):
            squares = squares + jnp.square(zbuf[(z + k) % NZ].astype(F32))
        stat[y] = row_tile(jnp.sum(squares, axis=1, keepdims=True))
        for k in range(1, NY):
            send(stat.at[y], stat.at[y], sr.at[y], at.at_y((y + k) % NY))

    turns = (2, 1, 3, 0)

    def group(k):
        return 2 * ((x + turns[k // 2]) % NX) + k % 2

    def y_send(k):
        block = xall.at[y, group(k)]
        sem = xr.at[group(k)]
        if k < 6:
            arrived(block, sem, up_y, sem)
        else:

            @pl.when(c != k % 2)
            def _():
                arrived(block, sem, up_y, sem)

            @pl.when(c == k % 2)
            def _():
                pltpu.make_async_copy(hid, block, xs.at[g]).wait()

        send(block, block, yr.at[0, k], up_y)
        send(block, block, yr.at[1, k], down_y)

    def y_relay(k):
        for side, step in ((0, 3), (1, 1)):
            block = xall.at[(y + step) % NY, group(k)]
            arrived(block, yr.at[side, k], up_y, yr.at[side, k])
            if k % 2 == side:
                send(block, block, y2.at[k], up_y if side == 0 else down_y)
        if k + 3 < 8:
            y_send(k + 3)

    def y_far(k):
        block = xall.at[(y + 2) % NY, group(k)]
        arrived(block, y2.at[k], up_y, y2.at[k])

    def normalise(k):
        i = group(k)
        scale = cols[i]
        scale = jnp.concatenate([scale, scale], axis=1)
        rows = pl.ds(pl.multiple_of(i * 128, 128), 128)
        for part in range(NY):
            columns = slice(part * 256, part * 256 + 256)
            values = xall[part, i].astype(F32)
            normed[rows, columns] = (values * scale * gain[:, columns]).astype(BF16)

    def pair_copy(step, t):
        return remote(
            pk.at[step, t, 1 - c], pr.at[step, t],
            pair_s.at[step, t], pair_r.at[step, t], at.partner(),
        )

    def multiply(step):
        rows = pl.ds(pl.multiple_of(((x + step) % NX) * 256, 256), 256)

        @pl.loop(0, 8)
        def _(t):
            tile = pl.ds(pl.multiple_of(t * 256, 256), 256)
            part = lax.dot_general(
                normed[rows, :],
                weight[tile, :],
                (((1,), (1,)), ((), ())),
                preferred_element_type=F32,
            )
            pk[step, t, 0] = part[:128]
            pk[step, t, 1] = part[128:]
            pair_copy(step, t).start()

    def total_of(step, t):
        arrived(pr.at[step, t], pair_r.at[step, t], at.partner(), pair_r.at[step, t])
        return pk[step, t, c] + pr[step, t]

    def ways(t):
        way = 1 + 2 * (t % 2)
        return way, 4 - way

    def first_hop(t):
        ahead, _ = ways(t)
        return remote(sb.at[t, 0], rl.at[t], sb_s.at[t, 0], rl_r.at[t], at.at_x((x + ahead) % NX))

    def direct(t):
        _, back = ways(t)
        return remote(
            sb.at[t, 1], fin.at[t, 0], sb_s.at[t, 1], fin_r.at[t, 0], at.at_x((x + back) % NX)
        )

    def onward(t):
        ahead, _ = ways(t)
        return remote(
            sb.at[t, 2], fin.at[t, 1], sb_s.at[t, 2], fin_r.at[t, 1], at.at_x((x + ahead) % NX)
        )

    def encode(t, k, value):
        top = jnp.max(jnp.abs(value), axis=0, keepdims=True)
        step = (120.0 / jnp.maximum(top, 1e-30)).astype(BF16)
        sb[t, k, 128:] = jnp.broadcast_to(step, (16, 256))
        step = sb[t, k, 128:].astype(F32)[0:1]
        sb[t, k, :128] = jnp.exp2(value * step).astype(BF16)

    def decode(block):
        step = block[128:].astype(F32)[0:1]
        return jnp.log2(block[:128].astype(F32)) * (1.0 / step)

    with phase("A_ysend"):
        for k in range(3):
            y_send(k)

    with phase("A_rf"):
        total = stat[y]
        for k in range(1, NY):
            other = (y + k) % NY
            arrived(stat.at[other], sr.at[other], up_y, sr.at[other])
            total = total + stat[other]
        factor = lax.rsqrt(total / (1024.0 * 8) + 1e-05)
        rf[g] = stack_rows(factor[0:1], live)
        for k in range(1, 8):
            send(rf.at[g], rf.at[g], fr.at[g], at.dp((g + k) % 8))

    with phase("A_y0123"):
        y_relay(0)
        y_relay(1)
        spread.middle(True)
        y_relay(2)
        for k in range(1, 8):
            other = (g + k) % 8
            arrived(rf.at[other], fr.at[other], up_y, fr.at[other])
        for i in range(8):
            cols[i] = column_tile(rf[i, 0:1])
        y_relay(3)
        load_weight.wait()
        load_targets.wait()
    with phase("A_far01"):
        y_far(0)
        y_far(1)
        normalise(0)
        normalise(1)
    with phase("F_mul2"):
        multiply(2)
        y_relay(4)
    with phase("F_hop"):

        @pl.loop(0, 8)
        def _(t):
            encode(t, 0, total_of(2, t))
            first_hop(t).start()

    with phase("A_y56"):
        y_relay(5)
        y_relay(6)
    with phase("A_far2345"):
        for k in range(2, 6):
            y_far(k)
            normalise(k)
    with phase("F_mul13"):
        multiply(1)
        multiply(3)
        y_relay(7)
    with phase("F_both"):

        @pl.loop(0, 8)
        def _(t):
            ahead, back = ways(t)
            encode(t, 1, total_of(back, t))
            direct(t).start()
            arrived(rl.at[t], rl_r.at[t], at.partner(), rl_r.at[t])
            encode(t, 2, total_of(ahead, t) + decode(rl.at[t]))
            onward(t).start()

    with phase("A_far67"):
        spread.middle(False)
        for k in range(6, 8):
            y_far(k)
            normalise(k)
    with phase("F_mul0"):
        multiply(0)
        top = jnp.max(targets[...].astype(F32), axis=1, keepdims=True)
        part = jnp.zeros((128, 256), F32)
        for k in range(8):
            part = part + jnp.exp(targets[:, k * 256 : k * 256 + 256].astype(F32) - top)
        tst[...] = stack_rows(
            jnp.zeros((1, 128), F32),
            jnp.zeros((1, 128), F32),
            row_tile(top)[0:1],
            row_tile(jnp.sum(part, axis=1, keepdims=True))[0:1],
        )

    with phase("F_fin"):

        @pl.loop(0, 8)
        def _(t):
            own = total_of(0, t)
            for k in range(2):
                arrived(fin.at[t, k], fin_r.at[t, k], at.partner(), fin_r.at[t, k])
            lg[t] = own + decode(fin.at[t, 0]) + decode(fin.at[t, 1])

    def tell_all(tile, send_sem, recv_sem):
        @pl.loop(1, 32)
        def _(k):
            remote(
                tile.at[v], tile.at[v], send_sem.at[k], recv_sem.at[v], (g, (v + k) % 32)
            ).start()

    def hear_all(tile, recv_sem):
        @pl.loop(1, 32)
        def _(k):
            other = (v + k) % 32
            arrived(tile.at[other], recv_sem.at[other], up_y, recv_sem.at[other])

    with phase("B_stat"):
        top = lg[0]
        for t in range(1, 8):
            top = jnp.maximum(top, lg[t])
        top = jnp.max(top, axis=1, keepdims=True)
        part = jnp.zeros((128, 256), F32)
        for t in range(8):
            part = part + jnp.exp(lg[t] - top)
        stat_v[v] = stack_rows(
            row_tile(top)[0:1],
            row_tile(jnp.sum(part, axis=1, keepdims=True))[0:1],
            tst[2:3],
            tst[3:4],
        )
        tell_all(stat_v, sv_s, sv_r)

    with phase("B_statv"):
        hear_all(stat_v, sv_r)
        wide = lambda row: jnp.concatenate([column_tile(row)] * 2, axis=1)
        tops, scales = [], []
        for k in (0, 2):
            top = jnp.max(stat_v[:, k, :], axis=0, keepdims=True)
            part = stat_v[:, k + 1, :] * jnp.exp(stat_v[:, k, :] - top)
            tops.append(wide(top))
            scales.append(wide(1.0 / jnp.sum(part, axis=0, keepdims=True)))
        count = jnp.zeros((1, 128), F32)
        for i in range(8):
            count = count + rf[i, 1:2]
        count = jnp.sum(count, axis=1, keepdims=True)
        scale = wide(1048576.0 * live / count)

    gather = Gather(at, gbuf, Sender(g_sems), g_near, g_far, g_pair)
    with phase("B_G"):
        acc = jnp.zeros((128, 256), F32)
        for t in range(8):
            draft = jnp.exp(lg[t] - tops[0]) * scales[0]
            target = (
                jnp.exp(targets[:, t * 256 : t * 256 + 256].astype(F32) - tops[1]) * scales[1]
            )
            column = (t % 4) * 256
            value = (scale * (draft - target)).astype(BF16)
            gbuf[g, t // 4, :, column : column + 256] = value
            acc = acc + value.astype(F32) * lg[t]
        gather.start()
        dot_v[v] = row_tile(jnp.sum(acc, axis=1, keepdims=True))
        tell_all(dot_v, dv_s, dv_r)

    steps = (0, 3, 1, 2)

    def block_of(k):
        return (x + steps[k]) % NX

    def backward(k):
        block = pl.ds(block_of(k) * NC, 2)

        @pl.loop(0, 4)
        def _(n):
            columns = pl.ds(pl.multiple_of(n * 256, 256), 256)
            part = jnp.zeros((256, 256), F32)
            for half in range(2):
                part = part + jnp.dot(
                    gbuf[block, half].reshape(256, 1024),
                    weight[half * 1024 : half * 1024 + 1024, columns],
                    preferred_element_type=F32,
                )
            for which in range(2):
                for dest in range(NY):
                    row = which * 128 + dest * 32
                    pf[k, dest, which, :, columns] = part[row : row + 32]

        way = 1 if k % 2 == 0 else 3
        ysb[k, 0] = pf[k, (y + 2) % NY].astype(BF16)
        send(ysb.at[k, 0], yrl.at[k], yrl_r.at[k], at.at_y((y + way) % NY))
        ysb[k, 1] = pf[k, (y + 4 - way) % NY].astype(BF16)
        send(ysb.at[k, 1], yfin.at[k, 0], yfin_r.at[k, 0], at.at_y((y + 4 - way) % NY))

    def y_second(k):
        way = 1 if k % 2 == 0 else 3
        arrived(yrl.at[k], yrl_r.at[k], up_y, yrl_r.at[k])
        ysb[k, 2] = (pf[k, (y + way) % NY] + yrl[k].astype(F32)).astype(BF16)
        send(ysb.at[k, 2], yfin.at[k, 1], yfin_r.at[k, 1], at.at_y((y + way) % NY))

    def z_send(k, dest):
        return remote(
            qs.at[k, dest], zrs.at[k, z], zs_s.at[k, dest], zs_r.at[k, z], at.at_z(dest)
        )

    far_first = (4, 3, 5, 2, 6, 1, 7)

    def y_third(k):
        for j in range(2):
            arrived(yfin.at[k, j], yfin_r.at[k, j], up_y, yfin_r.at[k, j])
        value = pf[k, y] + yfin[k, 0].astype(F32) + yfin[k, 1].astype(F32)
        for owner in range(NZ):
            piece = value[:, :, 128 * owner : 128 * owner + 128]
            qf[k, owner] = piece
            qs[k, owner] = piece.astype(BF16)
        for shift in far_first:
            z_send(k, (z + shift) % NZ).start()

    own_columns = pl.ds(pl.multiple_of(z * 128, 128), 128)

    def piece_of(k, owner):
        columns = pl.ds(pl.multiple_of(owner * 128, 128), 128)
        return grad_out.at[pl.ds(2 * block_of(k), 2), y, :, columns]

    def z_fourth(k):
        total = qf[k, z]
        for j in range(1, NZ):
            other = (z + j) % NZ
            arrived(zrs.at[k, other], zs_r.at[k, other], up_y, zs_r.at[k, other])
            total = total + zrs[k, other].astype(F32)
        rows = pl.ds(pl.multiple_of(y * 32, 32), 32)
        lanes = pl.ds(pl.multiple_of((z % 2) * 128, 128), 128)
        for which in range(2):
            i = 2 * block_of(k) + which
            values = xall[z // 2, i, rows, lanes].astype(F32)
            grad = cols[i, rows, :] * gain[:, own_columns] * total[which]
            grad = grad - values * scols[i, rows, :]
            grad_out[i, y, :, own_columns] = grad.astype(BF16)
        mine = piece_of(k, z)
        for shift in far_first:
            send(mine, mine, a_z.at[k, z], at.at_z((z + shift) % NZ))

    def across(k):
        for j in (1, 7, 2, 6, 3, 5, 4):
            other = (z + j) % NZ
            arrived(piece_of(k, other), a_z.at[k, other], up_y, a_z.at[k, other])
        mine = grad_out.at[pl.ds(2 * block_of(k), 2), y]
        send(mine, mine, a_y.at[0, k], up_y)
        send(mine, mine, a_y.at[1, k], down_y)

    def across_relay(k):
        for side, step in ((0, 3), (1, 1)):
            block = grad_out.at[pl.ds(2 * block_of(k), 2), (y + step) % NY]
            arrived(block, a_y.at[side, k], up_y, a_y.at[side, k])
            half = grad_out.at[2 * block_of(k) + side, (y + step) % NY]
            send(half, half, a_y2.at[side, k], up_y if side == 0 else down_y)

    def across_far(k):
        for side in range(2):
            half = grad_out.at[2 * block_of(k) + side, (y + 2) % NY]
            arrived(half, a_y2.at[side, k], up_y, a_y2.at[side, k])

    with phase("G_bw0"):
        gather.paired(0)
        backward(0)
    with phase("G_feat"):
        spread.last()
        spread.paired(0)
        spread.paired(1)
        spread.paired(3)
    with phase("G_mid"):
        gather.middle(True)
    with phase("G_ys0"):
        y_second(0)
    with phase("G_dot"):
        hear_all(dot_v, dv_r)
        dot = jnp.sum(dot_v[:, 0, :], axis=0, keepdims=True)
        factor = rf[g][0:1]
        srow[g] = jnp.broadcast_to(factor * factor * dot / (1024.0 * 8), (8, 128))
        for k in range(1, 8):
            send(srow.at[g], srow.at[g], sd_r.at[g], at.dp((g + k) % 8))
    with phase("G_yt0"):
        y_third(0)
    with phase("G_mid2"):
        gather.middle(False)
        gather.paired(3)
    with phase("G_bw1"):
        backward(1)
    with phase("G_bw2"):
        gather.paired(1)
        backward(2)
    with phase("G_s"):
        for k in range(1, 8):
            other = (g + k) % 8
            arrived(srow.at[other], sd_r.at[other], up_y, sd_r.at[other])
        for i in range(8):
            scols[i] = column_tile(srow[i, 0:1])
    with phase("G_z0"):
        z_fourth(0)
    with phase("G_last"):
        gather.last()
        y_second(1)
        gather.paired(2)
    with phase("G_bw3"):
        backward(3)
    with phase("H_ax0"):
        across(0)
    with phase("H_ys2"):
        y_second(2)
    with phase("H_yt1"):
        y_third(1)
    with phase("H_ys3"):
        y_second(3)
    with phase("H_ar0"):
        across_relay(0)
    with phase("H_yt2"):
        y_third(2)
    with phase("H_z1"):
        z_fourth(1)
    with phase("H_yt3"):
        y_third(3)
    with phase("H_ax1"):
        across(1)
    with phase("H_z2"):
        z_fourth(2)
    with phase("H_z3"):
        z_fourth(3)
    with phase("H_ax2"):
        across(2)
    with phase("H_ar1"):
        across_relay(1)
    with phase("H_ax3"):
        across(3)
    with phase("H_ar2"):
        across_relay(2)
    with phase("H_ar3"):
        across_relay(3)
    with phase("H_far"):
        for k in range(4):
            across_far(k)
        share_out[...] = grad_out[z, y]
        spread.paired(2)

    with phase("H_drain"):

        @pl.loop(0, 8)
        def _(t):
            for step in range(4):
                pair_copy(step, t).wait_send()
            first_hop(t).wait_send()
            direct(t).wait_send()
            onward(t).wait_send()

        @pl.loop(1, 32)
        def _(k):
            other = (g, (v + k) % 32)
            remote(stat_v.at[v], stat_v.at[v], sv_s.at[k], sv_r.at[v], other).wait_send()
            remote(dot_v.at[v], dot_v.at[v], dv_s.at[k], dv_r.at[v], other).wait_send()

        send.drain()
        spread.send.drain()
        gather.send.drain()
        for k in range(4):
            for j in range(1, NZ):
                z_send(k, (z + j) % NZ).wait_send()
        for j in range(8):

            @pl.when(g != j)
            def _():
                remote(hid, xall.at[y, g], xs.at[j], xr.at[g], at.dp(j)).wait_send()


VMEM = pl.BlockSpec(memory_space=pltpu.VMEM)
HBM = pl.BlockSpec(memory_space=pl.ANY)
LIMIT = 60 * 1024 * 1024


def call(*operands):
    return pl.pallas_call(
        kernel,
        out_shape=(
            jax.ShapeDtypeStruct((32, 1024), BF16),
            jax.ShapeDtypeStruct((8, NY, 32, 1024), BF16),
            jax.ShapeDtypeStruct((8, 2, 64, 768), BF16),
        ),
        in_specs=[VMEM] * 5 + [HBM] * 2,
        out_specs=[VMEM] * 3,
        scratch_shapes=[
            pltpu.VMEM((2048, 1024), BF16),
            pltpu.VMEM((128, 2048), BF16),
            pltpu.VMEM((NZ, 128, 256), BF16),
            pltpu.VMEM((NY, 8, 128, 256), BF16),
            pltpu.VMEM((1024, 1024), BF16),
            pltpu.VMEM((NY, 8, 128), F32),
            pltpu.VMEM((8, 128, 128), F32),
            pltpu.VMEM((8, 128, 128), F32),
            pltpu.VMEM((8, 8, 128), F32),
            pltpu.VMEM((8, 8, 128), F32),
            pltpu.VMEM((1, 1024), F32),
            pltpu.VMEM((NX, 8, 2, 128, 256), F32),
            pltpu.VMEM((NX, 8, 128, 256), F32),
            pltpu.VMEM((8, 3, 144, 256), BF16),
            pltpu.VMEM((8, 144, 256), BF16),
            pltpu.VMEM((8, 2, 144, 256), BF16),
            pltpu.VMEM((8, 128, 256), F32),
            pltpu.VMEM((8, 128), F32),
            pltpu.VMEM((32, 8, 128), F32),
            pltpu.VMEM((32, 8, 128), F32),
            pltpu.VMEM((8, 2, 128, 1024), BF16),
            pltpu.VMEM((4, NY, 2, 32, 1024), F32),
            pltpu.VMEM((4, 3, 2, 32, 1024), BF16),
            pltpu.VMEM((4, 2, 32, 1024), BF16),
            pltpu.VMEM((4, 2, 2, 32, 1024), BF16),
            pltpu.VMEM((4, NZ, 2, 32, 128), F32),
            pltpu.VMEM((4, NZ, 2, 32, 128), BF16),
            pltpu.VMEM((4, NZ, 2, 32, 128), BF16),
            DMA((2,)),
            DMA((120,)),
            DMA((GATHER_SENDS,)),
            DMA((NZ,)),
            DMA((8,)),
            DMA((8,)),
            DMA((2, 8)),
            DMA((8,)),
            DMA((NY,)),
            DMA((8,)),
            DMA((2, 2)),
            DMA((2,)),
            DMA((4, 2)),
            DMA((NX, 8)),
            DMA((NX, 8)),
            DMA((8, 3)),
            DMA((8,)),
            DMA((8, 2)),
            DMA((32,)),
            DMA((32,)),
            DMA((32,)),
            DMA((32,)),
            DMA((8,)),
            DMA((GATHER_SENDS,)),
            DMA((2, 2)),
            DMA((2,)),
            DMA((4, 2)),
            DMA((4,)),
            DMA((4, 2)),
            DMA((4, NZ)),
            DMA((4, NZ)),
            DMA((4, NZ)),
            DMA((2, 4)),
            DMA((2, 4)),
        ],
        compiler_params=pltpu.CompilerParams(
            collective_id=0, has_side_effects=True, vmem_limit_bytes=LIMIT
        ),
    )(*operands)


def body(hidden, norm_gain, head_weight, target_logits, valid_rows, parents, features):
    share, grad, parent_features = call(
        hidden,
        valid_rows.reshape(1, 128),
        parents.reshape(1, 128),
        features,
        norm_gain.reshape(8, 8, 128),
        head_weight,
        target_logits,
    )
    grad_joining = lax.dot_general(
        grad.reshape(1024, 1024),
        parent_features.reshape(1024, 768),
        (((0,), (0,)), ((), ())),
        preferred_element_type=F32,
    )
    return (share, grad_joining)


def solution(mesh):
    placed = (
        P("dp", "vocab"),
        P(),
        P("vocab", "dp"),
        P("dp", "vocab"),
        P("dp"),
        P("dp"),
        P("dp", "vocab"),
    )
    return jax.shard_map(
        body,
        mesh=mesh,
        in_specs=placed,
        out_specs=(P("vocab", "dp"), P("dp", "vocab")),
        check_vma=False,
    )
```

```python
import contextlib

import jax
import jax.numpy as jnp
from jax import lax
from jax.experimental import pallas as pl
from jax.experimental.pallas import tpu as pltpu
from jax.sharding import PartitionSpec as P

TREE = 64
NX, NC, NY, NZ = 4, 2, 4, 8
F32, BF16 = jnp.float32, jnp.bfloat16
DMA = pltpu.SemaphoreType.DMA


def remote(src, dst, send_sem, recv_sem, device):
    return pltpu.make_async_remote_copy(
        src_ref=src,
        dst_ref=dst,
        send_sem=send_sem,
        recv_sem=recv_sem,
        device_id=device,
        device_id_type=pl.DeviceIdType.MESH,
    )


def phase(name):
    return contextlib.nullcontext()


class Place:
    def __init__(self):
        self.g = lax.axis_index("dp")
        self.v = lax.axis_index("vocab")
        self.x, self.c = self.g // NC, self.g % NC
        self.z, self.y = self.v // NY, self.v % NY

    def dp(self, i):
        return (i, self.v)

    def at_x(self, x):
        return (x * NC + self.c, self.v)

    def partner(self):
        return (self.x * NC + 1 - self.c, self.v)

    def at_y(self, y):
        return (self.g, self.z * NY + y)

    def at_z(self, z):
        return (self.g, z * NY + self.y)


class Sender:
    def __init__(self, sems):
        self.sems, self.used, self.copies = sems, 0, []

    def __call__(self, src, dst, recv_sem, device):
        assert self.used < self.sems.shape[0]
        copy = remote(src, dst, self.sems.at[self.used], recv_sem, device)
        self.used += 1
        copy.start()
        self.copies.append(copy)

    def drain(self):
        for copy in self.copies:
            copy.wait_send()


def arrived(dst, recv_sem, device, any_sem):
    remote(dst, dst, any_sem, recv_sem, device).wait_recv()


class Gather:
    def __init__(self, at, buf, send, near, far, pair):
        self.at, self.buf, self.send = at, buf, send
        self.near, self.far, self.pair = near, far, pair

    def slot(self, step, core):
        return ((self.at.x + step) % NX) * NC + core

    def start(self):
        at, buf = self.at, self.buf
        up, down = at.at_x((at.x + 1) % NX), at.at_x((at.x + 3) % NX)
        for k in range(2):
            for side, half, device in ((0, k, up), (1, 1 - k, down)):
                mine = buf.at[at.g, half]
                self.send(mine, mine, self.near.at[side, half], device)
            mine = buf.at[at.g, k]
            self.send(mine, mine, self.pair.at[0, k], at.partner())

    def middle(self, first):
        at, buf = self.at, self.buf
        for side, step in ((0, 3), (1, 1)):
            half = side if first else 1 - side
            block = buf.at[self.slot(step, at.c), half]
            arrived(block, self.near.at[side, half], at.partner(), self.near.at[side, half])
            if first:
                onward = at.at_x((at.x + (1 if side == 0 else 3)) % NX)
                self.send(block, block, self.far.at[half], onward)
            self.send(block, block, self.pair.at[step, half], at.partner())

    def last(self):
        at, buf = self.at, self.buf
        for half in range(2):
            block = buf.at[self.slot(2, at.c), half]
            arrived(block, self.far.at[half], at.partner(), self.far.at[half])
            self.send(block, block, self.pair.at[2, half], at.partner())

    def paired(self, step, half):
        at = self.at
        block = self.buf.at[self.slot(step, 1 - at.c), half]
        arrived(block, self.pair.at[step, half], at.partner(), self.pair.at[step, half])


GATHER_SENDS = 14


def row_tile(column):
    return jnp.transpose(jnp.broadcast_to(column, (128, 128)))[0:8]


def column_tile(row):
    return jnp.transpose(jnp.broadcast_to(row, (128, 128)))


def stack_rows(*rows):
    index = lax.broadcasted_iota(jnp.int32, (8, 128), 0)
    tile = jnp.zeros((8, 128), F32)
    for k, row in enumerate(rows):
        tile = jnp.where(index == k, row, tile)
    return tile


def kernel(
    hid, valid, parents, feat, gains, weight_hbm, targets_hbm,
    share_out, grad_hbm, feat_hbm,
    grad_out, feat_out, fall,
    weight, targets, zbuf, xall, normed, stat, cols, scols, rf, srow, gain,
    pk, pr, sb, rl, fin, lg, tst, stat_v, dot_v, gbuf, pf, ysb, yrl, yfin,
    qf, qs, zrs,
    local_sems, send_sems, f_sems, zr, xs, xr, yr, y2, sr, fr,
    f_near, f_far, f_pair,
    pair_s, pair_r, sb_s, rl_r, fin_r,
    sv_s, sv_r, dv_s, dv_r, sd_r, g_sems, g_near, g_far, g_pair,
    yrl_r, yfin_r, zs_s, zs_r, a_z, a_y, a_y2,
):
    at = Place()
    x, c, y, z, g, v = at.x, at.c, at.y, at.z, at.g, at.v
    up_z, down_z = at.at_z((z + 1) % NZ), at.at_z((z + NZ - 1) % NZ)
    up_y, down_y = at.at_y((y + 1) % NY), at.at_y((y + 3) % NY)

    load_weight = pltpu.make_async_copy(weight_hbm, weight, local_sems.at[0])
    load_targets = pltpu.make_async_copy(targets_hbm, targets, local_sems.at[1])
    load_weight.start()
    load_targets.start()

    with phase("A_feat"):
        live = (valid[...] == 1).astype(F32)
        row = lax.broadcasted_iota(jnp.int32, (128, 128), 0)
        lane = lax.broadcasted_iota(jnp.int32, (128, 128), 1)
        wanted = column_tile(parents[...].astype(F32)).astype(jnp.int32) + row // TREE * TREE
        pick = (lane == wanted).astype(BF16)
        chosen = jnp.dot(pick, feat[...], preferred_element_type=F32).astype(BF16)
        fall[g, 0] = chosen[:64]
        fall[g, 1] = chosen[64:]
        own_gain = gains[g]
        gain[...] = jnp.concatenate([own_gain[k : k + 1] for k in range(8)], axis=1)

    with phase("A_greet"):
        barrier = pltpu.get_barrier_semaphore()

        @pl.loop(1, 32)
        def _(k):
            pl.semaphore_signal(
                barrier,
                inc=1,
                device_id=(g, (v + k) % 32),
                device_id_type=pl.DeviceIdType.MESH,
            )

        @pl.loop(1, 8)
        def _(k):
            pl.semaphore_signal(
                barrier,
                inc=1,
                device_id=((g + k) % 8, v),
                device_id_type=pl.DeviceIdType.MESH,
            )

        pl.semaphore_wait(barrier, 38)
    send = Sender(send_sems)
    spread = Gather(at, fall, Sender(f_sems), f_near, f_far, f_pair)

    def to_slice(src, j):
        @pl.when(j != g)
        def _():
            remote(src, xall.at[y, g], xs.at[j], xr.at[g], at.dp(j)).start()

        @pl.when(j == g)
        def _():
            pltpu.make_async_copy(src, xall.at[y, g], xs.at[j]).start()

    def piece(ref, q):
        return ref.at[32 * q : 32 * q + 32]

    with phase("A_z"):
        for q in range(4):
            send(piece(hid, q), piece(zbuf.at[z], q), zr.at[q, z], up_z)
            send(piece(hid, q), piece(zbuf.at[z], q), zr.at[q, z], down_z)
        to_slice(hid, z)
        spread.start()
        for step in range(1, 5):
            low, high = (z + NZ - step) % NZ, (z + step) % NZ
            for q in range(4):
                block = piece(zbuf.at[low], q)
                arrived(block, zr.at[q, low], up_z, zr.at[q, low])
                if step < 4:
                    send(block, block, zr.at[q, low], up_z)
                    block = piece(zbuf.at[high], q)
                    arrived(block, zr.at[q, high], up_z, zr.at[q, high])
                    if step < 3:
                        send(block, block, zr.at[q, high], down_z)
            to_slice(zbuf.at[low], low)
            if step < 4:
                to_slice(zbuf.at[high], high)

    with phase("A_stat"):
        squares = jnp.square(hid[...].astype(F32))
        for k in range(1, NZ):
            squares = squares + jnp.square(zbuf[(z + k) % NZ].astype(F32))
        stat[y] = row_tile(jnp.sum(squares, axis=1, keepdims=True))
        for k in range(1, NY):
            send(stat.at[y], stat.at[y], sr.at[y], at.at_y((y + k) % NY))

    turns = (2, 1, 3, 0)

    def group(k):
        return 2 * ((x + turns[k // 2]) % NX) + k % 2

    def y_send(k):
        block = xall.at[y, group(k)]
        sem = xr.at[group(k)]
        if k < 6:
            arrived(block, sem, up_y, sem)
        else:

            @pl.when(c != k % 2)
            def _():
                arrived(block, sem, up_y, sem)

            @pl.when(c == k % 2)
            def _():
                pltpu.make_async_copy(hid, block, xs.at[g]).wait()

        send(block, block, yr.at[0, k], up_y)
        send(block, block, yr.at[1, k], down_y)

    def y_relay(k):
        for side, step in ((0, 3), (1, 1)):
            block = xall.at[(y + step) % NY, group(k)]
            arrived(block, yr.at[side, k], up_y, yr.at[side, k])
            if k % 2 == side:
                send(block, block, y2.at[k], up_y if side == 0 else down_y)
        if k + 3 < 8:
            y_send(k + 3)

    def y_far(k):
        block = xall.at[(y + 2) % NY, group(k)]
        arrived(block, y2.at[k], up_y, y2.at[k])

    def normalise(k):
        i = group(k)
        scale = cols[i]
        scale = jnp.concatenate([scale, scale], axis=1)
        rows = pl.ds(pl.multiple_of(i * 128, 128), 128)
        for part in range(NY):
            columns = slice(part * 256, part * 256 + 256)
            values = xall[part, i].astype(F32)
            normed[rows, columns] = (values * scale * gain[:, columns]).astype(BF16)

    def pair_copy(step, t):
        return remote(
            pk.at[step, t, 1 - c], pr.at[step, t],
            pair_s.at[step, t], pair_r.at[step, t], at.partner(),
        )

    def multiply(step, t):
        rows = pl.ds(pl.multiple_of(((x + step) % NX) * 256, 256), 256)
        tile = pl.ds(pl.multiple_of(t * 256, 256), 256)
        part = lax.dot_general(
            normed[rows, :],
            weight[tile, :],
            (((1,), (1,)), ((), ())),
            preferred_element_type=F32,
        )
        pk[step, t, 0] = part[:128]
        pk[step, t, 1] = part[128:]
        pair_copy(step, t).start()

    def total_of(step, t):
        arrived(pr.at[step, t], pair_r.at[step, t], at.partner(), pair_r.at[step, t])
        return pk[step, t, c] + pr[step, t]

    def ways(t):
        way = 1 + 2 * (t % 2)
        return way, 4 - way

    def first_hop(t):
        ahead, _ = ways(t)
        return remote(sb.at[t, 0], rl.at[t], sb_s.at[t, 0], rl_r.at[t], at.at_x((x + ahead) % NX))

    def direct(t):
        _, back = ways(t)
        return remote(
            sb.at[t, 1], fin.at[t, 0], sb_s.at[t, 1], fin_r.at[t, 0], at.at_x((x + back) % NX)
        )

    def onward(t):
        ahead, _ = ways(t)
        return remote(
            sb.at[t, 2], fin.at[t, 1], sb_s.at[t, 2], fin_r.at[t, 1], at.at_x((x + ahead) % NX)
        )

    def encode(t, k, value):
        top = jnp.max(jnp.abs(value), axis=0, keepdims=True)
        step = (120.0 / jnp.maximum(top, 1e-30)).astype(BF16)
        sb[t, k, 128:] = jnp.broadcast_to(step, (16, 256))
        step = sb[t, k, 128:].astype(F32)[0:1]
        sb[t, k, :128] = jnp.exp2(value * step).astype(BF16)

    def decode(block):
        step = block[128:].astype(F32)[0:1]
        return jnp.log2(block[:128].astype(F32)) * (1.0 / step)

    with phase("A_ysend"):
        for k in range(3):
            y_send(k)

    with phase("A_rf"):
        total = stat[y]
        for k in range(1, NY):
            other = (y + k) % NY
            arrived(stat.at[other], sr.at[other], up_y, sr.at[other])
            total = total + stat[other]
        factor = lax.rsqrt(total / (1024.0 * 8) + 1e-05)
        rf[g] = stack_rows(factor[0:1], live)
        for k in range(1, 8):
            send(rf.at[g], rf.at[g], fr.at[g], at.dp((g + k) % 8))

    with phase("A_y0123"):
        y_relay(0)
        y_relay(1)
        spread.middle(True)
        y_relay(2)
        for k in range(1, 8):
            other = (g + k) % 8
            arrived(rf.at[other], fr.at[other], up_y, fr.at[other])
        for i in range(8):
            cols[i] = column_tile(rf[i, 0:1])
        y_relay(3)
        load_weight.wait()
        load_targets.wait()
    with phase("A_far01"):
        y_far(0)
        y_far(1)
        normalise(0)
        normalise(1)
    with phase("F_hop"):

        @pl.loop(0, 9)
        def _(t):
            @pl.when(t < 8)
            def _():
                multiply(2, t)

            @pl.when(t > 0)
            def _():
                encode(t - 1, 0, total_of(2, t - 1))
                first_hop(t - 1).start()

    with phase("A_y56"):
        y_relay(4)
        y_relay(5)
        y_relay(6)
    with phase("A_far2345"):
        for k in range(2, 6):
            y_far(k)
            normalise(k)
    with phase("F_both"):

        def both(t):
            ahead, back = ways(t)
            encode(t, 1, total_of(back, t))
            direct(t).start()
            arrived(rl.at[t], rl_r.at[t], at.partner(), rl_r.at[t])
            encode(t, 2, total_of(ahead, t) + decode(rl.at[t]))
            onward(t).start()

        @pl.loop(0, 9)
        def _(t):
            @pl.when(t < 8)
            def _():
                multiply(1, t)
                multiply(3, t)

            @pl.when(t > 0)
            def _():
                both(t - 1)

        y_relay(7)

    with phase("A_far67"):
        spread.middle(False)
        for k in range(6, 8):
            y_far(k)
            normalise(k)
    with phase("F_mul0"):

        @pl.loop(0, 8)
        def _(t):
            multiply(0, t)

        top = jnp.max(targets[...].astype(F32), axis=1, keepdims=True)
        part = jnp.zeros((128, 256), F32)
        for k in range(8):
            part = part + jnp.exp(targets[:, k * 256 : k * 256 + 256].astype(F32) - top)
        tst[...] = stack_rows(
            jnp.zeros((1, 128), F32),
            jnp.zeros((1, 128), F32),
            row_tile(top)[0:1],
            row_tile(jnp.sum(part, axis=1, keepdims=True))[0:1],
        )

    with phase("F_fin"):

        @pl.loop(0, 8)
        def _(t):
            own = total_of(0, t)
            for k in range(2):
                arrived(fin.at[t, k], fin_r.at[t, k], at.partner(), fin_r.at[t, k])
            lg[t] = own + decode(fin.at[t, 0]) + decode(fin.at[t, 1])

    def tell_all(tile, send_sem, recv_sem):
        @pl.loop(1, 32)
        def _(k):
            remote(
                tile.at[v], tile.at[v], send_sem.at[k], recv_sem.at[v], (g, (v + k) % 32)
            ).start()

    def hear_all(tile, recv_sem):
        @pl.loop(1, 32)
        def _(k):
            other = (v + k) % 32
            arrived(tile.at[other], recv_sem.at[other], up_y, recv_sem.at[other])

    with phase("B_stat"):
        top = lg[0]
        for t in range(1, 8):
            top = jnp.maximum(top, lg[t])
        top = jnp.max(top, axis=1, keepdims=True)
        part = jnp.zeros((128, 256), F32)
        for t in range(8):
            part = part + jnp.exp(lg[t] - top)
        stat_v[v] = stack_rows(
            row_tile(top)[0:1],
            row_tile(jnp.sum(part, axis=1, keepdims=True))[0:1],
            tst[2:3],
            tst[3:4],
        )
        tell_all(stat_v, sv_s, sv_r)

    with phase("B_statv"):
        hear_all(stat_v, sv_r)
        wide = lambda row: jnp.concatenate([column_tile(row)] * 2, axis=1)
        tops, scales = [], []
        for k in (0, 2):
            top = jnp.max(stat_v[:, k, :], axis=0, keepdims=True)
            part = stat_v[:, k + 1, :] * jnp.exp(stat_v[:, k, :] - top)
            tops.append(wide(top))
            scales.append(wide(1.0 / jnp.sum(part, axis=0, keepdims=True)))
        count = jnp.zeros((1, 128), F32)
        for i in range(8):
            count = count + rf[i, 1:2]
        count = jnp.sum(count, axis=1, keepdims=True)
        scale = wide(1048576.0 * live / count)

    gather = Gather(at, gbuf, Sender(g_sems), g_near, g_far, g_pair)
    with phase("B_G"):
        acc = jnp.zeros((128, 256), F32)
        for t in range(8):
            draft = jnp.exp(lg[t] - tops[0]) * scales[0]
            target = (
                jnp.exp(targets[:, t * 256 : t * 256 + 256].astype(F32) - tops[1]) * scales[1]
            )
            value = (scale * (draft - target)).astype(BF16)
            for k in range(8):
                gbuf[g, k % 2, k // 2 * 16 : k // 2 * 16 + 16, t * 256 : t * 256 + 256] = value[
                    k * 16 : k * 16 + 16
                ]
            acc = acc + value.astype(F32) * lg[t]
        gather.start()
        dot_v[v] = row_tile(jnp.sum(acc, axis=1, keepdims=True))
        tell_all(dot_v, dv_s, dv_r)

    units = (((0, 0), (0, 1)), ((3, 0), (1, 1)), ((3, 1), (1, 0)), ((2, 0), (2, 1)))

    def block_of(step):
        return (x + step) % NX

    def backward(k):
        for step, half in units[k]:
            gather.paired(step, half)

        @pl.loop(0, 4)
        def _(n):
            columns = pl.ds(pl.multiple_of(n * 256, 256), 256)
            rows = jnp.concatenate(
                [
                    gbuf[pl.ds(2 * block_of(step), 2), half].reshape(128, 2048)
                    for step, half in units[k]
                ],
                axis=0,
            )
            part = jnp.dot(rows, weight[:, columns], preferred_element_type=F32)
            for p in range(2):
                for which in range(2):
                    for dest in range(NY):
                        row = p * 128 + which * 64 + dest * 16
                        pf[k, dest, p, which, :, columns] = part[row : row + 16]

        way = 1 if k % 2 == 0 else 3
        ysb[k, 0] = pf[k, (y + 2) % NY].astype(BF16)
        send(ysb.at[k, 0], yrl.at[k], yrl_r.at[k], at.at_y((y + way) % NY))
        ysb[k, 1] = pf[k, (y + 4 - way) % NY].astype(BF16)
        send(ysb.at[k, 1], yfin.at[k, 0], yfin_r.at[k, 0], at.at_y((y + 4 - way) % NY))

    def y_second(k):
        way = 1 if k % 2 == 0 else 3
        arrived(yrl.at[k], yrl_r.at[k], up_y, yrl_r.at[k])
        ysb[k, 2] = (pf[k, (y + way) % NY] + yrl[k].astype(F32)).astype(BF16)
        send(ysb.at[k, 2], yfin.at[k, 1], yfin_r.at[k, 1], at.at_y((y + way) % NY))

    def z_send(k, dest):
        return remote(
            qs.at[k, dest], zrs.at[k, z], zs_s.at[k, dest], zs_r.at[k, z], at.at_z(dest)
        )

    far_first = (4, 3, 5, 2, 6, 1, 7)

    def y_third(k):
        for j in range(2):
            arrived(yfin.at[k, j], yfin_r.at[k, j], up_y, yfin_r.at[k, j])
        value = pf[k, y] + yfin[k, 0].astype(F32) + yfin[k, 1].astype(F32)
        for owner in range(NZ):
            part = value[:, :, :, 128 * owner : 128 * owner + 128]
            qf[k, owner] = part
            qs[k, owner] = part.astype(BF16)
        for shift in far_first:
            z_send(k, (z + shift) % NZ).start()

    own_columns = pl.ds(pl.multiple_of(z * 128, 128), 128)

    def piece_of(k, owner):
        columns = pl.ds(pl.multiple_of(owner * 128, 128), 128)
        return grad_out.at[k, y, :, :, :, columns]

    def z_fourth(k):
        total = qf[k, z]
        for j in range(1, NZ):
            other = (z + j) % NZ
            arrived(zrs.at[k, other], zs_r.at[k, other], up_y, zs_r.at[k, other])
            total = total + zrs[k, other].astype(F32)
        lanes = pl.ds(pl.multiple_of((z % 2) * 128, 128), 128)
        for p, (step, half) in enumerate(units[k]):
            rows = pl.ds(pl.multiple_of(y * 32 + half * 16, 16), 16)
            for which in range(2):
                i = 2 * block_of(step) + which
                values = xall[z // 2, i, rows, lanes].astype(F32)
                grad = cols[i, rows, :] * gain[:, own_columns] * total[p, which]
                grad = grad - values * scols[i, rows, :]
                grad_out[k, y, p, which, :, own_columns] = grad.astype(BF16)
        mine = piece_of(k, z)
        for shift in far_first:
            send(mine, mine, a_z.at[k, z], at.at_z((z + shift) % NZ))

    def across(k):
        for j in (1, 7, 2, 6, 3, 5, 4):
            other = (z + j) % NZ
            arrived(piece_of(k, other), a_z.at[k, other], up_y, a_z.at[k, other])
        mine = grad_out.at[k, y]
        send(mine, mine, a_y.at[0, k], up_y)
        send(mine, mine, a_y.at[1, k], down_y)

    def across_relay(k):
        for side, step in ((0, 3), (1, 1)):
            block = grad_out.at[k, (y + step) % NY]
            arrived(block, a_y.at[side, k], up_y, a_y.at[side, k])
            half = grad_out.at[k, (y + step) % NY, side]
            send(half, half, a_y2.at[side, k], up_y if side == 0 else down_y)

    def to_hbm(k):
        return pltpu.make_async_copy(grad_out.at[k], grad_hbm.at[k], local_sems.at[2 + k])

    def across_far(k):
        for side in range(2):
            half = grad_out.at[k, (y + 2) % NY, side]
            arrived(half, a_y2.at[side, k], up_y, a_y2.at[side, k])
        to_hbm(k).start()

    feat_to_hbm = pltpu.make_async_copy(feat_out, feat_hbm, local_sems.at[6])

    with phase("G_bw0"):
        backward(0)
    with phase("G_feat"):
        spread.last()
        for step in (0, 1, 3):
            for half in range(2):
                spread.paired(step, half)
    with phase("G_mid"):
        gather.middle(True)
    with phase("G_ys0"):
        y_second(0)
    with phase("G_bw1"):
        backward(1)
    with phase("G_dot"):
        hear_all(dot_v, dv_r)
        dot = jnp.sum(dot_v[:, 0, :], axis=0, keepdims=True)
        factor = rf[g][0:1]
        srow[g] = jnp.broadcast_to(factor * factor * dot / (1024.0 * 8), (8, 128))
        for k in range(1, 8):
            send(srow.at[g], srow.at[g], sd_r.at[g], at.dp((g + k) % 8))
    with phase("G_yt0"):
        y_third(0)
    with phase("G_mid2"):
        gather.middle(False)
    with phase("G_ys1"):
        y_second(1)
    with phase("G_bw2"):
        backward(2)
    with phase("G_s"):
        for k in range(1, 8):
            other = (g + k) % 8
            arrived(srow.at[other], sd_r.at[other], up_y, sd_r.at[other])
        for i in range(8):
            scols[i] = column_tile(srow[i, 0:1])
    with phase("G_z0"):
        z_fourth(0)
    with phase("G_yt1"):
        y_third(1)
    with phase("G_last"):
        gather.last()
    with phase("G_ys2"):
        y_second(2)
    with phase("G_bw3"):
        backward(3)
    with phase("H_ax0"):
        across(0)
    with phase("H_z1"):
        z_fourth(1)
    with phase("H_yt2"):
        y_third(2)
    with phase("H_feat"):
        spread.paired(2, 0)
        spread.paired(2, 1)
        for k in range(4):
            for p, (step, half) in enumerate(units[k]):
                for which in range(2):
                    for dest in range(NY):
                        row = dest % 2 * 32 + half * 16
                        feat_out[k, dest, p, which] = fall[
                            2 * block_of(step) + which, dest // 2, row : row + 16, :
                        ]
        feat_to_hbm.start()
    with phase("H_ys3"):
        y_second(3)
    with phase("H_ar0"):
        across_relay(0)
    with phase("H_ax1"):
        across(1)
    with phase("H_z2"):
        z_fourth(2)
    with phase("H_yt3"):
        y_third(3)
    with phase("H_ar1"):
        across_far(0)
        across_relay(1)
    with phase("H_ax2"):
        across(2)
    with phase("H_z3"):
        z_fourth(3)
    with phase("H_ar2"):
        across_far(1)
        across_relay(2)
    with phase("H_ax3"):
        across(3)
    with phase("H_far2"):
        across_far(2)
    with phase("H_ar3"):
        across_relay(3)
    with phase("H_far"):
        across_far(3)
        away = (z // 2 + NX - x) % NX
        odd, side = away % 2, away // 2
        for half in range(2):
            k = odd * (1 + (half + side + 1) % 2) + (1 - odd) * 3 * side
            p = odd * (1 - side) + (1 - odd) * half
            share_out[16 * half : 16 * half + 16, :] = grad_out[k, y, p, z % 2]
        for k in range(4):
            to_hbm(k).wait()
        feat_to_hbm.wait()

    with phase("H_drain"):

        @pl.loop(0, 8)
        def _(t):
            for step in range(4):
                pair_copy(step, t).wait_send()
            first_hop(t).wait_send()
            direct(t).wait_send()
            onward(t).wait_send()

        @pl.loop(1, 32)
        def _(k):
            other = (g, (v + k) % 32)
            remote(stat_v.at[v], stat_v.at[v], sv_s.at[k], sv_r.at[v], other).wait_send()
            remote(dot_v.at[v], dot_v.at[v], dv_s.at[k], dv_r.at[v], other).wait_send()

        send.drain()
        spread.send.drain()
        gather.send.drain()
        for k in range(4):
            for j in range(1, NZ):
                z_send(k, (z + j) % NZ).wait_send()
        for j in range(8):

            @pl.when(g != j)
            def _():
                remote(hid, xall.at[y, g], xs.at[j], xr.at[g], at.dp(j)).wait_send()


VMEM = pl.BlockSpec(memory_space=pltpu.VMEM)
HBM = pl.BlockSpec(memory_space=pl.ANY)
LIMIT = 60 * 1024 * 1024


def call(*operands):
    return pl.pallas_call(
        kernel,
        out_shape=(
            jax.ShapeDtypeStruct((32, 1024), BF16),
            jax.ShapeDtypeStruct((4, NY, 2, 2, 16, 1024), BF16),
            jax.ShapeDtypeStruct((4, NY, 2, 2, 16, 768), BF16),
        ),
        in_specs=[VMEM] * 5 + [HBM] * 2,
        out_specs=[VMEM, HBM, HBM],
        scratch_shapes=[
            pltpu.VMEM((4, NY, 2, 2, 16, 1024), BF16),
            pltpu.VMEM((4, NY, 2, 2, 16, 768), BF16),
            pltpu.VMEM((8, 2, 64, 768), BF16),
            pltpu.VMEM((2048, 1024), BF16),
            pltpu.VMEM((128, 2048), BF16),
            pltpu.VMEM((NZ, 128, 256), BF16),
            pltpu.VMEM((NY, 8, 128, 256), BF16),
            pltpu.VMEM((1024, 1024), BF16),
            pltpu.VMEM((NY, 8, 128), F32),
            pltpu.VMEM((8, 128, 128), F32),
            pltpu.VMEM((8, 128, 128), F32),
            pltpu.VMEM((8, 8, 128), F32),
            pltpu.VMEM((8, 8, 128), F32),
            pltpu.VMEM((1, 1024), F32),
            pltpu.VMEM((NX, 8, 2, 128, 256), F32),
            pltpu.VMEM((NX, 8, 128, 256), F32),
            pltpu.VMEM((8, 3, 144, 256), BF16),
            pltpu.VMEM((8, 144, 256), BF16),
            pltpu.VMEM((8, 2, 144, 256), BF16),
            pltpu.VMEM((8, 128, 256), F32),
            pltpu.VMEM((8, 128), F32),
            pltpu.VMEM((32, 8, 128), F32),
            pltpu.VMEM((32, 8, 128), F32),
            pltpu.VMEM((8, 2, 64, 2048), BF16),
            pltpu.VMEM((4, NY, 2, 2, 16, 1024), F32),
            pltpu.VMEM((4, 3, 2, 2, 16, 1024), BF16),
            pltpu.VMEM((4, 2, 2, 16, 1024), BF16),
            pltpu.VMEM((4, 2, 2, 2, 16, 1024), BF16),
            pltpu.VMEM((4, NZ, 2, 2, 16, 128), F32),
            pltpu.VMEM((4, NZ, 2, 2, 16, 128), BF16),
            pltpu.VMEM((4, NZ, 2, 2, 16, 128), BF16),
            DMA((7,)),
            DMA((140,)),
            DMA((GATHER_SENDS,)),
            DMA((4, NZ)),
            DMA((8,)),
            DMA((8,)),
            DMA((2, 8)),
            DMA((8,)),
            DMA((NY,)),
            DMA((8,)),
            DMA((2, 2)),
            DMA((2,)),
            DMA((4, 2)),
            DMA((NX, 8)),
            DMA((NX, 8)),
            DMA((8, 3)),
            DMA((8,)),
            DMA((8, 2)),
            DMA((32,)),
            DMA((32,)),
            DMA((32,)),
            DMA((32,)),
            DMA((8,)),
            DMA((GATHER_SENDS,)),
            DMA((2, 2)),
            DMA((2,)),
            DMA((4, 2)),
            DMA((4,)),
            DMA((4, 2)),
            DMA((4, NZ)),
            DMA((4, NZ)),
            DMA((4, NZ)),
            DMA((2, 4)),
            DMA((2, 4)),
        ],
        compiler_params=pltpu.CompilerParams(
            collective_id=0, has_side_effects=True, vmem_limit_bytes=LIMIT
        ),
    )(*operands)


def body(hidden, norm_gain, head_weight, target_logits, valid_rows, parents, features):
    share, grad, parent_features = call(
        hidden,
        valid_rows.reshape(1, 128),
        parents.reshape(1, 128),
        features,
        norm_gain.reshape(8, 8, 128),
        head_weight,
        target_logits,
    )
    grad_joining = lax.dot_general(
        grad.reshape(1024, 1024),
        parent_features.reshape(1024, 768),
        (((0,), (0,)), ((), ())),
        preferred_element_type=F32,
    )
    return (share, grad_joining)


def solution(mesh):
    placed = (
        P("dp", "vocab"),
        P(),
        P("vocab", "dp"),
        P("dp", "vocab"),
        P("dp"),
        P("dp"),
        P("dp", "vocab"),
    )
    return jax.shard_map(
        body,
        mesh=mesh,
        in_specs=placed,
        out_specs=(P("vocab", "dp"), P("dp", "vocab")),
        check_vma=False,
    )
```

```python
import contextlib

import jax
import jax.numpy as jnp
from jax import lax
from jax.experimental import pallas as pl
from jax.experimental.pallas import tpu as pltpu
from jax.sharding import PartitionSpec as P

TREE = 64
NX, NC, NY, NZ = 4, 2, 4, 8
F32, BF16 = jnp.float32, jnp.bfloat16
DMA = pltpu.SemaphoreType.DMA


def remote(src, dst, send_sem, recv_sem, device):
    return pltpu.make_async_remote_copy(
        src_ref=src,
        dst_ref=dst,
        send_sem=send_sem,
        recv_sem=recv_sem,
        device_id=device,
        device_id_type=pl.DeviceIdType.MESH,
    )


def phase(name):
    return contextlib.nullcontext()


class Place:
    def __init__(self):
        self.g = lax.axis_index("dp")
        self.v = lax.axis_index("vocab")
        self.x, self.c = self.g // NC, self.g % NC
        self.z, self.y = self.v // NY, self.v % NY

    def dp(self, i):
        return (i, self.v)

    def at_x(self, x):
        return (x * NC + self.c, self.v)

    def partner(self):
        return (self.x * NC + 1 - self.c, self.v)

    def at_y(self, y):
        return (self.g, self.z * NY + y)

    def at_z(self, z):
        return (self.g, z * NY + self.y)


class Sender:
    def __init__(self, sems):
        self.sems, self.used, self.copies = sems, 0, []

    def __call__(self, src, dst, recv_sem, device):
        assert self.used < self.sems.shape[0]
        copy = remote(src, dst, self.sems.at[self.used], recv_sem, device)
        self.used += 1
        copy.start()
        self.copies.append(copy)

    def drain(self):
        for copy in self.copies:
            copy.wait_send()


def arrived(dst, recv_sem, device, any_sem):
    remote(dst, dst, any_sem, recv_sem, device).wait_recv()


class Gather:
    def __init__(self, at, buf, send, near, far, pair):
        self.at, self.buf, self.send = at, buf, send
        self.near, self.far, self.pair = near, far, pair

    def slot(self, step, core):
        return ((self.at.x + step) % NX) * NC + core

    def start(self):
        at, buf = self.at, self.buf
        up, down = at.at_x((at.x + 1) % NX), at.at_x((at.x + 3) % NX)
        for k in range(2):
            for side, half, device in ((0, k, up), (1, 1 - k, down)):
                mine = buf.at[at.g, half]
                self.send(mine, mine, self.near.at[side, half], device)
            mine = buf.at[at.g, k]
            self.send(mine, mine, self.pair.at[0, k], at.partner())

    def middle(self, first):
        at, buf = self.at, self.buf
        for side, step in ((0, 3), (1, 1)):
            half = side if first else 1 - side
            block = buf.at[self.slot(step, at.c), half]
            arrived(block, self.near.at[side, half], at.partner(), self.near.at[side, half])
            if first:
                onward = at.at_x((at.x + (1 if side == 0 else 3)) % NX)
                self.send(block, block, self.far.at[half], onward)
            self.send(block, block, self.pair.at[step, half], at.partner())

    def last(self):
        at, buf = self.at, self.buf
        for half in range(2):
            block = buf.at[self.slot(2, at.c), half]
            arrived(block, self.far.at[half], at.partner(), self.far.at[half])
            self.send(block, block, self.pair.at[2, half], at.partner())

    def paired(self, step, half):
        at = self.at
        block = self.buf.at[self.slot(step, 1 - at.c), half]
        arrived(block, self.pair.at[step, half], at.partner(), self.pair.at[step, half])


GATHER_SENDS = 14


def row_tile(column):
    return jnp.transpose(jnp.broadcast_to(column, (128, 128)))[0:8]


def column_tile(row):
    return jnp.transpose(jnp.broadcast_to(row, (128, 128)))


def stack_rows(*rows):
    index = lax.broadcasted_iota(jnp.int32, (8, 128), 0)
    tile = jnp.zeros((8, 128), F32)
    for k, row in enumerate(rows):
        tile = jnp.where(index == k, row, tile)
    return tile


def kernel(
    hid, valid, parents, feat, gains, weight_hbm, targets_hbm,
    share_out, joined_hbm, grad_hbm, feat_hbm,
    joined, grad_out, feat_out, fall,
    weight, targets, zbuf, xall, normed, stat, cols, scols, rf, srow, gain,
    pk, pr, sb, rl, fin, lg, tst, stat_v, dot_v, gbuf, pf, ysb, yrl, yfin,
    qf, qs, zrs,
    local_sems, send_sems, f_sems, zr, xs, xr, yr, y2, sr, fr,
    f_near, f_far, f_pair,
    pair_s, pair_r, sb_s, rl_r, fin_r,
    sv_s, sv_r, dv_s, dv_r, sd_r, g_sems, g_near, g_far, g_pair,
    yrl_r, yfin_r, zs_s, zs_r, a_z, a_y, a_y2,
):
    at = Place()
    x, c, y, z, g, v = at.x, at.c, at.y, at.z, at.g, at.v
    up_z, down_z = at.at_z((z + 1) % NZ), at.at_z((z + NZ - 1) % NZ)
    up_y, down_y = at.at_y((y + 1) % NY), at.at_y((y + 3) % NY)

    load_weight = pltpu.make_async_copy(weight_hbm, weight, local_sems.at[0])
    load_targets = pltpu.make_async_copy(targets_hbm, targets, local_sems.at[1])
    load_weight.start()
    load_targets.start()

    with phase("A_feat"):
        live = (valid[...] == 1).astype(F32)
        row = lax.broadcasted_iota(jnp.int32, (128, 128), 0)
        lane = lax.broadcasted_iota(jnp.int32, (128, 128), 1)
        wanted = column_tile(parents[...].astype(F32)).astype(jnp.int32) + row // TREE * TREE
        pick = (lane == wanted).astype(BF16)
        chosen = jnp.dot(pick, feat[...], preferred_element_type=F32).astype(BF16)
        fall[g, 0] = chosen[:64]
        fall[g, 1] = chosen[64:]
        own_gain = gains[g]
        gain[...] = jnp.concatenate([own_gain[k : k + 1] for k in range(8)], axis=1)

    with phase("A_greet"):
        barrier = pltpu.get_barrier_semaphore()

        @pl.loop(1, 32)
        def _(k):
            pl.semaphore_signal(
                barrier,
                inc=1,
                device_id=(g, (v + k) % 32),
                device_id_type=pl.DeviceIdType.MESH,
            )

        @pl.loop(1, 8)
        def _(k):
            pl.semaphore_signal(
                barrier,
                inc=1,
                device_id=((g + k) % 8, v),
                device_id_type=pl.DeviceIdType.MESH,
            )

        pl.semaphore_wait(barrier, 38)
    send = Sender(send_sems)
    spread = Gather(at, fall, Sender(f_sems), f_near, f_far, f_pair)

    def to_slice(src, j):
        @pl.when(j != g)
        def _():
            remote(src, xall.at[y, g], xs.at[j], xr.at[g], at.dp(j)).start()

        @pl.when(j == g)
        def _():
            pltpu.make_async_copy(src, xall.at[y, g], xs.at[j]).start()

    def piece(ref, q):
        return ref.at[32 * q : 32 * q + 32]

    with phase("A_z"):
        for q in range(4):
            send(piece(hid, q), piece(zbuf.at[z], q), zr.at[q, z], up_z)
            send(piece(hid, q), piece(zbuf.at[z], q), zr.at[q, z], down_z)
        to_slice(hid, z)
        spread.start()
        for step in range(1, 5):
            low, high = (z + NZ - step) % NZ, (z + step) % NZ
            for q in range(4):
                block = piece(zbuf.at[low], q)
                arrived(block, zr.at[q, low], up_z, zr.at[q, low])
                if step < 4:
                    send(block, block, zr.at[q, low], up_z)
                    block = piece(zbuf.at[high], q)
                    arrived(block, zr.at[q, high], up_z, zr.at[q, high])
                    if step < 3:
                        send(block, block, zr.at[q, high], down_z)
            to_slice(zbuf.at[low], low)
            if step < 4:
                to_slice(zbuf.at[high], high)

    with phase("A_stat"):
        squares = jnp.square(hid[...].astype(F32))
        for k in range(1, NZ):
            squares = squares + jnp.square(zbuf[(z + k) % NZ].astype(F32))
        stat[y] = row_tile(jnp.sum(squares, axis=1, keepdims=True))
        for k in range(1, NY):
            send(stat.at[y], stat.at[y], sr.at[y], at.at_y((y + k) % NY))

    turns = (2, 1, 3, 0)

    def group(k):
        return 2 * ((x + turns[k // 2]) % NX) + k % 2

    def y_send(k):
        block = xall.at[y, group(k)]
        sem = xr.at[group(k)]
        if k < 6:
            arrived(block, sem, up_y, sem)
        else:

            @pl.when(c != k % 2)
            def _():
                arrived(block, sem, up_y, sem)

            @pl.when(c == k % 2)
            def _():
                pltpu.make_async_copy(hid, block, xs.at[g]).wait()

        send(block, block, yr.at[0, k], up_y)
        send(block, block, yr.at[1, k], down_y)

    def y_relay(k):
        for side, step in ((0, 3), (1, 1)):
            block = xall.at[(y + step) % NY, group(k)]
            arrived(block, yr.at[side, k], up_y, yr.at[side, k])
            if k % 2 == side:
                send(block, block, y2.at[k], up_y if side == 0 else down_y)
        if k + 3 < 8:
            y_send(k + 3)

    def y_far(k):
        block = xall.at[(y + 2) % NY, group(k)]
        arrived(block, y2.at[k], up_y, y2.at[k])

    def normalise(k):
        i = group(k)
        scale = cols[i]
        scale = jnp.concatenate([scale, scale], axis=1)
        rows = pl.ds(pl.multiple_of(i * 128, 128), 128)
        for part in range(NY):
            columns = slice(part * 256, part * 256 + 256)
            values = xall[part, i].astype(F32)
            normed[rows, columns] = (values * scale * gain[:, columns]).astype(BF16)

    def pair_copy(step, t):
        return remote(
            pk.at[step, t, 1 - c], pr.at[step, t],
            pair_s.at[step, t], pair_r.at[step, t], at.partner(),
        )

    def multiply(step, t):
        rows = pl.ds(pl.multiple_of(((x + step) % NX) * 256, 256), 256)
        tile = pl.ds(pl.multiple_of(t * 256, 256), 256)
        part = lax.dot_general(
            normed[rows, :],
            weight[tile, :],
            (((1,), (1,)), ((), ())),
            preferred_element_type=F32,
        )
        pk[step, t, 0] = part[:128]
        pk[step, t, 1] = part[128:]
        pair_copy(step, t).start()

    def total_of(step, t):
        arrived(pr.at[step, t], pair_r.at[step, t], at.partner(), pair_r.at[step, t])
        return pk[step, t, c] + pr[step, t]

    def ways(t):
        way = 1 + 2 * (t % 2)
        return way, 4 - way

    def first_hop(t):
        ahead, _ = ways(t)
        return remote(sb.at[t, 0], rl.at[t], sb_s.at[t, 0], rl_r.at[t], at.at_x((x + ahead) % NX))

    def direct(t):
        _, back = ways(t)
        return remote(
            sb.at[t, 1], fin.at[t, 0], sb_s.at[t, 1], fin_r.at[t, 0], at.at_x((x + back) % NX)
        )

    def onward(t):
        ahead, _ = ways(t)
        return remote(
            sb.at[t, 2], fin.at[t, 1], sb_s.at[t, 2], fin_r.at[t, 1], at.at_x((x + ahead) % NX)
        )

    def encode(t, k, value):
        top = jnp.max(jnp.abs(value), axis=0, keepdims=True)
        step = (120.0 / jnp.maximum(top, 1e-30)).astype(BF16)
        sb[t, k, 128:] = jnp.broadcast_to(step, (16, 256))
        step = sb[t, k, 128:].astype(F32)[0:1]
        sb[t, k, :128] = jnp.exp2(value * step).astype(BF16)

    def decode(block):
        step = block[128:].astype(F32)[0:1]
        return jnp.log2(block[:128].astype(F32)) * (1.0 / step)

    with phase("A_ysend"):
        for k in range(3):
            y_send(k)

    with phase("A_rf"):
        total = stat[y]
        for k in range(1, NY):
            other = (y + k) % NY
            arrived(stat.at[other], sr.at[other], up_y, sr.at[other])
            total = total + stat[other]
        factor = lax.rsqrt(total / (1024.0 * 8) + 1e-05)
        rf[g] = stack_rows(factor[0:1], live)
        for k in range(1, 8):
            send(rf.at[g], rf.at[g], fr.at[g], at.dp((g + k) % 8))

    with phase("A_y0123"):
        y_relay(0)
        y_relay(1)
        spread.middle(True)
        y_relay(2)
        for k in range(1, 8):
            other = (g + k) % 8
            arrived(rf.at[other], fr.at[other], up_y, fr.at[other])
        for i in range(8):
            cols[i] = column_tile(rf[i, 0:1])
        y_relay(3)
        load_weight.wait()
        load_targets.wait()
    with phase("A_far01"):
        y_far(0)
        y_far(1)
        normalise(0)
        normalise(1)
    def run(low, high, *stages):
        @pl.loop(low, high)
        def _(t):
            for stage, lag in stages:
                stage(t - lag)

    def hop(t):
        encode(t, 0, total_of(2, t))
        first_hop(t).start()

    with phase("F_hop"):
        far_rows = (lambda t: multiply(2, t)), 0
        run(0, 3, far_rows)
        run(3, 6, far_rows, (hop, 3))
        y_relay(4)
        run(6, 8, far_rows, (hop, 3))
        y_relay(5)
        run(5, 8, (hop, 0))
    with phase("A_y6"):
        y_relay(6)
    with phase("A_far2345"):
        for k in range(2, 6):
            y_far(k)
            normalise(k)
    with phase("F_both"):

        def both(t):
            ahead, back = ways(t)
            encode(t, 1, total_of(back, t))
            direct(t).start()
            arrived(rl.at[t], rl_r.at[t], at.partner(), rl_r.at[t])
            encode(t, 2, total_of(ahead, t) + decode(rl.at[t]))
            onward(t).start()

        def near_rows(t):
            multiply(1, t)
            multiply(3, t)

        run(0, 3, (near_rows, 0))
        run(3, 5, (near_rows, 0), (both, 3))
        y_relay(7)
        run(5, 8, (near_rows, 0), (both, 3))
        run(5, 8, (both, 0))

    with phase("A_far67"):
        spread.middle(False)
        top = jnp.max(targets[...].astype(F32), axis=1, keepdims=True)
        part = jnp.zeros((128, 256), F32)
        for k in range(8):
            part = part + jnp.exp(targets[:, k * 256 : k * 256 + 256].astype(F32) - top)
        tst[...] = stack_rows(
            jnp.zeros((1, 128), F32),
            jnp.zeros((1, 128), F32),
            row_tile(top)[0:1],
            row_tile(jnp.sum(part, axis=1, keepdims=True))[0:1],
        )
        for k in range(6, 8):
            y_far(k)
            normalise(k)

    def finish(t):
        own = total_of(0, t)
        for k in range(2):
            arrived(fin.at[t, k], fin_r.at[t, k], at.partner(), fin_r.at[t, k])
        lg[t] = own + decode(fin.at[t, 0]) + decode(fin.at[t, 1])

    with phase("F_fin"):
        own_rows = (lambda t: multiply(0, t)), 0
        run(0, 3, own_rows)
        run(3, 8, own_rows, (finish, 3))
        run(5, 8, (finish, 0))

    def tell_all(tile, send_sem, recv_sem):
        @pl.loop(1, 32)
        def _(k):
            remote(
                tile.at[v], tile.at[v], send_sem.at[k], recv_sem.at[v], (g, (v + k) % 32)
            ).start()

    def hear_all(tile, recv_sem):
        @pl.loop(1, 32)
        def _(k):
            other = (v + k) % 32
            arrived(tile.at[other], recv_sem.at[other], up_y, recv_sem.at[other])

    with phase("B_stat"):
        top = lg[0]
        for t in range(1, 8):
            top = jnp.maximum(top, lg[t])
        top = jnp.max(top, axis=1, keepdims=True)
        part = jnp.zeros((128, 256), F32)
        for t in range(8):
            part = part + jnp.exp(lg[t] - top)
        stat_v[v] = stack_rows(
            row_tile(top)[0:1],
            row_tile(jnp.sum(part, axis=1, keepdims=True))[0:1],
            tst[2:3],
            tst[3:4],
        )
        tell_all(stat_v, sv_s, sv_r)

    with phase("B_statv"):
        hear_all(stat_v, sv_r)
        wide = lambda row: jnp.concatenate([column_tile(row)] * 2, axis=1)
        tops, scales = [], []
        for k in (0, 2):
            top = jnp.max(stat_v[:, k, :], axis=0, keepdims=True)
            part = stat_v[:, k + 1, :] * jnp.exp(stat_v[:, k, :] - top)
            tops.append(wide(top))
            scales.append(wide(1.0 / jnp.sum(part, axis=0, keepdims=True)))
        count = jnp.zeros((1, 128), F32)
        for i in range(8):
            count = count + rf[i, 1:2]
        count = jnp.sum(count, axis=1, keepdims=True)
        scale = wide(1048576.0 * live / count)

    gather = Gather(at, gbuf, Sender(g_sems), g_near, g_far, g_pair)
    with phase("B_G"):
        acc = jnp.zeros((128, 256), F32)
        for t in range(8):
            draft = jnp.exp(lg[t] - tops[0]) * scales[0]
            target = (
                jnp.exp(targets[:, t * 256 : t * 256 + 256].astype(F32) - tops[1]) * scales[1]
            )
            value = (scale * (draft - target)).astype(BF16)
            for k in range(8):
                gbuf[g, k % 2, k // 2 * 16 : k // 2 * 16 + 16, t * 256 : t * 256 + 256] = value[
                    k * 16 : k * 16 + 16
                ]
            acc = acc + value.astype(F32) * lg[t]
        gather.start()
        dot_v[v] = row_tile(jnp.sum(acc, axis=1, keepdims=True))
        tell_all(dot_v, dv_s, dv_r)

    units = (((0, 0), (0, 1)), ((3, 0), (1, 1)), ((3, 1), (1, 0)), ((2, 0), (2, 1)))

    def block_of(step):
        return (x + step) % NX

    def backward(k):
        for step, half in units[k]:
            gather.paired(step, half)

        @pl.loop(0, 4)
        def _(n):
            columns = pl.ds(pl.multiple_of(n * 256, 256), 256)
            rows = jnp.concatenate(
                [
                    gbuf[pl.ds(2 * block_of(step), 2), half].reshape(128, 2048)
                    for step, half in units[k]
                ],
                axis=0,
            )
            part = jnp.dot(rows, weight[:, columns], preferred_element_type=F32)
            for p in range(2):
                for which in range(2):
                    for dest in range(NY):
                        row = p * 128 + which * 64 + dest * 16
                        pf[k, dest, p, which, :, columns] = part[row : row + 16]

        way = 1 if k % 2 == 0 else 3
        ysb[k, 0] = pf[k, (y + 2) % NY].astype(BF16)
        send(ysb.at[k, 0], yrl.at[k], yrl_r.at[k], at.at_y((y + way) % NY))
        ysb[k, 1] = pf[k, (y + 4 - way) % NY].astype(BF16)
        send(ysb.at[k, 1], yfin.at[k, 0], yfin_r.at[k, 0], at.at_y((y + 4 - way) % NY))

    def y_second(k):
        way = 1 if k % 2 == 0 else 3
        arrived(yrl.at[k], yrl_r.at[k], up_y, yrl_r.at[k])
        ysb[k, 2] = (pf[k, (y + way) % NY] + yrl[k].astype(F32)).astype(BF16)
        send(ysb.at[k, 2], yfin.at[k, 1], yfin_r.at[k, 1], at.at_y((y + way) % NY))

    def z_send(k, dest):
        return remote(
            qs.at[k, dest], zrs.at[k, z], zs_s.at[k, dest], zs_r.at[k, z], at.at_z(dest)
        )

    far_first = (4, 3, 5, 2, 6, 1, 7)

    def y_third(k):
        for j in range(2):
            arrived(yfin.at[k, j], yfin_r.at[k, j], up_y, yfin_r.at[k, j])
        value = pf[k, y] + yfin[k, 0].astype(F32) + yfin[k, 1].astype(F32)
        for owner in range(NZ):
            part = value[:, :, :, 128 * owner : 128 * owner + 128]
            qf[k, owner] = part
            qs[k, owner] = part.astype(BF16)
        for shift in far_first:
            z_send(k, (z + shift) % NZ).start()

    own_columns = pl.ds(pl.multiple_of(z * 128, 128), 128)

    def piece_of(k, owner):
        columns = pl.ds(pl.multiple_of(owner * 128, 128), 128)
        return grad_out.at[k, y, :, :, :, columns]

    def z_fourth(k):
        total = qf[k, z]
        for j in range(1, NZ):
            other = (z + j) % NZ
            arrived(zrs.at[k, other], zs_r.at[k, other], up_y, zs_r.at[k, other])
            total = total + zrs[k, other].astype(F32)
        lanes = pl.ds(pl.multiple_of((z % 2) * 128, 128), 128)
        for p, (step, half) in enumerate(units[k]):
            rows = pl.ds(pl.multiple_of(y * 32 + half * 16, 16), 16)
            for which in range(2):
                i = 2 * block_of(step) + which
                values = xall[z // 2, i, rows, lanes].astype(F32)
                grad = cols[i, rows, :] * gain[:, own_columns] * total[p, which]
                grad = grad - values * scols[i, rows, :]
                grad_out[k, y, p, which, :, own_columns] = grad.astype(BF16)
        mine = piece_of(k, z)
        for shift in far_first:
            send(mine, mine, a_z.at[k, z], at.at_z((z + shift) % NZ))

    def across(k):
        for j in (1, 7, 2, 6, 3, 5, 4):
            other = (z + j) % NZ
            arrived(piece_of(k, other), a_z.at[k, other], up_y, a_z.at[k, other])
        mine = grad_out.at[k, y]
        send(mine, mine, a_y.at[0, k], up_y)
        send(mine, mine, a_y.at[1, k], down_y)

    def across_relay(k):
        for side, step in ((0, 3), (1, 1)):
            block = grad_out.at[k, (y + step) % NY]
            arrived(block, a_y.at[side, k], up_y, a_y.at[side, k])
            half = grad_out.at[k, (y + step) % NY, side]
            send(half, half, a_y2.at[side, k], up_y if side == 0 else down_y)

    grad_to_hbm = pltpu.make_async_copy(grad_out.at[3], grad_hbm, local_sems.at[2])
    feat_to_hbm = pltpu.make_async_copy(feat_out.at[3], feat_hbm, local_sems.at[3])
    acc_to_hbm = pltpu.make_async_copy(joined, joined_hbm, local_sems.at[4])

    def fold(k):
        @pl.loop(0, 4)
        def _(n):
            columns = pl.ds(pl.multiple_of(n * 256, 256), 256)
            part = lax.dot_general(
                grad_out[k, :, :, :, :, columns].reshape(256, 256),
                feat_out[k].reshape(256, 768),
                (((0,), (0,)), ((), ())),
                preferred_element_type=F32,
            )
            if k == 0:
                joined[columns, :] = part
            else:
                joined[columns, :] += part

    def across_far(k):
        for side in range(2):
            half = grad_out.at[k, (y + 2) % NY, side]
            arrived(half, a_y2.at[side, k], up_y, a_y2.at[side, k])

    with phase("G_bw0"):
        backward(0)
    with phase("G_feat"):
        spread.last()
        for step in (0, 1, 3):
            for half in range(2):
                spread.paired(step, half)
    with phase("G_dot"):
        hear_all(dot_v, dv_r)
        dot = jnp.sum(dot_v[:, 0, :], axis=0, keepdims=True)
        factor = rf[g][0:1]
        srow[g] = jnp.broadcast_to(factor * factor * dot / (1024.0 * 8), (8, 128))
        for k in range(1, 8):
            send(srow.at[g], srow.at[g], sd_r.at[g], at.dp((g + k) % 8))
    with phase("G_mid"):
        gather.middle(True)
    with phase("G_ys0"):
        y_second(0)
    with phase("G_bw1"):
        backward(1)
    with phase("G_yt0"):
        y_third(0)
    with phase("G_mid2"):
        gather.middle(False)
    with phase("G_ys1"):
        y_second(1)
    with phase("G_bw2"):
        backward(2)
    with phase("G_s"):
        for k in range(1, 8):
            other = (g + k) % 8
            arrived(srow.at[other], sd_r.at[other], up_y, sd_r.at[other])
        for i in range(8):
            scols[i] = column_tile(srow[i, 0:1])
    with phase("G_z0"):
        z_fourth(0)
    with phase("G_yt1"):
        y_third(1)
    with phase("G_last"):
        gather.last()
    with phase("G_ys2"):
        y_second(2)
    with phase("G_bw3"):
        backward(3)
    with phase("H_ax0"):
        across(0)
    with phase("H_z1"):
        z_fourth(1)
    with phase("H_yt2"):
        y_third(2)
    with phase("H_feat"):
        spread.paired(2, 0)
        spread.paired(2, 1)
        for k in range(4):
            for p, (step, half) in enumerate(units[k]):
                for which in range(2):
                    for dest in range(NY):
                        row = dest % 2 * 32 + half * 16
                        feat_out[k, dest, p, which] = fall[
                            2 * block_of(step) + which, dest // 2, row : row + 16, :
                        ]
        feat_to_hbm.start()
    with phase("H_ys3"):
        y_second(3)
    with phase("H_ar0"):
        across_relay(0)
    with phase("H_ax1"):
        across(1)
    with phase("H_z2"):
        z_fourth(2)
    with phase("H_yt3"):
        y_third(3)
    with phase("H_far0"):
        across_far(0)
    with phase("H_fold0"):
        fold(0)
    with phase("H_ar1"):
        across_relay(1)
    with phase("H_ax2"):
        across(2)
    with phase("H_z3"):
        z_fourth(3)
    with phase("H_far1"):
        across_far(1)
    with phase("H_fold1"):
        fold(1)
    with phase("H_ar2"):
        across_relay(2)
    with phase("H_ax3"):
        across(3)
    with phase("H_far2"):
        across_far(2)
    with phase("H_fold2"):
        fold(2)
        acc_to_hbm.start()
    with phase("H_ar3"):
        across_relay(3)
    with phase("H_far"):
        across_far(3)
        grad_to_hbm.start()
        away = (z // 2 + NX - x) % NX
        odd, side = away % 2, away // 2
        for half in range(2):
            k = odd * (1 + (half + side + 1) % 2) + (1 - odd) * 3 * side
            p = odd * (1 - side) + (1 - odd) * half
            share_out[16 * half : 16 * half + 16, :] = grad_out[k, y, p, z % 2]
        grad_to_hbm.wait()
        feat_to_hbm.wait()
        acc_to_hbm.wait()

    with phase("H_drain"):

        @pl.loop(0, 8)
        def _(t):
            for step in range(4):
                pair_copy(step, t).wait_send()
            first_hop(t).wait_send()
            direct(t).wait_send()
            onward(t).wait_send()

        @pl.loop(1, 32)
        def _(k):
            other = (g, (v + k) % 32)
            remote(stat_v.at[v], stat_v.at[v], sv_s.at[k], sv_r.at[v], other).wait_send()
            remote(dot_v.at[v], dot_v.at[v], dv_s.at[k], dv_r.at[v], other).wait_send()

        send.drain()
        spread.send.drain()
        gather.send.drain()
        for k in range(4):
            for j in range(1, NZ):
                z_send(k, (z + j) % NZ).wait_send()
        for j in range(8):

            @pl.when(g != j)
            def _():
                remote(hid, xall.at[y, g], xs.at[j], xr.at[g], at.dp(j)).wait_send()


VMEM = pl.BlockSpec(memory_space=pltpu.VMEM)
HBM = pl.BlockSpec(memory_space=pl.ANY)
LIMIT = 60 * 1024 * 1024


def call(*operands):
    return pl.pallas_call(
        kernel,
        out_shape=(
            jax.ShapeDtypeStruct((32, 1024), BF16),
            jax.ShapeDtypeStruct((1024, 768), F32),
            jax.ShapeDtypeStruct((NY, 2, 2, 16, 1024), BF16),
            jax.ShapeDtypeStruct((NY, 2, 2, 16, 768), BF16),
        ),
        in_specs=[VMEM] * 5 + [HBM] * 2,
        out_specs=[VMEM, HBM, HBM, HBM],
        scratch_shapes=[
            pltpu.VMEM((1024, 768), F32),
            pltpu.VMEM((4, NY, 2, 2, 16, 1024), BF16),
            pltpu.VMEM((4, NY, 2, 2, 16, 768), BF16),
            pltpu.VMEM((8, 2, 64, 768), BF16),
            pltpu.VMEM((2048, 1024), BF16),
            pltpu.VMEM((128, 2048), BF16),
            pltpu.VMEM((NZ, 128, 256), BF16),
            pltpu.VMEM((NY, 8, 128, 256), BF16),
            pltpu.VMEM((1024, 1024), BF16),
            pltpu.VMEM((NY, 8, 128), F32),
            pltpu.VMEM((8, 128, 128), F32),
            pltpu.VMEM((8, 128, 128), F32),
            pltpu.VMEM((8, 8, 128), F32),
            pltpu.VMEM((8, 8, 128), F32),
            pltpu.VMEM((1, 1024), F32),
            pltpu.VMEM((NX, 8, 2, 128, 256), F32),
            pltpu.VMEM((NX, 8, 128, 256), F32),
            pltpu.VMEM((8, 3, 144, 256), BF16),
            pltpu.VMEM((8, 144, 256), BF16),
            pltpu.VMEM((8, 2, 144, 256), BF16),
            pltpu.VMEM((8, 128, 256), F32),
            pltpu.VMEM((8, 128), F32),
            pltpu.VMEM((32, 8, 128), F32),
            pltpu.VMEM((32, 8, 128), F32),
            pltpu.VMEM((8, 2, 64, 2048), BF16),
            pltpu.VMEM((4, NY, 2, 2, 16, 1024), F32),
            pltpu.VMEM((4, 3, 2, 2, 16, 1024), BF16),
            pltpu.VMEM((4, 2, 2, 16, 1024), BF16),
            pltpu.VMEM((4, 2, 2, 2, 16, 1024), BF16),
            pltpu.VMEM((4, NZ, 2, 2, 16, 128), F32),
            pltpu.VMEM((4, NZ, 2, 2, 16, 128), BF16),
            pltpu.VMEM((4, NZ, 2, 2, 16, 128), BF16),
            DMA((7,)),
            DMA((140,)),
            DMA((GATHER_SENDS,)),
            DMA((4, NZ)),
            DMA((8,)),
            DMA((8,)),
            DMA((2, 8)),
            DMA((8,)),
            DMA((NY,)),
            DMA((8,)),
            DMA((2, 2)),
            DMA((2,)),
            DMA((4, 2)),
            DMA((NX, 8)),
            DMA((NX, 8)),
            DMA((8, 3)),
            DMA((8,)),
            DMA((8, 2)),
            DMA((32,)),
            DMA((32,)),
            DMA((32,)),
            DMA((32,)),
            DMA((8,)),
            DMA((GATHER_SENDS,)),
            DMA((2, 2)),
            DMA((2,)),
            DMA((4, 2)),
            DMA((4,)),
            DMA((4, 2)),
            DMA((4, NZ)),
            DMA((4, NZ)),
            DMA((4, NZ)),
            DMA((2, 4)),
            DMA((2, 4)),
        ],
        compiler_params=pltpu.CompilerParams(
            collective_id=0, has_side_effects=True, vmem_limit_bytes=LIMIT
        ),
    )(*operands)


def body(hidden, norm_gain, head_weight, target_logits, valid_rows, parents, features):
    share, joined, grad, parent_features = call(
        hidden,
        valid_rows.reshape(1, 128),
        parents.reshape(1, 128),
        features,
        norm_gain.reshape(8, 8, 128),
        head_weight,
        target_logits,
    )
    grad_joining = joined + lax.dot_general(
        *lax.optimization_barrier(
            (grad.reshape(256, 1024), parent_features.reshape(256, 768))
        ),
        (((0,), (0,)), ((), ())),
        preferred_element_type=F32,
    )
    return (share, grad_joining)


def solution(mesh):
    placed = (
        P("dp", "vocab"),
        P(),
        P("vocab", "dp"),
        P("dp", "vocab"),
        P("dp"),
        P("dp"),
        P("dp", "vocab"),
    )
    return jax.shard_map(
        body,
        mesh=mesh,
        in_specs=placed,
        out_specs=(P("vocab", "dp"), P("dp", "vocab")),
        check_vma=False,
    )
```

```python
import contextlib

import jax
import jax.numpy as jnp
from jax import lax
from jax.experimental import pallas as pl
from jax.experimental.pallas import tpu as pltpu
from jax.sharding import PartitionSpec as P

TREE = 64
NX, NC, NY, NZ = 4, 2, 4, 8
F32, BF16 = jnp.float32, jnp.bfloat16
DMA = pltpu.SemaphoreType.DMA


def remote(src, dst, send_sem, recv_sem, device):
    return pltpu.make_async_remote_copy(
        src_ref=src,
        dst_ref=dst,
        send_sem=send_sem,
        recv_sem=recv_sem,
        device_id=device,
        device_id_type=pl.DeviceIdType.MESH,
    )


def phase(name):
    return contextlib.nullcontext()


class Place:
    def __init__(self):
        self.g = lax.axis_index("dp")
        self.v = lax.axis_index("vocab")
        self.x, self.c = self.g // NC, self.g % NC
        self.z, self.y = self.v // NY, self.v % NY

    def dp(self, i):
        return (i, self.v)

    def at_x(self, x):
        return (x * NC + self.c, self.v)

    def partner(self):
        return (self.x * NC + 1 - self.c, self.v)

    def at_y(self, y):
        return (self.g, self.z * NY + y)

    def at_z(self, z):
        return (self.g, z * NY + self.y)


class Sender:
    def __init__(self, sems):
        self.sems, self.used, self.copies = sems, 0, []

    def __call__(self, src, dst, recv_sem, device):
        assert self.used < self.sems.shape[0]
        copy = remote(src, dst, self.sems.at[self.used], recv_sem, device)
        self.used += 1
        copy.start()
        self.copies.append(copy)

    def drain(self):
        for copy in self.copies:
            copy.wait_send()


def arrived(dst, recv_sem, device, any_sem):
    remote(dst, dst, any_sem, recv_sem, device).wait_recv()


class Gather:
    def __init__(self, at, buf, send, near, far, pair):
        self.at, self.buf, self.send = at, buf, send
        self.near, self.far, self.pair = near, far, pair

    def slot(self, step, core):
        return ((self.at.x + step) % NX) * NC + core

    def start(self):
        at, buf = self.at, self.buf
        up, down = at.at_x((at.x + 1) % NX), at.at_x((at.x + 3) % NX)
        for k in range(2):
            for side, half, device in ((0, k, up), (1, 1 - k, down)):
                mine = buf.at[at.g, half]
                self.send(mine, mine, self.near.at[side, half], device)
            mine = buf.at[at.g, k]
            self.send(mine, mine, self.pair.at[0, k], at.partner())

    def middle(self, first):
        at, buf = self.at, self.buf
        for side, step in ((0, 3), (1, 1)):
            half = side if first else 1 - side
            block = buf.at[self.slot(step, at.c), half]
            arrived(block, self.near.at[side, half], at.partner(), self.near.at[side, half])
            if first:
                onward = at.at_x((at.x + (1 if side == 0 else 3)) % NX)
                self.send(block, block, self.far.at[half], onward)
            self.send(block, block, self.pair.at[step, half], at.partner())

    def last(self):
        at, buf = self.at, self.buf
        for half in range(2):
            block = buf.at[self.slot(2, at.c), half]
            arrived(block, self.far.at[half], at.partner(), self.far.at[half])
            self.send(block, block, self.pair.at[2, half], at.partner())

    def paired(self, step, half):
        at = self.at
        block = self.buf.at[self.slot(step, 1 - at.c), half]
        arrived(block, self.pair.at[step, half], at.partner(), self.pair.at[step, half])


GATHER_SENDS = 14


def row_tile(column):
    return jnp.transpose(jnp.broadcast_to(column, (128, 128)))[0:8]


def column_tile(row):
    return jnp.transpose(jnp.broadcast_to(row, (128, 128)))


def stack_rows(*rows):
    index = lax.broadcasted_iota(jnp.int32, (8, 128), 0)
    tile = jnp.zeros((8, 128), F32)
    for k, row in enumerate(rows):
        tile = jnp.where(index == k, row, tile)
    return tile


def kernel(
    hid, valid, parents, feat, gains, weight_hbm, targets_hbm,
    share_out, joined_hbm, grad_hbm, feat_hbm,
    joined, grad_out, feat_out, fall,
    weight, targets, zbuf, xall, normed, stat, cols, scols, rf, srow, gain,
    pk, pr, sb, rl, fin, lg, tst, stat_v, dot_v, gbuf, pf, ysb, yrl, yfin,
    qf, qs, zrs,
    local_sems, send_sems, f_sems, zr, xs, xr, yr, y2, sr, fr,
    f_near, f_far, f_pair,
    pair_s, pair_r, sb_s, rl_r, fin_r,
    sv_s, sv_r, dv_s, dv_r, sd_r, g_sems, g_near, g_far, g_pair,
    yrl_r, yfin_r, zs_s, zs_r, a_z, a_y, a_y2,
):
    at = Place()
    x, c, y, z, g, v = at.x, at.c, at.y, at.z, at.g, at.v
    up_z, down_z = at.at_z((z + 1) % NZ), at.at_z((z + NZ - 1) % NZ)
    up_y, down_y = at.at_y((y + 1) % NY), at.at_y((y + 3) % NY)

    load_weight = pltpu.make_async_copy(weight_hbm, weight, local_sems.at[0])
    load_targets = pltpu.make_async_copy(targets_hbm, targets, local_sems.at[1])
    load_weight.start()
    load_targets.start()

    with phase("A_feat"):
        live = (valid[...] == 1).astype(F32)
        row = lax.broadcasted_iota(jnp.int32, (128, 128), 0)
        lane = lax.broadcasted_iota(jnp.int32, (128, 128), 1)
        wanted = column_tile(parents[...].astype(F32)).astype(jnp.int32) + row // TREE * TREE
        pick = (lane == wanted).astype(BF16)
        chosen = jnp.dot(pick, feat[...], preferred_element_type=F32).astype(BF16)
        fall[g, 0] = chosen[:64]
        fall[g, 1] = chosen[64:]
        own_gain = gains[g]
        gain[...] = jnp.concatenate([own_gain[k : k + 1] for k in range(8)], axis=1)

    with phase("A_greet"):
        barrier = pltpu.get_barrier_semaphore()

        @pl.loop(1, 32)
        def _(k):
            pl.semaphore_signal(
                barrier,
                inc=1,
                device_id=(g, (v + k) % 32),
                device_id_type=pl.DeviceIdType.MESH,
            )

        @pl.loop(1, 8)
        def _(k):
            pl.semaphore_signal(
                barrier,
                inc=1,
                device_id=((g + k) % 8, v),
                device_id_type=pl.DeviceIdType.MESH,
            )

        pl.semaphore_wait(barrier, 38)
    send = Sender(send_sems)
    spread = Gather(at, fall, Sender(f_sems), f_near, f_far, f_pair)

    def to_slice(src, j):
        @pl.when(j != g)
        def _():
            remote(src, xall.at[y, g], xs.at[j], xr.at[g], at.dp(j)).start()

        @pl.when(j == g)
        def _():
            pltpu.make_async_copy(src, xall.at[y, g], xs.at[j]).start()

    def piece(ref, q):
        return ref.at[32 * q : 32 * q + 32]

    with phase("A_z"):
        for q in range(4):
            send(piece(hid, q), piece(zbuf.at[z], q), zr.at[q, z], up_z)
            send(piece(hid, q), piece(zbuf.at[z], q), zr.at[q, z], down_z)
        to_slice(hid, z)
        spread.start()
        for step in range(1, 5):
            low, high = (z + NZ - step) % NZ, (z + step) % NZ
            for q in range(4):
                block = piece(zbuf.at[low], q)
                arrived(block, zr.at[q, low], up_z, zr.at[q, low])
                if step < 4:
                    send(block, block, zr.at[q, low], up_z)
                    block = piece(zbuf.at[high], q)
                    arrived(block, zr.at[q, high], up_z, zr.at[q, high])
                    if step < 3:
                        send(block, block, zr.at[q, high], down_z)
            to_slice(zbuf.at[low], low)
            if step < 4:
                to_slice(zbuf.at[high], high)

    with phase("A_stat"):
        squares = jnp.square(hid[...].astype(F32))
        for k in range(1, NZ):
            squares = squares + jnp.square(zbuf[(z + k) % NZ].astype(F32))
        stat[y] = row_tile(jnp.sum(squares, axis=1, keepdims=True))
        for k in range(1, NY):
            send(stat.at[y], stat.at[y], sr.at[y], at.at_y((y + k) % NY))

    turns = (2, 1, 3, 0)

    def group(k):
        return 2 * ((x + turns[k // 2]) % NX) + k % 2

    def y_send(k):
        block = xall.at[y, group(k)]
        sem = xr.at[group(k)]
        if k < 6:
            arrived(block, sem, up_y, sem)
        else:

            @pl.when(c != k % 2)
            def _():
                arrived(block, sem, up_y, sem)

            @pl.when(c == k % 2)
            def _():
                pltpu.make_async_copy(hid, block, xs.at[g]).wait()

        send(block, block, yr.at[0, k], up_y)
        send(block, block, yr.at[1, k], down_y)

    def y_relay(k):
        for side, step in ((0, 3), (1, 1)):
            block = xall.at[(y + step) % NY, group(k)]
            arrived(block, yr.at[side, k], up_y, yr.at[side, k])
            if k % 2 == side:
                send(block, block, y2.at[k], up_y if side == 0 else down_y)
        if k + 3 < 8:
            y_send(k + 3)

    def y_far(k):
        block = xall.at[(y + 2) % NY, group(k)]
        arrived(block, y2.at[k], up_y, y2.at[k])

    def normalise(k):
        i = group(k)
        scale = cols[i]
        scale = jnp.concatenate([scale, scale], axis=1)
        rows = pl.ds(pl.multiple_of(i * 128, 128), 128)
        for part in range(NY):
            columns = slice(part * 256, part * 256 + 256)
            values = xall[part, i].astype(F32)
            normed[rows, columns] = (values * scale * gain[:, columns]).astype(BF16)

    def pair_copy(step, t):
        return remote(
            pk.at[step, t, 1 - c], pr.at[step, t],
            pair_s.at[step, t], pair_r.at[step, t], at.partner(),
        )

    def multiply(step, t):
        rows = pl.ds(pl.multiple_of(((x + step) % NX) * 256, 256), 256)
        tile = pl.ds(pl.multiple_of(t * 256, 256), 256)
        part = lax.dot_general(
            normed[rows, :],
            weight[tile, :],
            (((1,), (1,)), ((), ())),
            preferred_element_type=F32,
        )
        pk[step, t, 0] = part[:128]
        pk[step, t, 1] = part[128:]
        pair_copy(step, t).start()

    def total_of(step, t):
        arrived(pr.at[step, t], pair_r.at[step, t], at.partner(), pair_r.at[step, t])
        return pk[step, t, c] + pr[step, t]

    def ways(t):
        way = 1 + 2 * (t % 2)
        return way, 4 - way

    def first_hop(t):
        ahead, _ = ways(t)
        return remote(sb.at[t, 0], rl.at[t], sb_s.at[t, 0], rl_r.at[t], at.at_x((x + ahead) % NX))

    def direct(t):
        _, back = ways(t)
        return remote(
            sb.at[t, 1], fin.at[t, 0], sb_s.at[t, 1], fin_r.at[t, 0], at.at_x((x + back) % NX)
        )

    def onward(t):
        ahead, _ = ways(t)
        return remote(
            sb.at[t, 2], fin.at[t, 1], sb_s.at[t, 2], fin_r.at[t, 1], at.at_x((x + ahead) % NX)
        )

    def encode(t, k, value):
        left, right = value[:, :128], value[:, 128:]
        top = jnp.max(jnp.maximum(jnp.abs(left), jnp.abs(right)), axis=0, keepdims=True)
        step = (120.0 / jnp.maximum(top, 1e-30)).astype(BF16)
        sb[t, k, 256:] = jnp.broadcast_to(step, (16, 128))
        step = sb[t, k, 256:].astype(F32)[0:1]
        sb[t, k, :128] = jnp.exp2(left * step).astype(BF16)
        sb[t, k, 128:256] = jnp.exp2(right * step).astype(BF16)

    def decode(block):
        size = 1.0 / block[256:].astype(F32)[0:1]
        return jnp.concatenate(
            [
                jnp.log2(block[:128].astype(F32)) * size,
                jnp.log2(block[128:256].astype(F32)) * size,
            ],
            axis=1,
        )

    with phase("A_ysend"):
        for k in range(3):
            y_send(k)

    with phase("A_rf"):
        total = stat[y]
        for k in range(1, NY):
            other = (y + k) % NY
            arrived(stat.at[other], sr.at[other], up_y, sr.at[other])
            total = total + stat[other]
        factor = lax.rsqrt(total / (1024.0 * 8) + 1e-05)
        rf[g] = stack_rows(factor[0:1], live)
        for k in range(1, 8):
            send(rf.at[g], rf.at[g], fr.at[g], at.dp((g + k) % 8))

    with phase("A_y0123"):
        y_relay(0)
        y_relay(1)
        spread.middle(True)
        y_relay(2)
        for k in range(1, 8):
            other = (g + k) % 8
            arrived(rf.at[other], fr.at[other], up_y, fr.at[other])
        for i in range(8):
            cols[i] = column_tile(rf[i, 0:1])
        y_relay(3)
        load_weight.wait()
        load_targets.wait()
    with phase("A_far01"):
        y_far(0)
        y_far(1)
        normalise(0)
        normalise(1)
    def run(low, high, *stages):
        @pl.loop(low, high)
        def _(t):
            for stage, lag in stages:
                stage(t - lag)

    def hop(t):
        encode(t, 0, total_of(2, t))
        first_hop(t).start()

    with phase("F_hop"):
        far_rows = (lambda t: multiply(2, t)), 0
        run(0, 3, far_rows)
        run(3, 6, far_rows, (hop, 3))
        y_relay(4)
        run(6, 8, far_rows, (hop, 3))
        y_relay(5)
        run(5, 8, (hop, 0))
    with phase("A_y6"):
        y_relay(6)
    with phase("A_far2345"):
        for k in range(2, 6):
            y_far(k)
            normalise(k)
    with phase("F_both"):

        def both(t):
            ahead, back = ways(t)
            encode(t, 1, total_of(back, t))
            direct(t).start()
            arrived(rl.at[t], rl_r.at[t], at.partner(), rl_r.at[t])
            encode(t, 2, total_of(ahead, t) + decode(rl.at[t]))
            onward(t).start()

        def near_rows(t):
            multiply(1, t)
            multiply(3, t)

        run(0, 3, (near_rows, 0))
        run(3, 5, (near_rows, 0), (both, 3))
        y_relay(7)
        run(5, 8, (near_rows, 0), (both, 3))
        run(5, 8, (both, 0))

    with phase("A_far67"):
        spread.middle(False)
        top = jnp.max(targets[...].astype(F32), axis=1, keepdims=True)
        part = jnp.zeros((128, 256), F32)
        for k in range(8):
            part = part + jnp.exp(targets[:, k * 256 : k * 256 + 256].astype(F32) - top)
        tst[...] = stack_rows(
            jnp.zeros((1, 128), F32),
            jnp.zeros((1, 128), F32),
            row_tile(top)[0:1],
            row_tile(jnp.sum(part, axis=1, keepdims=True))[0:1],
        )
        for k in range(6, 8):
            y_far(k)
            normalise(k)

    def finish(t):
        own = total_of(0, t)
        for k in range(2):
            arrived(fin.at[t, k], fin_r.at[t, k], at.partner(), fin_r.at[t, k])
        lg[t] = own + decode(fin.at[t, 0]) + decode(fin.at[t, 1])

    with phase("F_fin"):
        own_rows = (lambda t: multiply(0, t)), 0
        run(0, 3, own_rows)
        run(3, 8, own_rows, (finish, 3))
        run(5, 8, (finish, 0))

    def tell_all(tile, send_sem, recv_sem):
        @pl.loop(1, 32)
        def _(k):
            remote(
                tile.at[v], tile.at[v], send_sem.at[k], recv_sem.at[v], (g, (v + k) % 32)
            ).start()

    def hear_all(tile, recv_sem):
        @pl.loop(1, 32)
        def _(k):
            other = (v + k) % 32
            arrived(tile.at[other], recv_sem.at[other], up_y, recv_sem.at[other])

    with phase("B_stat"):
        top = lg[0]
        for t in range(1, 8):
            top = jnp.maximum(top, lg[t])
        top = jnp.max(top, axis=1, keepdims=True)
        part = jnp.zeros((128, 256), F32)
        for t in range(8):
            part = part + jnp.exp(lg[t] - top)
        stat_v[v] = stack_rows(
            row_tile(top)[0:1],
            row_tile(jnp.sum(part, axis=1, keepdims=True))[0:1],
            tst[2:3],
            tst[3:4],
        )
        tell_all(stat_v, sv_s, sv_r)

    with phase("B_statv"):
        hear_all(stat_v, sv_r)
        wide = lambda row: jnp.concatenate([column_tile(row)] * 2, axis=1)
        tops, scales = [], []
        for k in (0, 2):
            top = jnp.max(stat_v[:, k, :], axis=0, keepdims=True)
            part = stat_v[:, k + 1, :] * jnp.exp(stat_v[:, k, :] - top)
            tops.append(wide(top))
            scales.append(wide(1.0 / jnp.sum(part, axis=0, keepdims=True)))
        count = jnp.zeros((1, 128), F32)
        for i in range(8):
            count = count + rf[i, 1:2]
        count = jnp.sum(count, axis=1, keepdims=True)
        scale = wide(1048576.0 * live / count)

    gather = Gather(at, gbuf, Sender(g_sems), g_near, g_far, g_pair)
    with phase("B_G"):
        acc = jnp.zeros((128, 256), F32)
        for t in range(8):
            draft = jnp.exp(lg[t] - tops[0]) * scales[0]
            target = (
                jnp.exp(targets[:, t * 256 : t * 256 + 256].astype(F32) - tops[1]) * scales[1]
            )
            value = (scale * (draft - target)).astype(BF16)
            for k in range(8):
                gbuf[g, k % 2, k // 2 * 16 : k // 2 * 16 + 16, t * 256 : t * 256 + 256] = value[
                    k * 16 : k * 16 + 16
                ]
            acc = acc + value.astype(F32) * lg[t]
        gather.start()
        dot_v[v] = row_tile(jnp.sum(acc, axis=1, keepdims=True))
        tell_all(dot_v, dv_s, dv_r)

    units = (((0, 0), (0, 1)), ((3, 0), (1, 1)), ((3, 1), (1, 0)), ((2, 0), (2, 1)))

    def block_of(step):
        return (x + step) % NX

    def backward(k):
        for step, half in units[k]:
            gather.paired(step, half)

        @pl.loop(0, 4)
        def _(n):
            columns = pl.ds(pl.multiple_of(n * 256, 256), 256)
            rows = jnp.concatenate(
                [
                    gbuf[pl.ds(2 * block_of(step), 2), half].reshape(128, 2048)
                    for step, half in units[k]
                ],
                axis=0,
            )
            part = jnp.dot(rows, weight[:, columns], preferred_element_type=F32)
            for p in range(2):
                for which in range(2):
                    for dest in range(NY):
                        row = p * 128 + which * 64 + dest * 16
                        pf[k, dest, p, which, :, columns] = part[row : row + 16]

        way = 1 if k % 2 == 0 else 3
        ysb[k, 0] = pf[k, (y + 2) % NY].astype(BF16)
        send(ysb.at[k, 0], yrl.at[k], yrl_r.at[k], at.at_y((y + way) % NY))
        ysb[k, 1] = pf[k, (y + 4 - way) % NY].astype(BF16)
        send(ysb.at[k, 1], yfin.at[k, 0], yfin_r.at[k, 0], at.at_y((y + 4 - way) % NY))

    def y_second(k):
        way = 1 if k % 2 == 0 else 3
        arrived(yrl.at[k], yrl_r.at[k], up_y, yrl_r.at[k])
        ysb[k, 2] = (pf[k, (y + way) % NY] + yrl[k].astype(F32)).astype(BF16)
        send(ysb.at[k, 2], yfin.at[k, 1], yfin_r.at[k, 1], at.at_y((y + way) % NY))

    def z_send(k, dest):
        return remote(
            qs.at[k, dest], zrs.at[k, z], zs_s.at[k, dest], zs_r.at[k, z], at.at_z(dest)
        )

    far_first = (4, 3, 5, 2, 6, 1, 7)

    def y_third(k):
        for j in range(2):
            arrived(yfin.at[k, j], yfin_r.at[k, j], up_y, yfin_r.at[k, j])
        value = pf[k, y] + yfin[k, 0].astype(F32) + yfin[k, 1].astype(F32)
        for owner in range(NZ):
            part = value[:, :, :, 128 * owner : 128 * owner + 128]
            qf[k, owner] = part
            qs[k, owner] = part.astype(BF16)
        for shift in far_first:
            z_send(k, (z + shift) % NZ).start()

    own_columns = pl.ds(pl.multiple_of(z * 128, 128), 128)

    def piece_of(k, owner):
        columns = pl.ds(pl.multiple_of(owner * 128, 128), 128)
        return grad_out.at[k, y, :, :, :, columns]

    def z_fourth(k):
        total = qf[k, z]
        for j in range(1, NZ):
            other = (z + j) % NZ
            arrived(zrs.at[k, other], zs_r.at[k, other], up_y, zs_r.at[k, other])
            total = total + zrs[k, other].astype(F32)
        lanes = pl.ds(pl.multiple_of((z % 2) * 128, 128), 128)
        for p, (step, half) in enumerate(units[k]):
            rows = pl.ds(pl.multiple_of(y * 32 + half * 16, 16), 16)
            for which in range(2):
                i = 2 * block_of(step) + which
                values = xall[z // 2, i, rows, lanes].astype(F32)
                grad = cols[i, rows, :] * gain[:, own_columns] * total[p, which]
                grad = grad - values * scols[i, rows, :]
                grad_out[k, y, p, which, :, own_columns] = grad.astype(BF16)
        mine = piece_of(k, z)
        for shift in far_first:
            send(mine, mine, a_z.at[k, z], at.at_z((z + shift) % NZ))

    def across(k):
        for j in (1, 7, 2, 6, 3, 5, 4):
            other = (z + j) % NZ
            arrived(piece_of(k, other), a_z.at[k, other], up_y, a_z.at[k, other])
        for turn in range(2):
            for side, device in ((0, up_y), (1, down_y)):
                p = side if turn == 0 else 1 - side
                mine = grad_out.at[k, y, p]
                send(mine, mine, a_y.at[side, k, p], device)

    def across_near(k, side, p):
        half = grad_out.at[k, (y + (3 if side == 0 else 1)) % NY, p]
        arrived(half, a_y.at[side, k, p], up_y, a_y.at[side, k, p])
        return half

    def across_relay(k):
        for side in range(2):
            half = across_near(k, side, side)
            send(half, half, a_y2.at[side, k], up_y if side == 0 else down_y)

    grad_to_hbm = pltpu.make_async_copy(grad_out.at[3], grad_hbm, local_sems.at[2])
    feat_to_hbm = pltpu.make_async_copy(feat_out.at[3], feat_hbm, local_sems.at[3])
    acc_to_hbm = pltpu.make_async_copy(joined, joined_hbm, local_sems.at[4])

    def fold(k):
        @pl.loop(0, 4)
        def _(n):
            columns = pl.ds(pl.multiple_of(n * 256, 256), 256)
            part = lax.dot_general(
                grad_out[k, :, :, :, :, columns].reshape(256, 256),
                feat_out[k].reshape(256, 768),
                (((0,), (0,)), ((), ())),
                preferred_element_type=F32,
            )
            if k == 0:
                joined[columns, :] = part
            else:
                joined[columns, :] += part

    def across_far(k):
        for side in range(2):
            across_near(k, side, 1 - side)
        for side in range(2):
            half = grad_out.at[k, (y + 2) % NY, side]
            arrived(half, a_y2.at[side, k], up_y, a_y2.at[side, k])

    with phase("G_bw0"):
        backward(0)
    with phase("G_feat"):
        spread.last()
        for step in (0, 1, 3):
            for half in range(2):
                spread.paired(step, half)
    with phase("G_dot"):
        hear_all(dot_v, dv_r)
        dot = jnp.sum(dot_v[:, 0, :], axis=0, keepdims=True)
        factor = rf[g][0:1]
        srow[g] = jnp.broadcast_to(factor * factor * dot / (1024.0 * 8), (8, 128))
        for k in range(1, 8):
            send(srow.at[g], srow.at[g], sd_r.at[g], at.dp((g + k) % 8))
    with phase("G_mid"):
        gather.middle(True)
    with phase("G_ys0"):
        y_second(0)
    with phase("G_bw1"):
        backward(1)
    with phase("G_yt0"):
        y_third(0)
    with phase("G_mid2"):
        gather.middle(False)
    with phase("G_ys1"):
        y_second(1)
    with phase("G_bw2"):
        backward(2)
    with phase("G_s"):
        for k in range(1, 8):
            other = (g + k) % 8
            arrived(srow.at[other], sd_r.at[other], up_y, sd_r.at[other])
        for i in range(8):
            scols[i] = column_tile(srow[i, 0:1])
    with phase("G_z0"):
        z_fourth(0)
    with phase("G_last"):
        gather.last()
    with phase("G_bw3"):
        backward(3)
    with phase("G_yt1"):
        y_third(1)
    with phase("G_ys2"):
        y_second(2)
    with phase("H_ax0"):
        across(0)
    with phase("H_feat"):
        spread.paired(2, 0)
        spread.paired(2, 1)
        for k in range(4):
            for p, (step, half) in enumerate(units[k]):
                for which in range(2):
                    for dest in range(NY):
                        row = dest % 2 * 32 + half * 16
                        feat_out[k, dest, p, which] = fall[
                            2 * block_of(step) + which, dest // 2, row : row + 16, :
                        ]
        feat_to_hbm.start()
    with phase("H_ys3"):
        y_second(3)
    with phase("H_ar0"):
        across_relay(0)
    with phase("H_yt2"):
        y_third(2)
    with phase("H_z1"):
        z_fourth(1)
    with phase("H_yt3"):
        y_third(3)
    with phase("H_z2"):
        z_fourth(2)
    with phase("H_ax1"):
        across(1)
    with phase("H_far0"):
        across_far(0)
    with phase("H_fold0"):
        fold(0)
    with phase("H_ar1"):
        across_relay(1)
    with phase("H_z3"):
        z_fourth(3)
    with phase("H_ax2"):
        across(2)
    with phase("H_far1"):
        across_far(1)
    with phase("H_fold1"):
        fold(1)
    with phase("H_ar2"):
        across_relay(2)
    with phase("H_ax3"):
        across(3)
    with phase("H_far2"):
        across_far(2)
    with phase("H_ar3"):
        across_relay(3)
    with phase("H_fold2"):
        fold(2)
        acc_to_hbm.start()
    with phase("H_far"):
        across_far(3)
        grad_to_hbm.start()
        away = (z // 2 + NX - x) % NX
        odd, side = away % 2, away // 2
        for half in range(2):
            k = odd * (1 + (half + side + 1) % 2) + (1 - odd) * 3 * side
            p = odd * (1 - side) + (1 - odd) * half
            share_out[16 * half : 16 * half + 16, :] = grad_out[k, y, p, z % 2]
        grad_to_hbm.wait()
        feat_to_hbm.wait()
        acc_to_hbm.wait()

    with phase("H_drain"):

        @pl.loop(0, 8)
        def _(t):
            for step in range(4):
                pair_copy(step, t).wait_send()
            first_hop(t).wait_send()
            direct(t).wait_send()
            onward(t).wait_send()

        @pl.loop(1, 32)
        def _(k):
            other = (g, (v + k) % 32)
            remote(stat_v.at[v], stat_v.at[v], sv_s.at[k], sv_r.at[v], other).wait_send()
            remote(dot_v.at[v], dot_v.at[v], dv_s.at[k], dv_r.at[v], other).wait_send()

        send.drain()
        spread.send.drain()
        gather.send.drain()
        for k in range(4):
            for j in range(1, NZ):
                z_send(k, (z + j) % NZ).wait_send()
        for j in range(8):

            @pl.when(g != j)
            def _():
                remote(hid, xall.at[y, g], xs.at[j], xr.at[g], at.dp(j)).wait_send()


VMEM = pl.BlockSpec(memory_space=pltpu.VMEM)
HBM = pl.BlockSpec(memory_space=pl.ANY)
LIMIT = 60 * 1024 * 1024


def call(*operands):
    return pl.pallas_call(
        kernel,
        out_shape=(
            jax.ShapeDtypeStruct((32, 1024), BF16),
            jax.ShapeDtypeStruct((1024, 768), F32),
            jax.ShapeDtypeStruct((NY, 2, 2, 16, 1024), BF16),
            jax.ShapeDtypeStruct((NY, 2, 2, 16, 768), BF16),
        ),
        in_specs=[VMEM] * 5 + [HBM] * 2,
        out_specs=[VMEM, HBM, HBM, HBM],
        scratch_shapes=[
            pltpu.VMEM((1024, 768), F32),
            pltpu.VMEM((4, NY, 2, 2, 16, 1024), BF16),
            pltpu.VMEM((4, NY, 2, 2, 16, 768), BF16),
            pltpu.VMEM((8, 2, 64, 768), BF16),
            pltpu.VMEM((2048, 1024), BF16),
            pltpu.VMEM((128, 2048), BF16),
            pltpu.VMEM((NZ, 128, 256), BF16),
            pltpu.VMEM((NY, 8, 128, 256), BF16),
            pltpu.VMEM((1024, 1024), BF16),
            pltpu.VMEM((NY, 8, 128), F32),
            pltpu.VMEM((8, 128, 128), F32),
            pltpu.VMEM((8, 128, 128), F32),
            pltpu.VMEM((8, 8, 128), F32),
            pltpu.VMEM((8, 8, 128), F32),
            pltpu.VMEM((1, 1024), F32),
            pltpu.VMEM((NX, 8, 2, 128, 256), F32),
            pltpu.VMEM((NX, 8, 128, 256), F32),
            pltpu.VMEM((8, 3, 272, 128), BF16),
            pltpu.VMEM((8, 272, 128), BF16),
            pltpu.VMEM((8, 2, 272, 128), BF16),
            pltpu.VMEM((8, 128, 256), F32),
            pltpu.VMEM((8, 128), F32),
            pltpu.VMEM((32, 8, 128), F32),
            pltpu.VMEM((32, 8, 128), F32),
            pltpu.VMEM((8, 2, 64, 2048), BF16),
            pltpu.VMEM((4, NY, 2, 2, 16, 1024), F32),
            pltpu.VMEM((4, 3, 2, 2, 16, 1024), BF16),
            pltpu.VMEM((4, 2, 2, 16, 1024), BF16),
            pltpu.VMEM((4, 2, 2, 2, 16, 1024), BF16),
            pltpu.VMEM((4, NZ, 2, 2, 16, 128), F32),
            pltpu.VMEM((4, NZ, 2, 2, 16, 128), BF16),
            pltpu.VMEM((4, NZ, 2, 2, 16, 128), BF16),
            DMA((7,)),
            DMA((148,)),
            DMA((GATHER_SENDS,)),
            DMA((4, NZ)),
            DMA((8,)),
            DMA((8,)),
            DMA((2, 8)),
            DMA((8,)),
            DMA((NY,)),
            DMA((8,)),
            DMA((2, 2)),
            DMA((2,)),
            DMA((4, 2)),
            DMA((NX, 8)),
            DMA((NX, 8)),
            DMA((8, 3)),
            DMA((8,)),
            DMA((8, 2)),
            DMA((32,)),
            DMA((32,)),
            DMA((32,)),
            DMA((32,)),
            DMA((8,)),
            DMA((GATHER_SENDS,)),
            DMA((2, 2)),
            DMA((2,)),
            DMA((4, 2)),
            DMA((4,)),
            DMA((4, 2)),
            DMA((4, NZ)),
            DMA((4, NZ)),
            DMA((4, NZ)),
            DMA((2, 4, 2)),
            DMA((2, 4)),
        ],
        compiler_params=pltpu.CompilerParams(
            collective_id=0, has_side_effects=True, vmem_limit_bytes=LIMIT
        ),
    )(*operands)


def body(hidden, norm_gain, head_weight, target_logits, valid_rows, parents, features):
    share, joined, grad, parent_features = call(
        hidden,
        valid_rows.reshape(1, 128),
        parents.reshape(1, 128),
        features,
        norm_gain.reshape(8, 8, 128),
        head_weight,
        target_logits,
    )
    grad_joining = joined + lax.dot_general(
        *lax.optimization_barrier(
            (grad.reshape(256, 1024), parent_features.reshape(256, 768))
        ),
        (((0,), (0,)), ((), ())),
        preferred_element_type=F32,
    )
    return (share, grad_joining)


def solution(mesh):
    placed = (
        P("dp", "vocab"),
        P(),
        P("vocab", "dp"),
        P("dp", "vocab"),
        P("dp"),
        P("dp"),
        P("dp", "vocab"),
    )
    return jax.shard_map(
        body,
        mesh=mesh,
        in_specs=placed,
        out_specs=(P("vocab", "dp"), P("dp", "vocab")),
        check_vma=False,
    )
```

```python
import contextlib

import jax
import jax.numpy as jnp
from jax import lax
from jax.experimental import pallas as pl
from jax.experimental.pallas import tpu as pltpu
from jax.sharding import PartitionSpec as P

TREE = 64
NX, NC, NY, NZ = 4, 2, 4, 8
F32, BF16 = jnp.float32, jnp.bfloat16
DMA = pltpu.SemaphoreType.DMA


def remote(src, dst, send_sem, recv_sem, device):
    return pltpu.make_async_remote_copy(
        src_ref=src,
        dst_ref=dst,
        send_sem=send_sem,
        recv_sem=recv_sem,
        device_id=device,
        device_id_type=pl.DeviceIdType.MESH,
    )


def phase(name):
    return contextlib.nullcontext()


class Place:
    def __init__(self):
        self.g = lax.axis_index("dp")
        self.v = lax.axis_index("vocab")
        self.x, self.c = self.g // NC, self.g % NC
        self.z, self.y = self.v // NY, self.v % NY

    def dp(self, i):
        return (i, self.v)

    def at_x(self, x):
        return (x * NC + self.c, self.v)

    def partner(self):
        return (self.x * NC + 1 - self.c, self.v)

    def at_y(self, y):
        return (self.g, self.z * NY + y)

    def at_z(self, z):
        return (self.g, z * NY + self.y)


class Sender:
    def __init__(self, sems):
        self.sems, self.used, self.copies = sems, 0, []

    def __call__(self, src, dst, recv_sem, device):
        assert self.used < self.sems.shape[0]
        copy = remote(src, dst, self.sems.at[self.used], recv_sem, device)
        self.used += 1
        copy.start()
        self.copies.append(copy)

    def drain(self):
        for copy in self.copies:
            copy.wait_send()


def arrived(dst, recv_sem, device, any_sem):
    remote(dst, dst, any_sem, recv_sem, device).wait_recv()


class Gather:
    def __init__(self, at, buf, send, near, far, pair):
        self.at, self.buf, self.send = at, buf, send
        self.near, self.far, self.pair = near, far, pair

    def slot(self, step, core):
        return ((self.at.x + step) % NX) * NC + core

    def start(self):
        at, buf = self.at, self.buf
        up, down = at.at_x((at.x + 1) % NX), at.at_x((at.x + 3) % NX)
        for k in range(2):
            for side, half, device in ((0, k, up), (1, 1 - k, down)):
                mine = buf.at[at.g, half]
                self.send(mine, mine, self.near.at[side, half], device)
            mine = buf.at[at.g, k]
            self.send(mine, mine, self.pair.at[0, k], at.partner())

    def middle(self, first):
        at, buf = self.at, self.buf
        for side, step in ((0, 3), (1, 1)):
            half = side if first else 1 - side
            block = buf.at[self.slot(step, at.c), half]
            arrived(block, self.near.at[side, half], at.partner(), self.near.at[side, half])
            if first:
                onward = at.at_x((at.x + (1 if side == 0 else 3)) % NX)
                self.send(block, block, self.far.at[half], onward)
            self.send(block, block, self.pair.at[step, half], at.partner())

    def last(self):
        at, buf = self.at, self.buf
        for half in range(2):
            block = buf.at[self.slot(2, at.c), half]
            arrived(block, self.far.at[half], at.partner(), self.far.at[half])
            self.send(block, block, self.pair.at[2, half], at.partner())

    def paired(self, step, half):
        at = self.at
        block = self.buf.at[self.slot(step, 1 - at.c), half]
        arrived(block, self.pair.at[step, half], at.partner(), self.pair.at[step, half])


GATHER_SENDS = 14


def row_tile(column):
    return jnp.transpose(jnp.broadcast_to(column, (128, 128)))[0:8]


def column_tile(row):
    return jnp.transpose(jnp.broadcast_to(row, (128, 128)))


def stack_rows(*rows):
    index = lax.broadcasted_iota(jnp.int32, (8, 128), 0)
    tile = jnp.zeros((8, 128), F32)
    for k, row in enumerate(rows):
        tile = jnp.where(index == k, row, tile)
    return tile


def kernel(
    hid_hbm, valid_hbm, parents_hbm, feat_hbm_in, gains_hbm, weight_hbm, targets_hbm,
    share_hbm, joined_hbm, grad_hbm, feat_hbm,
    hid, valid, parents, feat, gains, share_out,
    joined, grad_out, feat_out, fall,
    weight, targets, zbuf, xall, normed, stat, cols, scols, rf, srow, gain,
    pk, pr, sb, rl, fin, lg, tst, stat_v, dot_v, gbuf, pf, ysb, yrl, yfin,
    qf, qs, zrs,
    local_sems, send_sems, f_sems, zr, xs, xr, yr, y2, sr, fr,
    f_near, f_far, f_pair,
    pair_s, pair_r, sb_s, rl_r, fin_r,
    sv_s, sv_r, dv_s, dv_r, sd_r, g_sems, g_near, g_far, g_pair,
    yrl_r, yfin_r, zs_s, zs_r, a_z, a_y, a_y2,
):
    at = Place()
    x, c, y, z, g, v = at.x, at.c, at.y, at.z, at.g, at.v
    up_z, down_z = at.at_z((z + 1) % NZ), at.at_z((z + NZ - 1) % NZ)
    up_y, down_y = at.at_y((y + 1) % NY), at.at_y((y + 3) % NY)

    loads = [
        pltpu.make_async_copy(src, dst, local_sems.at[5 + k])
        for k, (src, dst) in enumerate(
            (
                (hid_hbm, hid),
                (parents_hbm, parents),
                (feat_hbm_in, feat),
                (valid_hbm, valid),
                (gains_hbm, gains),
            )
        )
    ]
    for load in loads:
        load.start()
    load_weight = pltpu.make_async_copy(weight_hbm, weight, local_sems.at[0])
    load_targets = pltpu.make_async_copy(targets_hbm, targets, local_sems.at[1])
    load_weight.start()
    load_targets.start()

    with phase("A_feat"):
        barrier = pltpu.get_barrier_semaphore()

        @pl.loop(1, 32)
        def _(k):
            pl.semaphore_signal(
                barrier,
                inc=1,
                device_id=(g, (v + k) % 32),
                device_id_type=pl.DeviceIdType.MESH,
            )

        @pl.loop(1, 8)
        def _(k):
            pl.semaphore_signal(
                barrier,
                inc=1,
                device_id=((g + k) % 8, v),
                device_id_type=pl.DeviceIdType.MESH,
            )

    with phase("A_load"):
        for load in loads:
            load.wait()
    with phase("A_own"):
        live = (valid[...] == 1).astype(F32)
        row = lax.broadcasted_iota(jnp.int32, (128, 128), 0)
        lane = lax.broadcasted_iota(jnp.int32, (128, 128), 1)
        wanted = column_tile(parents[...].astype(F32)).astype(jnp.int32) + row // TREE * TREE
        pick = (lane == wanted).astype(BF16)
        chosen = jnp.dot(pick, feat[...], preferred_element_type=F32).astype(BF16)
        fall[g, 0] = chosen[:64]
        fall[g, 1] = chosen[64:]
        own_gain = gains[g]
        gain[...] = jnp.concatenate([own_gain[k : k + 1] for k in range(8)], axis=1)

    with phase("A_greet"):
        pl.semaphore_wait(barrier, 38)
    send = Sender(send_sems)
    spread = Gather(at, fall, Sender(f_sems), f_near, f_far, f_pair)

    def to_slice(src, j):
        @pl.when(j != g)
        def _():
            remote(src, xall.at[y, g], xs.at[j], xr.at[g], at.dp(j)).start()

        @pl.when(j == g)
        def _():
            pltpu.make_async_copy(src, xall.at[y, g], xs.at[j]).start()

    def piece(ref, q):
        return ref.at[32 * q : 32 * q + 32]

    with phase("A_z"):
        for q in range(4):
            send(piece(hid, q), piece(zbuf.at[z], q), zr.at[q, z], up_z)
            send(piece(hid, q), piece(zbuf.at[z], q), zr.at[q, z], down_z)
        to_slice(hid, z)
        spread.start()
        for step in range(1, 5):
            low, high = (z + NZ - step) % NZ, (z + step) % NZ
            for q in range(4):
                block = piece(zbuf.at[low], q)
                arrived(block, zr.at[q, low], up_z, zr.at[q, low])
                if step < 4:
                    send(block, block, zr.at[q, low], up_z)
                    block = piece(zbuf.at[high], q)
                    arrived(block, zr.at[q, high], up_z, zr.at[q, high])
                    if step < 3:
                        send(block, block, zr.at[q, high], down_z)
            to_slice(zbuf.at[low], low)
            if step < 4:
                to_slice(zbuf.at[high], high)

    with phase("A_stat"):
        squares = jnp.square(hid[...].astype(F32))
        for k in range(1, NZ):
            squares = squares + jnp.square(zbuf[(z + k) % NZ].astype(F32))
        stat[y] = row_tile(jnp.sum(squares, axis=1, keepdims=True))
        for k in range(1, NY):
            send(stat.at[y], stat.at[y], sr.at[y], at.at_y((y + k) % NY))

    turns = (2, 1, 3, 0)

    def group(k):
        return 2 * ((x + turns[k // 2]) % NX) + k % 2

    def y_send(k):
        block = xall.at[y, group(k)]
        sem = xr.at[group(k)]
        if k < 6:
            arrived(block, sem, up_y, sem)
        else:

            @pl.when(c != k % 2)
            def _():
                arrived(block, sem, up_y, sem)

            @pl.when(c == k % 2)
            def _():
                pltpu.make_async_copy(hid, block, xs.at[g]).wait()

        send(block, block, yr.at[0, k], up_y)
        send(block, block, yr.at[1, k], down_y)

    def y_relay(k):
        for side, step in ((0, 3), (1, 1)):
            block = xall.at[(y + step) % NY, group(k)]
            arrived(block, yr.at[side, k], up_y, yr.at[side, k])
            if k % 2 == side:
                send(block, block, y2.at[k], up_y if side == 0 else down_y)
        if k + 3 < 8:
            y_send(k + 3)

    def y_far(k):
        block = xall.at[(y + 2) % NY, group(k)]
        arrived(block, y2.at[k], up_y, y2.at[k])

    def normalise(k):
        i = group(k)
        scale = cols[i]
        scale = jnp.concatenate([scale, scale], axis=1)
        rows = pl.ds(pl.multiple_of(i * 128, 128), 128)
        for part in range(NY):
            columns = slice(part * 256, part * 256 + 256)
            values = xall[part, i].astype(F32)
            normed[rows, columns] = (values * scale * gain[:, columns]).astype(BF16)

    def pair_copy(step, t):
        return remote(
            pk.at[step, t, 1 - c], pr.at[step, t],
            pair_s.at[step, t], pair_r.at[step, t], at.partner(),
        )

    def multiply(step, t):
        rows = pl.ds(pl.multiple_of(((x + step) % NX) * 256, 256), 256)
        tile = pl.ds(pl.multiple_of(t * 256, 256), 256)
        part = lax.dot_general(
            normed[rows, :],
            weight[tile, :],
            (((1,), (1,)), ((), ())),
            preferred_element_type=F32,
        )
        pk[step, t, 0] = part[:128]
        pk[step, t, 1] = part[128:]
        pair_copy(step, t).start()

    def total_of(step, t):
        arrived(pr.at[step, t], pair_r.at[step, t], at.partner(), pair_r.at[step, t])
        return pk[step, t, c] + pr[step, t]

    def ways(t):
        way = 1 + 2 * (t % 2)
        return way, 4 - way

    def first_hop(t):
        ahead, _ = ways(t)
        return remote(sb.at[t, 0], rl.at[t], sb_s.at[t, 0], rl_r.at[t], at.at_x((x + ahead) % NX))

    def direct(t):
        _, back = ways(t)
        return remote(
            sb.at[t, 1], fin.at[t, 0], sb_s.at[t, 1], fin_r.at[t, 0], at.at_x((x + back) % NX)
        )

    def onward(t):
        ahead, _ = ways(t)
        return remote(
            sb.at[t, 2], fin.at[t, 1], sb_s.at[t, 2], fin_r.at[t, 1], at.at_x((x + ahead) % NX)
        )

    def encode(t, k, value):
        left, right = value[:, :128], value[:, 128:]
        top = jnp.max(jnp.maximum(jnp.abs(left), jnp.abs(right)), axis=0, keepdims=True)
        step = (120.0 / jnp.maximum(top, 1e-30)).astype(BF16)
        sb[t, k, 256:] = jnp.broadcast_to(step, (16, 128))
        step = sb[t, k, 256:].astype(F32)[0:1]
        sb[t, k, :128] = jnp.exp2(left * step).astype(BF16)
        sb[t, k, 128:256] = jnp.exp2(right * step).astype(BF16)

    def decode(block):
        size = 1.0 / block[256:].astype(F32)[0:1]
        return jnp.concatenate(
            [
                jnp.log2(block[:128].astype(F32)) * size,
                jnp.log2(block[128:256].astype(F32)) * size,
            ],
            axis=1,
        )

    with phase("A_ysend"):
        for k in range(3):
            y_send(k)

    with phase("A_rf"):
        total = stat[y]
        for k in range(1, NY):
            other = (y + k) % NY
            arrived(stat.at[other], sr.at[other], up_y, sr.at[other])
            total = total + stat[other]
        factor = lax.rsqrt(total / (1024.0 * 8) + 1e-05)
        rf[g] = stack_rows(factor[0:1], live)
        for k in range(1, 8):
            send(rf.at[g], rf.at[g], fr.at[g], at.dp((g + k) % 8))

    with phase("A_y0123"):
        y_relay(0)
        y_relay(1)
        spread.middle(True)
        y_relay(2)
        for k in range(1, 8):
            other = (g + k) % 8
            arrived(rf.at[other], fr.at[other], up_y, fr.at[other])
        for i in range(8):
            cols[i] = column_tile(rf[i, 0:1])
        y_relay(3)
        load_weight.wait()
        load_targets.wait()
    with phase("A_far01"):
        y_far(0)
        y_far(1)
        normalise(0)
        normalise(1)
    def run(low, high, *stages):
        @pl.loop(low, high)
        def _(t):
            for stage, lag in stages:
                stage(t - lag)

    def hop(t):
        encode(t, 0, total_of(2, t))
        first_hop(t).start()

    with phase("F_hop"):
        far_rows = (lambda t: multiply(2, t)), 0
        run(0, 3, far_rows)
        run(3, 6, far_rows, (hop, 3))
        y_relay(4)
        run(6, 8, far_rows, (hop, 3))
        y_relay(5)
        run(5, 8, (hop, 0))
    with phase("A_y6"):
        y_relay(6)
    with phase("A_far2345"):
        for k in range(2, 6):
            y_far(k)
            normalise(k)
    with phase("F_both"):

        def both(t):
            ahead, back = ways(t)
            encode(t, 1, total_of(back, t))
            direct(t).start()
            arrived(rl.at[t], rl_r.at[t], at.partner(), rl_r.at[t])
            encode(t, 2, total_of(ahead, t) + decode(rl.at[t]))
            onward(t).start()

        def near_rows(t):
            multiply(1, t)
            multiply(3, t)

        run(0, 3, (near_rows, 0))
        run(3, 5, (near_rows, 0), (both, 3))
        y_relay(7)
        run(5, 8, (near_rows, 0), (both, 3))
        run(5, 8, (both, 0))

    with phase("A_far67"):
        spread.middle(False)
        top = jnp.max(targets[...].astype(F32), axis=1, keepdims=True)
        part = jnp.zeros((128, 256), F32)
        for k in range(8):
            part = part + jnp.exp(targets[:, k * 256 : k * 256 + 256].astype(F32) - top)
        tst[...] = stack_rows(
            jnp.zeros((1, 128), F32),
            jnp.zeros((1, 128), F32),
            row_tile(top)[0:1],
            row_tile(jnp.sum(part, axis=1, keepdims=True))[0:1],
        )
        for k in range(6, 8):
            y_far(k)
            normalise(k)

    def finish(t):
        own = total_of(0, t)
        for k in range(2):
            arrived(fin.at[t, k], fin_r.at[t, k], at.partner(), fin_r.at[t, k])
        lg[t] = own + decode(fin.at[t, 0]) + decode(fin.at[t, 1])

    with phase("F_fin"):
        own_rows = (lambda t: multiply(0, t)), 0
        run(0, 3, own_rows)
        run(3, 8, own_rows, (finish, 3))
        run(5, 8, (finish, 0))

    def tell_all(tile, send_sem, recv_sem):
        @pl.loop(1, 32)
        def _(k):
            remote(
                tile.at[v], tile.at[v], send_sem.at[k], recv_sem.at[v], (g, (v + k) % 32)
            ).start()

    def hear_all(tile, recv_sem):
        @pl.loop(1, 32)
        def _(k):
            other = (v + k) % 32
            arrived(tile.at[other], recv_sem.at[other], up_y, recv_sem.at[other])

    with phase("B_stat"):
        top = lg[0]
        for t in range(1, 8):
            top = jnp.maximum(top, lg[t])
        top = jnp.max(top, axis=1, keepdims=True)
        part = jnp.zeros((128, 256), F32)
        for t in range(8):
            part = part + jnp.exp(lg[t] - top)
        stat_v[v] = stack_rows(
            row_tile(top)[0:1],
            row_tile(jnp.sum(part, axis=1, keepdims=True))[0:1],
            tst[2:3],
            tst[3:4],
        )
        tell_all(stat_v, sv_s, sv_r)

    with phase("B_statv"):
        hear_all(stat_v, sv_r)
        wide = lambda row: jnp.concatenate([column_tile(row)] * 2, axis=1)
        tops, scales = [], []
        for k in (0, 2):
            top = jnp.max(stat_v[:, k, :], axis=0, keepdims=True)
            part = stat_v[:, k + 1, :] * jnp.exp(stat_v[:, k, :] - top)
            tops.append(wide(top))
            scales.append(wide(1.0 / jnp.sum(part, axis=0, keepdims=True)))
        count = jnp.zeros((1, 128), F32)
        for i in range(8):
            count = count + rf[i, 1:2]
        count = jnp.sum(count, axis=1, keepdims=True)
        scale = wide(1048576.0 * live / count)

    gather = Gather(at, gbuf, Sender(g_sems), g_near, g_far, g_pair)
    with phase("B_G"):
        acc = jnp.zeros((128, 256), F32)
        for t in range(8):
            draft = jnp.exp(lg[t] - tops[0]) * scales[0]
            target = (
                jnp.exp(targets[:, t * 256 : t * 256 + 256].astype(F32) - tops[1]) * scales[1]
            )
            value = (scale * (draft - target)).astype(BF16)
            for k in range(8):
                gbuf[g, k % 2, k // 2 * 16 : k // 2 * 16 + 16, t * 256 : t * 256 + 256] = value[
                    k * 16 : k * 16 + 16
                ]
            acc = acc + value.astype(F32) * lg[t]
        gather.start()
        dot_v[v] = row_tile(jnp.sum(acc, axis=1, keepdims=True))
        tell_all(dot_v, dv_s, dv_r)

    units = (((0, 0), (0, 1)), ((3, 0), (1, 1)), ((3, 1), (1, 0)), ((2, 0), (2, 1)))

    def block_of(step):
        return (x + step) % NX

    def backward(k):
        for step, half in units[k]:
            gather.paired(step, half)

        @pl.loop(0, 4)
        def _(n):
            columns = pl.ds(pl.multiple_of(n * 256, 256), 256)
            rows = jnp.concatenate(
                [
                    gbuf[pl.ds(2 * block_of(step), 2), half].reshape(128, 2048)
                    for step, half in units[k]
                ],
                axis=0,
            )
            part = jnp.dot(rows, weight[:, columns], preferred_element_type=F32)
            for p in range(2):
                for which in range(2):
                    for dest in range(NY):
                        row = p * 128 + which * 64 + dest * 16
                        pf[k, dest, p, which, :, columns] = part[row : row + 16]

        way = 1 if k % 2 == 0 else 3
        ysb[k, 0] = pf[k, (y + 2) % NY].astype(BF16)
        send(ysb.at[k, 0], yrl.at[k], yrl_r.at[k], at.at_y((y + way) % NY))
        ysb[k, 1] = pf[k, (y + 4 - way) % NY].astype(BF16)
        send(ysb.at[k, 1], yfin.at[k, 0], yfin_r.at[k, 0], at.at_y((y + 4 - way) % NY))

    def y_second(k):
        way = 1 if k % 2 == 0 else 3
        arrived(yrl.at[k], yrl_r.at[k], up_y, yrl_r.at[k])
        ysb[k, 2] = (pf[k, (y + way) % NY] + yrl[k].astype(F32)).astype(BF16)
        send(ysb.at[k, 2], yfin.at[k, 1], yfin_r.at[k, 1], at.at_y((y + way) % NY))

    def z_send(k, dest):
        return remote(
            qs.at[k, dest], zrs.at[k, z], zs_s.at[k, dest], zs_r.at[k, z], at.at_z(dest)
        )

    far_first = (4, 3, 5, 2, 6, 1, 7)

    def y_third(k):
        for j in range(2):
            arrived(yfin.at[k, j], yfin_r.at[k, j], up_y, yfin_r.at[k, j])
        value = pf[k, y] + yfin[k, 0].astype(F32) + yfin[k, 1].astype(F32)
        for owner in range(NZ):
            part = value[:, :, :, 128 * owner : 128 * owner + 128]
            qf[k, owner] = part
            qs[k, owner] = part.astype(BF16)
        for shift in far_first:
            z_send(k, (z + shift) % NZ).start()

    own_columns = pl.ds(pl.multiple_of(z * 128, 128), 128)

    def piece_of(k, owner):
        columns = pl.ds(pl.multiple_of(owner * 128, 128), 128)
        return grad_out.at[k, y, :, :, :, columns]

    def z_fourth(k):
        total = qf[k, z]
        for j in range(1, NZ):
            other = (z + j) % NZ
            arrived(zrs.at[k, other], zs_r.at[k, other], up_y, zs_r.at[k, other])
            total = total + zrs[k, other].astype(F32)
        lanes = pl.ds(pl.multiple_of((z % 2) * 128, 128), 128)
        for p, (step, half) in enumerate(units[k]):
            rows = pl.ds(pl.multiple_of(y * 32 + half * 16, 16), 16)
            for which in range(2):
                i = 2 * block_of(step) + which
                values = xall[z // 2, i, rows, lanes].astype(F32)
                grad = cols[i, rows, :] * gain[:, own_columns] * total[p, which]
                grad = grad - values * scols[i, rows, :]
                grad_out[k, y, p, which, :, own_columns] = grad.astype(BF16)
        mine = piece_of(k, z)
        for shift in far_first:
            send(mine, mine, a_z.at[k, z], at.at_z((z + shift) % NZ))

    def across(k):
        for j in (1, 7, 2, 6, 3, 5, 4):
            other = (z + j) % NZ
            arrived(piece_of(k, other), a_z.at[k, other], up_y, a_z.at[k, other])
        for turn in range(2):
            for side, device in ((0, up_y), (1, down_y)):
                p = side if turn == 0 else 1 - side
                mine = grad_out.at[k, y, p]
                send(mine, mine, a_y.at[side, k, p], device)

    def across_near(k, side, p):
        half = grad_out.at[k, (y + (3 if side == 0 else 1)) % NY, p]
        arrived(half, a_y.at[side, k, p], up_y, a_y.at[side, k, p])
        return half

    def across_relay(k):
        for side in range(2):
            half = across_near(k, side, side)
            send(half, half, a_y2.at[side, k], up_y if side == 0 else down_y)

    grad_to_hbm = pltpu.make_async_copy(grad_out.at[3], grad_hbm, local_sems.at[2])
    feat_to_hbm = pltpu.make_async_copy(feat_out.at[3], feat_hbm, local_sems.at[3])
    share_to_hbm = pltpu.make_async_copy(share_out, share_hbm, local_sems.at[10])
    acc_to_hbm = pltpu.make_async_copy(joined, joined_hbm, local_sems.at[4])

    def fold(k):
        @pl.loop(0, 4)
        def _(n):
            columns = pl.ds(pl.multiple_of(n * 256, 256), 256)
            part = lax.dot_general(
                grad_out[k, :, :, :, :, columns].reshape(256, 256),
                feat_out[k].reshape(256, 768),
                (((0,), (0,)), ((), ())),
                preferred_element_type=F32,
            )
            if k == 0:
                joined[columns, :] = part
            else:
                joined[columns, :] += part

    def across_far(k):
        for side in range(2):
            across_near(k, side, 1 - side)
        for side in range(2):
            half = grad_out.at[k, (y + 2) % NY, side]
            arrived(half, a_y2.at[side, k], up_y, a_y2.at[side, k])

    with phase("G_bw0"):
        backward(0)
    with phase("G_feat"):
        spread.last()
        for step in (0, 1, 3):
            for half in range(2):
                spread.paired(step, half)
    with phase("G_mid"):
        gather.middle(True)
    with phase("G_ys0"):
        y_second(0)
    with phase("G_dot"):
        hear_all(dot_v, dv_r)
        dot = jnp.sum(dot_v[:, 0, :], axis=0, keepdims=True)
        factor = rf[g][0:1]
        srow[g] = jnp.broadcast_to(factor * factor * dot / (1024.0 * 8), (8, 128))
        for k in range(1, 8):
            send(srow.at[g], srow.at[g], sd_r.at[g], at.dp((g + k) % 8))
    with phase("G_bw1"):
        backward(1)
    with phase("G_yt0"):
        y_third(0)
    with phase("G_mid2"):
        gather.middle(False)
    with phase("G_ys1"):
        y_second(1)
    with phase("G_bw2"):
        backward(2)
    with phase("G_s"):
        for k in range(1, 8):
            other = (g + k) % 8
            arrived(srow.at[other], sd_r.at[other], up_y, sd_r.at[other])
        for i in range(8):
            scols[i] = column_tile(srow[i, 0:1])
    with phase("G_z0"):
        z_fourth(0)
    with phase("G_last"):
        gather.last()
    with phase("G_yt1"):
        y_third(1)
    with phase("G_bw3"):
        backward(3)
    with phase("G_ys2"):
        y_second(2)
    with phase("H_ax0"):
        across(0)
    with phase("H_feat"):
        spread.paired(2, 0)
        spread.paired(2, 1)
        for k in range(4):
            for p, (step, half) in enumerate(units[k]):
                for which in range(2):
                    for dest in range(NY):
                        row = dest % 2 * 32 + half * 16
                        feat_out[k, dest, p, which] = fall[
                            2 * block_of(step) + which, dest // 2, row : row + 16, :
                        ]
        feat_to_hbm.start()
    with phase("H_z1"):
        z_fourth(1)
    with phase("G_ys3"):
        y_second(3)
    with phase("G_yt2"):
        y_third(2)
    with phase("H_ax1"):
        across(1)
    with phase("G_yt3"):
        y_third(3)
    with phase("H_ar0"):
        across_relay(0)
    with phase("H_z2"):
        z_fourth(2)
    with phase("H_far0"):
        across_far(0)
    with phase("H_ar1"):
        across_relay(1)
    with phase("H_z3"):
        z_fourth(3)
    with phase("H_ax2"):
        across(2)
    with phase("H_fold0"):
        fold(0)
    with phase("H_far1"):
        across_far(1)
    with phase("H_ar2"):
        across_relay(2)
    with phase("H_ax3"):
        across(3)
    with phase("H_fold1"):
        fold(1)
    with phase("H_far2"):
        across_far(2)
    with phase("H_ar3"):
        across_relay(3)
    with phase("H_fold2"):
        fold(2)
        acc_to_hbm.start()
    with phase("H_far"):
        across_far(3)
        grad_to_hbm.start()
        away = (z // 2 + NX - x) % NX
        odd, side = away % 2, away // 2
        for half in range(2):
            k = odd * (1 + (half + side + 1) % 2) + (1 - odd) * 3 * side
            p = odd * (1 - side) + (1 - odd) * half
            share_out[16 * half : 16 * half + 16, :] = grad_out[k, y, p, z % 2]
        share_to_hbm.start()
        share_to_hbm.wait()
        grad_to_hbm.wait()
        feat_to_hbm.wait()
        acc_to_hbm.wait()

    with phase("H_drain"):

        @pl.loop(0, 8)
        def _(t):
            for step in range(4):
                pair_copy(step, t).wait_send()
            first_hop(t).wait_send()
            direct(t).wait_send()
            onward(t).wait_send()

        @pl.loop(1, 32)
        def _(k):
            other = (g, (v + k) % 32)
            remote(stat_v.at[v], stat_v.at[v], sv_s.at[k], sv_r.at[v], other).wait_send()
            remote(dot_v.at[v], dot_v.at[v], dv_s.at[k], dv_r.at[v], other).wait_send()

        send.drain()
        spread.send.drain()
        gather.send.drain()
        for k in range(4):
            for j in range(1, NZ):
                z_send(k, (z + j) % NZ).wait_send()
        for j in range(8):

            @pl.when(g != j)
            def _():
                remote(hid, xall.at[y, g], xs.at[j], xr.at[g], at.dp(j)).wait_send()


VMEM = pl.BlockSpec(memory_space=pltpu.VMEM)
HBM = pl.BlockSpec(memory_space=pl.ANY)
LIMIT = 60 * 1024 * 1024


def call(*operands):
    return pl.pallas_call(
        kernel,
        out_shape=(
            jax.ShapeDtypeStruct((32, 1024), BF16),
            jax.ShapeDtypeStruct((1024, 768), F32),
            jax.ShapeDtypeStruct((NY, 2, 2, 16, 1024), BF16),
            jax.ShapeDtypeStruct((NY, 2, 2, 16, 768), BF16),
        ),
        in_specs=[HBM] * 7,
        out_specs=[HBM] * 4,
        scratch_shapes=[
            pltpu.VMEM((128, 256), BF16),
            pltpu.VMEM((1, 128), jnp.int32),
            pltpu.VMEM((1, 128), jnp.int32),
            pltpu.VMEM((128, 768), BF16),
            pltpu.VMEM((8, 8, 128), F32),
            pltpu.VMEM((32, 1024), BF16),
            pltpu.VMEM((1024, 768), F32),
            pltpu.VMEM((4, NY, 2, 2, 16, 1024), BF16),
            pltpu.VMEM((4, NY, 2, 2, 16, 768), BF16),
            pltpu.VMEM((8, 2, 64, 768), BF16),
            pltpu.VMEM((2048, 1024), BF16),
            pltpu.VMEM((128, 2048), BF16),
            pltpu.VMEM((NZ, 128, 256), BF16),
            pltpu.VMEM((NY, 8, 128, 256), BF16),
            pltpu.VMEM((1024, 1024), BF16),
            pltpu.VMEM((NY, 8, 128), F32),
            pltpu.VMEM((8, 128, 128), F32),
            pltpu.VMEM((8, 128, 128), F32),
            pltpu.VMEM((8, 8, 128), F32),
            pltpu.VMEM((8, 8, 128), F32),
            pltpu.VMEM((1, 1024), F32),
            pltpu.VMEM((NX, 8, 2, 128, 256), F32),
            pltpu.VMEM((NX, 8, 128, 256), F32),
            pltpu.VMEM((8, 3, 272, 128), BF16),
            pltpu.VMEM((8, 272, 128), BF16),
            pltpu.VMEM((8, 2, 272, 128), BF16),
            pltpu.VMEM((8, 128, 256), F32),
            pltpu.VMEM((8, 128), F32),
            pltpu.VMEM((32, 8, 128), F32),
            pltpu.VMEM((32, 8, 128), F32),
            pltpu.VMEM((8, 2, 64, 2048), BF16),
            pltpu.VMEM((4, NY, 2, 2, 16, 1024), F32),
            pltpu.VMEM((4, 3, 2, 2, 16, 1024), BF16),
            pltpu.VMEM((4, 2, 2, 16, 1024), BF16),
            pltpu.VMEM((4, 2, 2, 2, 16, 1024), BF16),
            pltpu.VMEM((4, NZ, 2, 2, 16, 128), F32),
            pltpu.VMEM((4, NZ, 2, 2, 16, 128), BF16),
            pltpu.VMEM((4, NZ, 2, 2, 16, 128), BF16),
            DMA((11,)),
            DMA((148,)),
            DMA((GATHER_SENDS,)),
            DMA((4, NZ)),
            DMA((8,)),
            DMA((8,)),
            DMA((2, 8)),
            DMA((8,)),
            DMA((NY,)),
            DMA((8,)),
            DMA((2, 2)),
            DMA((2,)),
            DMA((4, 2)),
            DMA((NX, 8)),
            DMA((NX, 8)),
            DMA((8, 3)),
            DMA((8,)),
            DMA((8, 2)),
            DMA((32,)),
            DMA((32,)),
            DMA((32,)),
            DMA((32,)),
            DMA((8,)),
            DMA((GATHER_SENDS,)),
            DMA((2, 2)),
            DMA((2,)),
            DMA((4, 2)),
            DMA((4,)),
            DMA((4, 2)),
            DMA((4, NZ)),
            DMA((4, NZ)),
            DMA((4, NZ)),
            DMA((2, 4, 2)),
            DMA((2, 4)),
        ],
        compiler_params=pltpu.CompilerParams(
            collective_id=0, has_side_effects=True, vmem_limit_bytes=LIMIT
        ),
    )(*operands)


def body(hidden, norm_gain, head_weight, target_logits, valid_rows, parents, features):
    share, joined, grad, parent_features = call(
        hidden,
        valid_rows.reshape(1, 128),
        parents.reshape(1, 128),
        features,
        norm_gain.reshape(8, 8, 128),
        head_weight,
        target_logits,
    )
    grad_joining = joined + lax.dot_general(
        *lax.optimization_barrier(
            (grad.reshape(256, 1024), parent_features.reshape(256, 768))
        ),
        (((0,), (0,)), ((), ())),
        preferred_element_type=F32,
    )
    return (share, grad_joining)


def solution(mesh):
    placed = (
        P("dp", "vocab"),
        P(),
        P("vocab", "dp"),
        P("dp", "vocab"),
        P("dp"),
        P("dp"),
        P("dp", "vocab"),
    )
    return jax.shard_map(
        body,
        mesh=mesh,
        in_specs=placed,
        out_specs=(P("vocab", "dp"), P("dp", "vocab")),
        check_vma=False,
    )
```

```python
import contextlib

import jax
import jax.numpy as jnp
from jax import lax
from jax.experimental import pallas as pl
from jax.experimental.pallas import tpu as pltpu
from jax.sharding import PartitionSpec as P

TREE = 64
NX, NC, NY, NZ = 4, 2, 4, 8
F32, BF16 = jnp.float32, jnp.bfloat16
DMA = pltpu.SemaphoreType.DMA


def remote(src, dst, send_sem, recv_sem, device):
    return pltpu.make_async_remote_copy(
        src_ref=src,
        dst_ref=dst,
        send_sem=send_sem,
        recv_sem=recv_sem,
        device_id=device,
        device_id_type=pl.DeviceIdType.MESH,
    )


def phase(name):
    return contextlib.nullcontext()


class Place:
    def __init__(self):
        self.g = lax.axis_index("dp")
        self.v = lax.axis_index("vocab")
        self.x, self.c = self.g // NC, self.g % NC
        self.z, self.y = self.v // NY, self.v % NY

    def dp(self, i):
        return (i, self.v)

    def at_x(self, x):
        return (x * NC + self.c, self.v)

    def partner(self):
        return (self.x * NC + 1 - self.c, self.v)

    def at_y(self, y):
        return (self.g, self.z * NY + y)

    def at_z(self, z):
        return (self.g, z * NY + self.y)


class Sender:
    def __init__(self, sems):
        self.sems, self.used, self.copies = sems, 0, []

    def __call__(self, src, dst, recv_sem, device):
        assert self.used < self.sems.shape[0]
        copy = remote(src, dst, self.sems.at[self.used], recv_sem, device)
        self.used += 1
        copy.start()
        self.copies.append(copy)

    def drain(self):
        for copy in self.copies:
            copy.wait_send()
        self.used, self.copies = 0, []


class Group:
    def __init__(self, sem):
        self.sem = sem

    def __call__(self, src, dst, recv_sem, device):
        remote(src, dst, self.sem, recv_sem, device).start()

    def drain(self, like, device):
        remote(like, like, self.sem, self.sem, device).wait_send()


def arrived(dst, recv_sem, device, any_sem):
    remote(dst, dst, any_sem, recv_sem, device).wait_recv()


class Gather:
    def __init__(self, at, buf, send, near, far, pair):
        self.at, self.buf, self.send = at, buf, send
        self.near, self.far, self.pair = near, far, pair

    def slot(self, step, core):
        return ((self.at.x + step) % NX) * NC + core

    def start(self):
        at, buf = self.at, self.buf
        up, down = at.at_x((at.x + 1) % NX), at.at_x((at.x + 3) % NX)
        for k in range(2):
            for side, half, device in ((0, k, up), (1, 1 - k, down)):
                mine = buf.at[at.g, half]
                self.send(mine, mine, self.near.at[side, half], device)
            mine = buf.at[at.g, k]
            self.send(mine, mine, self.pair.at[0, k], at.partner())

    def middle(self, first):
        at, buf = self.at, self.buf
        for side, step in ((0, 3), (1, 1)):
            half = side if first else 1 - side
            block = buf.at[self.slot(step, at.c), half]
            arrived(block, self.near.at[side, half], at.partner(), self.near.at[side, half])
            if first:
                onward = at.at_x((at.x + (1 if side == 0 else 3)) % NX)
                self.send(block, block, self.far.at[half], onward)
            self.send(block, block, self.pair.at[step, half], at.partner())

    def last(self):
        at, buf = self.at, self.buf
        for half in range(2):
            block = buf.at[self.slot(2, at.c), half]
            arrived(block, self.far.at[half], at.partner(), self.far.at[half])
            self.send(block, block, self.pair.at[2, half], at.partner())

    def paired(self, step, half):
        at = self.at
        block = self.buf.at[self.slot(step, 1 - at.c), half]
        arrived(block, self.pair.at[step, half], at.partner(), self.pair.at[step, half])


def row_tile(column):
    return jnp.transpose(jnp.broadcast_to(column, (128, 128)))[0:8]


def column_tile(row):
    return jnp.transpose(jnp.broadcast_to(row, (128, 128)))


def stack_rows(*rows):
    index = lax.broadcasted_iota(jnp.int32, (8, 128), 0)
    tile = jnp.zeros((8, 128), F32)
    for k, row in enumerate(rows):
        tile = jnp.where(index == k, row, tile)
    return tile


def kernel(
    hid_hbm, valid_hbm, parents_hbm, feat_hbm_in, gains_hbm, weight_hbm, targets_hbm,
    share_hbm, joined_hbm, grad_hbm, feat_hbm,
    hid, valid, parents, feat, gains, share_out,
    joined, grad_out, feat_out, fall,
    weight, targets, zbuf, xall, normed, stat, cols, scols, rf, srow, gain,
    pk, pr, sb, rl, fin, lg, tst, stat_v, dot_v, gbuf, pf, ysb, yrl, yfin,
    qf, qs, zrs,
    local_sems, send_sems, group_sems, zr, xs, xr, yr, y2, sr, fr,
    f_near, f_far, f_pair,
    pair_s, pair_r, sb_s, rl_r, fin_r,
    sv_r, dv_r, sd_r, g_near, g_far, g_pair,
    yrl_r, yfin_r, zs_s, zs_r, az_s, a_z, a_y, a_y2,
):
    at = Place()
    x, c, y, z, g, v = at.x, at.c, at.y, at.z, at.g, at.v
    up_z, down_z = at.at_z((z + 1) % NZ), at.at_z((z + NZ - 1) % NZ)
    up_y, down_y = at.at_y((y + 1) % NY), at.at_y((y + 3) % NY)

    loads = [
        pltpu.make_async_copy(src, dst, local_sems.at[5 + k])
        for k, (src, dst) in enumerate(
            (
                (hid_hbm, hid),
                (parents_hbm, parents),
                (feat_hbm_in, feat),
                (valid_hbm, valid),
                (gains_hbm, gains),
            )
        )
    ]
    for load in loads:
        load.start()
    load_weight = pltpu.make_async_copy(weight_hbm, weight, local_sems.at[0])
    load_targets = pltpu.make_async_copy(targets_hbm, targets, local_sems.at[1])
    load_weight.start()
    load_targets.start()

    with phase("A_feat"):
        barrier = pltpu.get_barrier_semaphore()

        @pl.loop(1, 32)
        def _(k):
            pl.semaphore_signal(
                barrier,
                inc=1,
                device_id=(g, (v + k) % 32),
                device_id_type=pl.DeviceIdType.MESH,
            )

        @pl.loop(1, 8)
        def _(k):
            pl.semaphore_signal(
                barrier,
                inc=1,
                device_id=((g + k) % 8, v),
                device_id_type=pl.DeviceIdType.MESH,
            )

    with phase("A_load"):
        for load in loads:
            load.wait()
    with phase("A_own"):
        live = (valid[...] == 1).astype(F32)
        row = lax.broadcasted_iota(jnp.int32, (128, 128), 0)
        lane = lax.broadcasted_iota(jnp.int32, (128, 128), 1)
        wanted = column_tile(parents[...].astype(F32)).astype(jnp.int32) + row // TREE * TREE
        pick = (lane == wanted).astype(BF16)
        chosen = jnp.dot(pick, feat[...], preferred_element_type=F32).astype(BF16)
        fall[g, 0] = chosen[:64]
        fall[g, 1] = chosen[64:]
        own_gain = gains[g]
        gain[...] = jnp.concatenate([own_gain[k : k + 1] for k in range(8)], axis=1)

    with phase("A_greet"):
        pl.semaphore_wait(barrier, 38)
    send = Sender(send_sems)
    spread = Gather(at, fall, Group(group_sems.at[0]), f_near, f_far, f_pair)

    def to_slice(src, j):
        @pl.when(j != g)
        def _():
            remote(src, xall.at[y, g], xs.at[j], xr.at[g], at.dp(j)).start()

        @pl.when(j == g)
        def _():
            pltpu.make_async_copy(src, xall.at[y, g], xs.at[j]).start()

    def piece(ref, q):
        return ref.at[64 * q : 64 * q + 64]

    with phase("A_z"):
        for q in range(2):
            send(piece(hid, q), piece(zbuf.at[z], q), zr.at[q, z], up_z)
            send(piece(hid, q), piece(zbuf.at[z], q), zr.at[q, z], down_z)
        to_slice(hid, z)
        spread.start()
        for step in range(1, 5):
            low, high = (z + NZ - step) % NZ, (z + step) % NZ
            for q in range(2):
                block = piece(zbuf.at[low], q)
                arrived(block, zr.at[q, low], up_z, zr.at[q, low])
                if step < 4:
                    send(block, block, zr.at[q, low], up_z)
                    block = piece(zbuf.at[high], q)
                    arrived(block, zr.at[q, high], up_z, zr.at[q, high])
                    if step < 3:
                        send(block, block, zr.at[q, high], down_z)
            to_slice(zbuf.at[low], low)
            if step < 4:
                to_slice(zbuf.at[high], high)

    with phase("A_stat"):
        small = Group(group_sems.at[2])
        squares = jnp.square(hid[...].astype(F32))
        for k in range(1, NZ):
            squares = squares + jnp.square(zbuf[(z + k) % NZ].astype(F32))
        stat[y] = row_tile(jnp.sum(squares, axis=1, keepdims=True))
        for k in range(1, NY):
            small(stat.at[y], stat.at[y], sr.at[0], at.at_y((y + k) % NY))

    turns = (2, 1, 3, 0)

    def group(k):
        return 2 * ((x + turns[k // 2]) % NX) + k % 2

    def y_send(k):
        block = xall.at[y, group(k)]
        sem = xr.at[group(k)]
        if k < 6:
            arrived(block, sem, up_y, sem)
        else:

            @pl.when(c != k % 2)
            def _():
                arrived(block, sem, up_y, sem)

            @pl.when(c == k % 2)
            def _():
                pltpu.make_async_copy(hid, block, xs.at[g]).wait()

        send(block, block, yr.at[0, k], up_y)
        send(block, block, yr.at[1, k], down_y)

    def y_relay(k):
        for side, step in ((0, 3), (1, 1)):
            block = xall.at[(y + step) % NY, group(k)]
            arrived(block, yr.at[side, k], up_y, yr.at[side, k])
            if k % 2 == side:
                send(block, block, y2.at[k], up_y if side == 0 else down_y)
        if k + 3 < 8:
            y_send(k + 3)

    def y_far(k):
        block = xall.at[(y + 2) % NY, group(k)]
        arrived(block, y2.at[k], up_y, y2.at[k])

    def normalise(k):
        i = group(k)
        scale = cols[i]
        scale = jnp.concatenate([scale, scale], axis=1)
        rows = pl.ds(pl.multiple_of(i * 128, 128), 128)
        for part in range(NY):
            columns = slice(part * 256, part * 256 + 256)
            values = xall[part, i].astype(F32)
            normed[rows, columns] = (values * scale * gain[:, columns]).astype(BF16)

    def pair_copy(step, t):
        return remote(
            pk.at[step, t, 1 - c], pr.at[step, t],
            pair_s.at[step], pair_r.at[step, t], at.partner(),
        )

    def multiply(step, t):
        rows = pl.ds(pl.multiple_of(((x + step) % NX) * 256, 256), 256)
        tile = pl.ds(pl.multiple_of(t * 256, 256), 256)
        part = lax.dot_general(
            normed[rows, :],
            weight[tile, :],
            (((1,), (1,)), ((), ())),
            preferred_element_type=F32,
        )
        pk[step, t, 0] = part[:128]
        pk[step, t, 1] = part[128:]
        pair_copy(step, t).start()

    def total_of(step, t):
        arrived(pr.at[step, t], pair_r.at[step, t], at.partner(), pair_r.at[step, t])
        return pk[step, t, c] + pr[step, t]

    def ways(t):
        way = 1 + 2 * (t % 2)
        return way, 4 - way

    def first_hop(t):
        ahead, _ = ways(t)
        return remote(sb.at[t, 0], rl.at[t], sb_s.at[0], rl_r.at[t], at.at_x((x + ahead) % NX))

    def direct(t):
        _, back = ways(t)
        return remote(
            sb.at[t, 1], fin.at[t, 0], sb_s.at[1], fin_r.at[t, 0], at.at_x((x + back) % NX)
        )

    def onward(t):
        ahead, _ = ways(t)
        return remote(
            sb.at[t, 2], fin.at[t, 1], sb_s.at[2], fin_r.at[t, 1], at.at_x((x + ahead) % NX)
        )

    def encode(t, k, value):
        left, right = value[:, :128], value[:, 128:]
        top = jnp.max(jnp.maximum(jnp.abs(left), jnp.abs(right)), axis=0, keepdims=True)
        step = (120.0 / jnp.maximum(top, 1e-30)).astype(BF16)
        sb[t, k, 256:] = jnp.broadcast_to(step, (16, 128))
        step = sb[t, k, 256:].astype(F32)[0:1]
        sb[t, k, :128] = jnp.exp2(left * step).astype(BF16)
        sb[t, k, 128:256] = jnp.exp2(right * step).astype(BF16)

    def decode(block):
        size = 1.0 / block[256:].astype(F32)[0:1]
        return jnp.concatenate(
            [
                jnp.log2(block[:128].astype(F32)) * size,
                jnp.log2(block[128:256].astype(F32)) * size,
            ],
            axis=1,
        )

    with phase("A_ysend"):
        for k in range(3):
            y_send(k)

    with phase("A_rf"):
        arrived(stat.at[0:3], sr.at[0], up_y, sr.at[0])
        total = stat[y]
        for k in range(1, NY):
            total = total + stat[(y + k) % NY]
        factor = lax.rsqrt(total / (1024.0 * 8) + 1e-05)
        rf[g] = stack_rows(factor[0:1], live)
        factors = Group(group_sems.at[3])
        for k in range(1, 8):
            factors(rf.at[g], rf.at[g], fr.at[0], at.dp((g + k) % 8))

    with phase("A_y0123"):
        y_relay(0)
        y_relay(1)
        spread.middle(True)
        y_relay(2)
        arrived(rf.at[0:7], fr.at[0], up_y, fr.at[0])
        for i in range(8):
            cols[i] = column_tile(rf[i, 0:1])
        y_relay(3)
        load_weight.wait()
        load_targets.wait()
    with phase("A_far01"):
        y_far(0)
        y_far(1)
        normalise(0)
        normalise(1)
    def run(low, high, *stages):
        @pl.loop(low, high)
        def _(t):
            for stage, lag in stages:
                stage(t - lag)

    def hop(t):
        encode(t, 0, total_of(2, t))
        first_hop(t).start()

    with phase("F_hop"):
        far_rows = (lambda t: multiply(2, t)), 0
        run(0, 3, far_rows)
        run(3, 6, far_rows, (hop, 3))
        y_relay(4)
        run(6, 8, far_rows, (hop, 3))
        y_relay(5)
        run(5, 8, (hop, 0))
    with phase("A_y6"):
        y_relay(6)
    with phase("A_far2345"):
        for k in range(2, 6):
            y_far(k)
            normalise(k)
    with phase("F_both"):

        def both(t):
            ahead, back = ways(t)
            encode(t, 1, total_of(back, t))
            direct(t).start()
            arrived(rl.at[t], rl_r.at[t], at.partner(), rl_r.at[t])
            encode(t, 2, total_of(ahead, t) + decode(rl.at[t]))
            onward(t).start()

        def near_rows(t):
            multiply(1, t)
            multiply(3, t)

        run(0, 3, (near_rows, 0))
        run(3, 5, (near_rows, 0), (both, 3))
        y_relay(7)
        run(5, 8, (near_rows, 0), (both, 3))
        run(5, 8, (both, 0))

    with phase("A_far67"):
        spread.middle(False)
        top = jnp.max(targets[...].astype(F32), axis=1, keepdims=True)
        part = jnp.zeros((128, 256), F32)
        for k in range(8):
            part = part + jnp.exp(targets[:, k * 256 : k * 256 + 256].astype(F32) - top)
        tst[...] = stack_rows(
            jnp.zeros((1, 128), F32),
            jnp.zeros((1, 128), F32),
            row_tile(top)[0:1],
            row_tile(jnp.sum(part, axis=1, keepdims=True))[0:1],
        )
        for k in range(6, 8):
            y_far(k)
            normalise(k)

    def finish(t):
        own = total_of(0, t)
        for k in range(2):
            arrived(fin.at[t, k], fin_r.at[t, k], at.partner(), fin_r.at[t, k])
        lg[t] = own + decode(fin.at[t, 0]) + decode(fin.at[t, 1])

    with phase("F_fin"):
        own_rows = (lambda t: multiply(0, t)), 0
        run(0, 3, own_rows)
        run(3, 8, own_rows, (finish, 3))
        run(5, 8, (finish, 0))

    def tell_all(tile, send_sem, recv_sem):
        @pl.loop(1, 32)
        def _(k):
            remote(
                tile.at[v], tile.at[v], send_sem, recv_sem.at[0], (g, (v + k) % 32)
            ).start()

    def hear_all(tile, recv_sem):
        arrived(tile.at[0:31], recv_sem.at[0], up_y, recv_sem.at[0])

    with phase("B_stat"):
        top = lg[0]
        for t in range(1, 8):
            top = jnp.maximum(top, lg[t])
        top = jnp.max(top, axis=1, keepdims=True)
        part = jnp.zeros((128, 256), F32)
        for t in range(8):
            part = part + jnp.exp(lg[t] - top)
        stat_v[v] = stack_rows(
            row_tile(top)[0:1],
            row_tile(jnp.sum(part, axis=1, keepdims=True))[0:1],
            tst[2:3],
            tst[3:4],
        )
        tell_all(stat_v, group_sems.at[5], sv_r)
        send.drain()

    with phase("B_statv"):
        hear_all(stat_v, sv_r)
        wide = lambda row: jnp.concatenate([column_tile(row)] * 2, axis=1)
        tops, scales = [], []
        for k in (0, 2):
            top = jnp.max(stat_v[:, k, :], axis=0, keepdims=True)
            part = stat_v[:, k + 1, :] * jnp.exp(stat_v[:, k, :] - top)
            tops.append(wide(top))
            scales.append(wide(1.0 / jnp.sum(part, axis=0, keepdims=True)))
        count = jnp.zeros((1, 128), F32)
        for i in range(8):
            count = count + rf[i, 1:2]
        count = jnp.sum(count, axis=1, keepdims=True)
        scale = wide(1048576.0 * live / count)

    gather = Gather(at, gbuf, Group(group_sems.at[1]), g_near, g_far, g_pair)
    with phase("B_G"):
        acc = jnp.zeros((128, 256), F32)
        for t in range(8):
            draft = jnp.exp(lg[t] - tops[0]) * scales[0]
            target = (
                jnp.exp(targets[:, t * 256 : t * 256 + 256].astype(F32) - tops[1]) * scales[1]
            )
            value = (scale * (draft - target)).astype(BF16)
            for k in range(8):
                gbuf[g, k % 2, k // 2 * 16 : k // 2 * 16 + 16, t * 256 : t * 256 + 256] = value[
                    k * 16 : k * 16 + 16
                ]
            acc = acc + value.astype(F32) * lg[t]
        gather.start()
        dot_v[v] = row_tile(jnp.sum(acc, axis=1, keepdims=True))
        tell_all(dot_v, group_sems.at[6], dv_r)

    units = (((0, 0), (0, 1)), ((3, 0), (1, 1)), ((3, 1), (1, 0)), ((2, 0), (2, 1)))

    def block_of(step):
        return (x + step) % NX

    def backward(k):
        for step, half in units[k]:
            gather.paired(step, half)

        @pl.loop(0, 4)
        def _(n):
            columns = pl.ds(pl.multiple_of(n * 256, 256), 256)
            rows = jnp.concatenate(
                [
                    gbuf[pl.ds(2 * block_of(step), 2), half].reshape(128, 2048)
                    for step, half in units[k]
                ],
                axis=0,
            )
            part = jnp.dot(rows, weight[:, columns], preferred_element_type=F32)
            for p in range(2):
                for which in range(2):
                    for dest in range(NY):
                        row = p * 128 + which * 64 + dest * 16
                        pf[k, dest, p, which, :, columns] = part[row : row + 16]

        way = 1 if k % 2 == 0 else 3
        ysb[k, 0] = pf[k, (y + 2) % NY].astype(BF16)
        send(ysb.at[k, 0], yrl.at[k], yrl_r.at[k], at.at_y((y + way) % NY))
        ysb[k, 1] = pf[k, (y + 4 - way) % NY].astype(BF16)
        send(ysb.at[k, 1], yfin.at[k, 0], yfin_r.at[k, 0], at.at_y((y + 4 - way) % NY))

    def y_second(k):
        way = 1 if k % 2 == 0 else 3
        arrived(yrl.at[k], yrl_r.at[k], up_y, yrl_r.at[k])
        ysb[k, 2] = (pf[k, (y + way) % NY] + yrl[k].astype(F32)).astype(BF16)
        send(ysb.at[k, 2], yfin.at[k, 1], yfin_r.at[k, 1], at.at_y((y + way) % NY))

    def z_send(k, dest):
        return remote(
            qs.at[k, dest], zrs.at[k, z], zs_s.at[k], zs_r.at[k], at.at_z(dest)
        )

    far_first = (4, 3, 5, 2, 6, 1, 7)

    def y_third(k):
        for j in range(2):
            arrived(yfin.at[k, j], yfin_r.at[k, j], up_y, yfin_r.at[k, j])
        value = pf[k, y] + yfin[k, 0].astype(F32) + yfin[k, 1].astype(F32)
        for owner in range(NZ):
            part = value[:, :, :, 128 * owner : 128 * owner + 128]
            qf[k, owner] = part
            qs[k, owner] = part.astype(BF16)
        for shift in far_first:
            z_send(k, (z + shift) % NZ).start()

    own_columns = pl.ds(pl.multiple_of(z * 128, 128), 128)

    def piece_of(k, owner):
        columns = pl.ds(pl.multiple_of(owner * 128, 128), 128)
        return grad_out.at[k, y, :, :, :, columns]

    def seven(k):
        return grad_out.at[k, y, :, :, :, 0:896]

    def z_fourth(k):
        total = qf[k, z]
        arrived(zrs.at[k, 0:7], zs_r.at[k], up_y, zs_r.at[k])
        for j in range(1, NZ):
            total = total + zrs[k, (z + j) % NZ].astype(F32)
        lanes = pl.ds(pl.multiple_of((z % 2) * 128, 128), 128)
        for p, (step, half) in enumerate(units[k]):
            rows = pl.ds(pl.multiple_of(y * 32 + half * 16, 16), 16)
            for which in range(2):
                i = 2 * block_of(step) + which
                values = xall[z // 2, i, rows, lanes].astype(F32)
                grad = cols[i, rows, :] * gain[:, own_columns] * total[p, which]
                grad = grad - values * scols[i, rows, :]
                grad_out[k, y, p, which, :, own_columns] = grad.astype(BF16)
        mine = piece_of(k, z)
        for shift in far_first:
            remote(mine, mine, az_s.at[k], a_z.at[k], at.at_z((z + shift) % NZ)).start()

    def across(k):
        arrived(seven(k), a_z.at[k], up_y, a_z.at[k])
        for turn in range(2):
            for side, device in ((0, up_y), (1, down_y)):
                p = side if turn == 0 else 1 - side
                mine = grad_out.at[k, y, p]
                send(mine, mine, a_y.at[side, k, p], device)

    def across_near(k, side, p):
        half = grad_out.at[k, (y + (3 if side == 0 else 1)) % NY, p]
        arrived(half, a_y.at[side, k, p], up_y, a_y.at[side, k, p])
        return half

    def across_relay(k):
        for side in range(2):
            half = across_near(k, side, side)
            send(half, half, a_y2.at[side, k], up_y if side == 0 else down_y)

    grad_to_hbm = pltpu.make_async_copy(grad_out.at[3], grad_hbm, local_sems.at[2])
    feat_to_hbm = pltpu.make_async_copy(feat_out.at[3], feat_hbm, local_sems.at[3])
    share_to_hbm = pltpu.make_async_copy(share_out, share_hbm, local_sems.at[10])
    acc_to_hbm = pltpu.make_async_copy(joined, joined_hbm, local_sems.at[4])

    def fold(k):
        @pl.loop(0, 4)
        def _(n):
            columns = pl.ds(pl.multiple_of(n * 256, 256), 256)
            part = lax.dot_general(
                grad_out[k, :, :, :, :, columns].reshape(256, 256),
                feat_out[k].reshape(256, 768),
                (((0,), (0,)), ((), ())),
                preferred_element_type=F32,
            )
            if k == 0:
                joined[columns, :] = part
            else:
                joined[columns, :] += part

    def across_far(k):
        for side in range(2):
            across_near(k, side, 1 - side)
        for side in range(2):
            half = grad_out.at[k, (y + 2) % NY, side]
            arrived(half, a_y2.at[side, k], up_y, a_y2.at[side, k])

    with phase("G_bw0"):
        backward(0)
    with phase("G_feat"):
        spread.last()
        for step in (0, 1, 3):
            for half in range(2):
                spread.paired(step, half)
    with phase("G_mid"):
        gather.middle(True)
    with phase("G_ys0"):
        y_second(0)
    with phase("G_dot"):
        hear_all(dot_v, dv_r)
        dot = jnp.sum(dot_v[:, 0, :], axis=0, keepdims=True)
        factor = rf[g][0:1]
        srow[g] = jnp.broadcast_to(factor * factor * dot / (1024.0 * 8), (8, 128))
        pulls = Group(group_sems.at[4])
        for k in range(1, 8):
            pulls(srow.at[g], srow.at[g], sd_r.at[0], at.dp((g + k) % 8))
    with phase("G_bw1"):
        backward(1)
    with phase("G_yt0"):
        y_third(0)
    with phase("G_mid2"):
        gather.middle(False)
    with phase("G_ys1"):
        y_second(1)
    with phase("G_bw2"):
        backward(2)
    with phase("G_s"):
        arrived(srow.at[0:7], sd_r.at[0], up_y, sd_r.at[0])
        for i in range(8):
            scols[i] = column_tile(srow[i, 0:1])
    with phase("G_z0"):
        z_fourth(0)
    with phase("G_last"):
        gather.last()
    with phase("G_yt1"):
        y_third(1)
    with phase("G_bw3"):
        backward(3)
    with phase("G_ys2"):
        y_second(2)
    with phase("H_ax0"):
        across(0)
    with phase("H_feat"):
        spread.paired(2, 0)
        spread.paired(2, 1)
        for k in range(4):
            for p, (step, half) in enumerate(units[k]):
                for which in range(2):
                    for dest in range(NY):
                        row = dest % 2 * 32 + half * 16
                        feat_out[k, dest, p, which] = fall[
                            2 * block_of(step) + which, dest // 2, row : row + 16, :
                        ]
        feat_to_hbm.start()
    with phase("H_z1"):
        z_fourth(1)
    with phase("G_ys3"):
        y_second(3)
    with phase("G_yt2"):
        y_third(2)
    with phase("H_ax1"):
        across(1)
    with phase("G_yt3"):
        y_third(3)
    with phase("H_ar0"):
        across_relay(0)
    with phase("H_z2"):
        z_fourth(2)
    with phase("H_far0"):
        across_far(0)
    with phase("H_ar1"):
        across_relay(1)
    with phase("H_z3"):
        z_fourth(3)
    with phase("H_ax2"):
        across(2)
    with phase("H_fold0"):
        fold(0)
    with phase("H_far1"):
        across_far(1)
    with phase("H_ar2"):
        across_relay(2)
    with phase("H_ax3"):
        across(3)
    with phase("H_fold1"):
        fold(1)
    with phase("H_far2"):
        across_far(2)
    with phase("H_ar3"):
        across_relay(3)
    with phase("H_fold2"):
        fold(2)
        acc_to_hbm.start()
    with phase("H_far"):
        across_far(3)
        grad_to_hbm.start()
        away = (z // 2 + NX - x) % NX
        odd, side = away % 2, away // 2
        for half in range(2):
            k = odd * (1 + (half + side + 1) % 2) + (1 - odd) * 3 * side
            p = odd * (1 - side) + (1 - odd) * half
            share_out[16 * half : 16 * half + 16, :] = grad_out[k, y, p, z % 2]
        share_to_hbm.start()
        share_to_hbm.wait()
        grad_to_hbm.wait()
        feat_to_hbm.wait()
        acc_to_hbm.wait()

    with phase("H_drain"):
        there = at.partner()
        for step in range(NX):
            remote(
                pr.at[step], pr.at[step], pair_s.at[step], pair_r.at[step, 0], there
            ).wait_send()
        for k in range(3):
            remote(rl, rl, sb_s.at[k], rl_r.at[0], there).wait_send()
        for k, like in enumerate(
            (
                fall.at[0:7], gbuf.at[0:7], stat.at[0:3], rf.at[0:7],
                srow.at[0:7], stat_v.at[0:31], dot_v.at[0:31],
            )
        ):
            Group(group_sems.at[k]).drain(like, there)
        send.drain()
        for k in range(4):
            remote(
                qs.at[k, 0:7], zrs.at[k, 0:7], zs_s.at[k], zs_r.at[k], there
            ).wait_send()
            remote(seven(k), seven(k), az_s.at[k], a_z.at[k], there).wait_send()
        for j in range(8):

            @pl.when(g != j)
            def _():
                remote(hid, xall.at[y, g], xs.at[j], xr.at[g], at.dp(j)).wait_send()


VMEM = pl.BlockSpec(memory_space=pltpu.VMEM)
HBM = pl.BlockSpec(memory_space=pl.ANY)
LIMIT = 60 * 1024 * 1024


def call(*operands):
    return pl.pallas_call(
        kernel,
        out_shape=(
            jax.ShapeDtypeStruct((32, 1024), BF16),
            jax.ShapeDtypeStruct((1024, 768), F32),
            jax.ShapeDtypeStruct((NY, 2, 2, 16, 1024), BF16),
            jax.ShapeDtypeStruct((NY, 2, 2, 16, 768), BF16),
        ),
        in_specs=[HBM] * 7,
        out_specs=[HBM] * 4,
        scratch_shapes=[
            pltpu.VMEM((128, 256), BF16),
            pltpu.VMEM((1, 128), jnp.int32),
            pltpu.VMEM((1, 128), jnp.int32),
            pltpu.VMEM((128, 768), BF16),
            pltpu.VMEM((8, 8, 128), F32),
            pltpu.VMEM((32, 1024), BF16),
            pltpu.VMEM((1024, 768), F32),
            pltpu.VMEM((4, NY, 2, 2, 16, 1024), BF16),
            pltpu.VMEM((4, NY, 2, 2, 16, 768), BF16),
            pltpu.VMEM((8, 2, 64, 768), BF16),
            pltpu.VMEM((2048, 1024), BF16),
            pltpu.VMEM((128, 2048), BF16),
            pltpu.VMEM((NZ, 128, 256), BF16),
            pltpu.VMEM((NY, 8, 128, 256), BF16),
            pltpu.VMEM((1024, 1024), BF16),
            pltpu.VMEM((NY, 8, 128), F32),
            pltpu.VMEM((8, 128, 128), F32),
            pltpu.VMEM((8, 128, 128), F32),
            pltpu.VMEM((8, 8, 128), F32),
            pltpu.VMEM((8, 8, 128), F32),
            pltpu.VMEM((1, 1024), F32),
            pltpu.VMEM((NX, 8, 2, 128, 256), F32),
            pltpu.VMEM((NX, 8, 128, 256), F32),
            pltpu.VMEM((8, 3, 272, 128), BF16),
            pltpu.VMEM((8, 272, 128), BF16),
            pltpu.VMEM((8, 2, 272, 128), BF16),
            pltpu.VMEM((8, 128, 256), F32),
            pltpu.VMEM((8, 128), F32),
            pltpu.VMEM((32, 8, 128), F32),
            pltpu.VMEM((32, 8, 128), F32),
            pltpu.VMEM((8, 2, 64, 2048), BF16),
            pltpu.VMEM((4, NY, 2, 2, 16, 1024), F32),
            pltpu.VMEM((4, 3, 2, 2, 16, 1024), BF16),
            pltpu.VMEM((4, 2, 2, 16, 1024), BF16),
            pltpu.VMEM((4, 2, 2, 2, 16, 1024), BF16),
            pltpu.VMEM((4, NZ, 2, 2, 16, 128), F32),
            pltpu.VMEM((4, NZ, 2, 2, 16, 128), BF16),
            pltpu.VMEM((4, NZ, 2, 2, 16, 128), BF16),
            DMA((11,)),
            DMA((38,)),
            DMA((7,)),
            DMA((2, NZ)),
            DMA((8,)),
            DMA((8,)),
            DMA((2, 8)),
            DMA((8,)),
            DMA((1,)),
            DMA((1,)),
            DMA((2, 2)),
            DMA((2,)),
            DMA((4, 2)),
            DMA((NX,)),
            DMA((NX, 8)),
            DMA((3,)),
            DMA((8,)),
            DMA((8, 2)),
            DMA((1,)),
            DMA((1,)),
            DMA((1,)),
            DMA((2, 2)),
            DMA((2,)),
            DMA((4, 2)),
            DMA((4,)),
            DMA((4, 2)),
            DMA((4,)),
            DMA((4,)),
            DMA((4,)),
            DMA((4,)),
            DMA((2, 4, 2)),
            DMA((2, 4)),
        ],
        compiler_params=pltpu.CompilerParams(
            collective_id=0, has_side_effects=True, vmem_limit_bytes=LIMIT
        ),
    )(*operands)


def body(hidden, norm_gain, head_weight, target_logits, valid_rows, parents, features):
    share, joined, grad, parent_features = call(
        hidden,
        valid_rows.reshape(1, 128),
        parents.reshape(1, 128),
        features,
        norm_gain.reshape(8, 8, 128),
        head_weight,
        target_logits,
    )
    grad_joining = joined + lax.dot_general(
        *lax.optimization_barrier(
            (grad.reshape(256, 1024), parent_features.reshape(256, 768))
        ),
        (((0,), (0,)), ((), ())),
        preferred_element_type=F32,
    )
    return (share, grad_joining)


def solution(mesh):
    placed = (
        P("dp", "vocab"),
        P(),
        P("vocab", "dp"),
        P("dp", "vocab"),
        P("dp"),
        P("dp"),
        P("dp", "vocab"),
    )
    return jax.shard_map(
        body,
        mesh=mesh,
        in_specs=placed,
        out_specs=(P("vocab", "dp"), P("dp", "vocab")),
        check_vma=False,
    )
```

```python
import contextlib

import jax
import jax.numpy as jnp
from jax import lax
from jax.experimental import pallas as pl
from jax.experimental.pallas import tpu as pltpu
from jax.sharding import PartitionSpec as P

TREE = 64
NX, NC, NY, NZ = 4, 2, 4, 8
F32, BF16 = jnp.float32, jnp.bfloat16
DMA = pltpu.SemaphoreType.DMA


def remote(src, dst, send_sem, recv_sem, device):
    return pltpu.make_async_remote_copy(
        src_ref=src,
        dst_ref=dst,
        send_sem=send_sem,
        recv_sem=recv_sem,
        device_id=device,
        device_id_type=pl.DeviceIdType.MESH,
    )


def phase(name):
    return contextlib.nullcontext()


class Place:
    def __init__(self):
        self.g = lax.axis_index("dp")
        self.v = lax.axis_index("vocab")
        self.x, self.c = self.g // NC, self.g % NC
        self.z, self.y = self.v // NY, self.v % NY

    def dp(self, i):
        return (i, self.v)

    def at_x(self, x):
        return (x * NC + self.c, self.v)

    def partner(self):
        return (self.x * NC + 1 - self.c, self.v)

    def at_y(self, y):
        return (self.g, self.z * NY + y)

    def at_z(self, z):
        return (self.g, z * NY + self.y)


class Group:
    def __init__(self, sem):
        self.sem = sem

    def __call__(self, src, dst, recv_sem, device):
        remote(src, dst, self.sem, recv_sem, device).start()

    def drain(self, like, device):
        remote(like, like, self.sem, self.sem, device).wait_send()


def arrived(dst, recv_sem, device, any_sem):
    remote(dst, dst, any_sem, recv_sem, device).wait_recv()


class Gather:
    def __init__(self, at, buf, send, near, far, pair):
        self.at, self.buf, self.send = at, buf, send
        self.near, self.far, self.pair = near, far, pair

    def slot(self, step, core):
        return ((self.at.x + step) % NX) * NC + core

    def start(self):
        at, buf = self.at, self.buf
        up, down = at.at_x((at.x + 1) % NX), at.at_x((at.x + 3) % NX)
        for k in range(2):
            for side, half, device in ((0, k, up), (1, 1 - k, down)):
                mine = buf.at[at.g, half]
                self.send(mine, mine, self.near.at[side, half], device)
            mine = buf.at[at.g, k]
            self.send(mine, mine, self.pair.at[0, k], at.partner())

    def middle(self, first):
        at, buf = self.at, self.buf
        for side, step in ((0, 3), (1, 1)):
            half = side if first else 1 - side
            block = buf.at[self.slot(step, at.c), half]
            arrived(block, self.near.at[side, half], at.partner(), self.near.at[side, half])
            if first:
                onward = at.at_x((at.x + (1 if side == 0 else 3)) % NX)
                self.send(block, block, self.far.at[half], onward)
            self.send(block, block, self.pair.at[step, half], at.partner())

    def last(self):
        at, buf = self.at, self.buf
        for half in range(2):
            block = buf.at[self.slot(2, at.c), half]
            arrived(block, self.far.at[half], at.partner(), self.far.at[half])
            self.send(block, block, self.pair.at[2, half], at.partner())

    def paired(self, step, half):
        at = self.at
        block = self.buf.at[self.slot(step, 1 - at.c), half]
        arrived(block, self.pair.at[step, half], at.partner(), self.pair.at[step, half])


def row_tile(column):
    return jnp.transpose(jnp.broadcast_to(column, (128, 128)))[0:8]


def column_tile(row):
    return jnp.transpose(jnp.broadcast_to(row, (128, 128)))


def stack_rows(*rows):
    index = lax.broadcasted_iota(jnp.int32, (8, 128), 0)
    tile = jnp.zeros((8, 128), F32)
    for k, row in enumerate(rows):
        tile = jnp.where(index == k, row, tile)
    return tile


def kernel(
    hid_hbm, valid_hbm, parents_hbm, feat_hbm_in, gains_hbm, weight_hbm, targets_hbm,
    share_hbm, joined_hbm, grad_hbm, feat_hbm,
    hid, valid, parents, feat, gains, share_out,
    joined, grad_out, feat_out, fall,
    weight, targets, zbuf, xall, normed, stat, cols, scols, rf, srow, gain,
    pk, pr, sb, rl, fin, lg, tst, stat_v, dot_v, gbuf, pf, ysb, yrl, yfin,
    qf, qs, zrs,
    local_sems, group_sems, zr, xs, xr, yr, y2, sr, fr,
    f_near, f_far, f_pair,
    pair_s, pair_r, sb_s, rl_r, fin_r,
    sv_r, dv_r, sd_r, g_near, g_far, g_pair,
    yrl_r, yfin_r, zs_s, zs_r, az_s, a_z, a_y, a_y2,
):
    at = Place()
    x, c, y, z, g, v = at.x, at.c, at.y, at.z, at.g, at.v
    up_z, down_z = at.at_z((z + 1) % NZ), at.at_z((z + NZ - 1) % NZ)
    up_y, down_y = at.at_y((y + 1) % NY), at.at_y((y + 3) % NY)

    loads = [
        pltpu.make_async_copy(src, dst, local_sems.at[5 + k])
        for k, (src, dst) in enumerate(
            (
                (hid_hbm, hid),
                (parents_hbm, parents),
                (feat_hbm_in, feat),
                (valid_hbm, valid),
                (gains_hbm, gains),
            )
        )
    ]
    for load in loads:
        load.start()
    load_weight = pltpu.make_async_copy(weight_hbm, weight, local_sems.at[0])
    load_targets = pltpu.make_async_copy(targets_hbm, targets, local_sems.at[1])
    load_weight.start()
    load_targets.start()

    with phase("A_feat"):
        barrier = pltpu.get_barrier_semaphore()

        @pl.loop(1, 32)
        def _(k):
            pl.semaphore_signal(
                barrier,
                inc=1,
                device_id=(g, (v + k) % 32),
                device_id_type=pl.DeviceIdType.MESH,
            )

        @pl.loop(1, 8)
        def _(k):
            pl.semaphore_signal(
                barrier,
                inc=1,
                device_id=((g + k) % 8, v),
                device_id_type=pl.DeviceIdType.MESH,
            )

    with phase("A_load"):
        for load in loads:
            load.wait()
    with phase("A_own"):
        live = (valid[...] == 1).astype(F32)
        row = lax.broadcasted_iota(jnp.int32, (128, 128), 0)
        lane = lax.broadcasted_iota(jnp.int32, (128, 128), 1)
        wanted = column_tile(parents[...].astype(F32)).astype(jnp.int32) + row // TREE * TREE
        pick = (lane == wanted).astype(BF16)
        chosen = jnp.dot(pick, feat[...], preferred_element_type=F32).astype(BF16)
        fall[g, 0] = chosen[:64]
        fall[g, 1] = chosen[64:]
        own_gain = gains[g]
        gain[...] = jnp.concatenate([own_gain[k : k + 1] for k in range(8)], axis=1)

    with phase("A_greet"):
        pl.semaphore_wait(barrier, 38)
    send_z, send_y = Group(group_sems.at[7]), Group(group_sems.at[8])
    send_part, send_grad = Group(group_sems.at[9]), Group(group_sems.at[10])
    send_x = Group(group_sems.at[11])
    spread = Gather(at, fall, Group(group_sems.at[0]), f_near, f_far, f_pair)

    def to_slice(src, j):
        @pl.when(j != g)
        def _():
            send_x(src, xall.at[y, g], xr.at[g], at.dp(j))

        @pl.when(j == g)
        def _():
            pltpu.make_async_copy(src, xall.at[y, g], xs.at[0]).start()

    def piece(ref, q):
        return ref.at[64 * q : 64 * q + 64]

    with phase("A_z"):
        for q in range(2):
            send_z(piece(hid, q), piece(zbuf.at[z], q), zr.at[q, z], up_z)
            send_z(piece(hid, q), piece(zbuf.at[z], q), zr.at[q, z], down_z)
        to_slice(hid, z)
        spread.start()
        for step in range(1, 5):
            low, high = (z + NZ - step) % NZ, (z + step) % NZ
            for q in range(2):
                block = piece(zbuf.at[low], q)
                arrived(block, zr.at[q, low], up_z, zr.at[q, low])
                if step < 4:
                    send_z(block, block, zr.at[q, low], up_z)
                    block = piece(zbuf.at[high], q)
                    arrived(block, zr.at[q, high], up_z, zr.at[q, high])
                    if step < 3:
                        send_z(block, block, zr.at[q, high], down_z)
            to_slice(zbuf.at[low], low)
            if step < 4:
                to_slice(zbuf.at[high], high)

    with phase("A_stat"):
        small = Group(group_sems.at[2])
        squares = jnp.square(hid[...].astype(F32))
        for k in range(1, NZ):
            squares = squares + jnp.square(zbuf[(z + k) % NZ].astype(F32))
        stat[y] = row_tile(jnp.sum(squares, axis=1, keepdims=True))
        for k in range(1, NY):
            small(stat.at[y], stat.at[y], sr.at[0], at.at_y((y + k) % NY))

    turns = (2, 1, 3, 0)

    def group(k):
        return 2 * ((x + turns[k // 2]) % NX) + k % 2

    def y_send(k):
        block = xall.at[y, group(k)]
        sem = xr.at[group(k)]
        if k < 6:
            arrived(block, sem, up_y, sem)
        else:

            @pl.when(c != k % 2)
            def _():
                arrived(block, sem, up_y, sem)

            @pl.when(c == k % 2)
            def _():
                pltpu.make_async_copy(hid, block, xs.at[0]).wait()

        send_y(block, block, yr.at[0, k], up_y)
        send_y(block, block, yr.at[1, k], down_y)

    def y_relay(k):
        for side, step in ((0, 3), (1, 1)):
            block = xall.at[(y + step) % NY, group(k)]
            arrived(block, yr.at[side, k], up_y, yr.at[side, k])
            if k % 2 == side:
                send_y(block, block, y2.at[k], up_y if side == 0 else down_y)
        if k + 3 < 8:
            y_send(k + 3)

    def y_far(k):
        block = xall.at[(y + 2) % NY, group(k)]
        arrived(block, y2.at[k], up_y, y2.at[k])

    def normalise(k):
        i = group(k)
        scale = cols[i]
        scale = jnp.concatenate([scale, scale], axis=1)
        rows = pl.ds(pl.multiple_of(i * 128, 128), 128)
        for part in range(NY):
            columns = slice(part * 256, part * 256 + 256)
            values = xall[part, i].astype(F32)
            normed[rows, columns] = (values * scale * gain[:, columns]).astype(BF16)

    def pair_copy(step, t):
        return remote(
            pk.at[step, t, 1 - c], pr.at[step, t],
            pair_s.at[step], pair_r.at[step, t], at.partner(),
        )

    def multiply(step, t):
        rows = pl.ds(pl.multiple_of(((x + step) % NX) * 256, 256), 256)
        tile = pl.ds(pl.multiple_of(t * 256, 256), 256)
        part = lax.dot_general(
            normed[rows, :],
            weight[tile, :],
            (((1,), (1,)), ((), ())),
            preferred_element_type=F32,
        )
        pk[step, t, 0] = part[:128]
        pk[step, t, 1] = part[128:]
        pair_copy(step, t).start()

    def total_of(step, t):
        arrived(pr.at[step, t], pair_r.at[step, t], at.partner(), pair_r.at[step, t])
        return pk[step, t, c] + pr[step, t]

    def ways(t):
        way = 1 + 2 * (t % 2)
        return way, 4 - way

    def first_hop(t):
        ahead, _ = ways(t)
        return remote(sb.at[t, 0], rl.at[t], sb_s.at[0], rl_r.at[t], at.at_x((x + ahead) % NX))

    def direct(t):
        _, back = ways(t)
        return remote(
            sb.at[t, 1], fin.at[t, 0], sb_s.at[1], fin_r.at[t, 0], at.at_x((x + back) % NX)
        )

    def onward(t):
        ahead, _ = ways(t)
        return remote(
            sb.at[t, 2], fin.at[t, 1], sb_s.at[2], fin_r.at[t, 1], at.at_x((x + ahead) % NX)
        )

    def encode(t, k, value):
        left, right = value[:, :128], value[:, 128:]
        top = jnp.max(jnp.maximum(jnp.abs(left), jnp.abs(right)), axis=0, keepdims=True)
        step = (120.0 / jnp.maximum(top, 1e-30)).astype(BF16)
        sb[t, k, 256:] = jnp.broadcast_to(step, (16, 128))
        step = sb[t, k, 256:].astype(F32)[0:1]
        sb[t, k, :128] = jnp.exp2(left * step).astype(BF16)
        sb[t, k, 128:256] = jnp.exp2(right * step).astype(BF16)

    def decode(block):
        size = 1.0 / block[256:].astype(F32)[0:1]
        return jnp.concatenate(
            [
                jnp.log2(block[:128].astype(F32)) * size,
                jnp.log2(block[128:256].astype(F32)) * size,
            ],
            axis=1,
        )

    with phase("A_ysend"):
        for k in range(3):
            y_send(k)

    with phase("A_rf"):
        arrived(stat.at[0:3], sr.at[0], up_y, sr.at[0])
        total = stat[y]
        for k in range(1, NY):
            total = total + stat[(y + k) % NY]
        factor = lax.rsqrt(total / (1024.0 * 8) + 1e-05)
        rf[g] = stack_rows(factor[0:1], live)
        factors = Group(group_sems.at[3])
        for k in range(1, 8):
            factors(rf.at[g], rf.at[g], fr.at[0], at.dp((g + k) % 8))

    with phase("A_y0123"):
        y_relay(0)
        y_relay(1)
        spread.middle(True)
        y_relay(2)
        arrived(rf.at[0:7], fr.at[0], up_y, fr.at[0])
        for i in range(8):
            cols[i] = column_tile(rf[i, 0:1])
        y_relay(3)
        load_weight.wait()
        load_targets.wait()
    with phase("A_far01"):
        y_far(0)
        y_far(1)
        normalise(0)
        normalise(1)
    def run(low, high, *stages):
        @pl.loop(low, high)
        def _(t):
            for stage, lag in stages:
                stage(t - lag)

    def hop(t):
        encode(t, 0, total_of(2, t))
        first_hop(t).start()

    with phase("F_hop"):
        far_rows = (lambda t: multiply(2, t)), 0
        run(0, 3, far_rows)
        run(3, 6, far_rows, (hop, 3))
        y_relay(4)
        run(6, 8, far_rows, (hop, 3))
        y_relay(5)
        run(5, 8, (hop, 0))
    with phase("A_y6"):
        y_relay(6)
    with phase("A_far2345"):
        for k in range(2, 6):
            y_far(k)
            normalise(k)
    with phase("F_both"):

        def both(t):
            ahead, back = ways(t)
            encode(t, 1, total_of(back, t))
            direct(t).start()
            arrived(rl.at[t], rl_r.at[t], at.partner(), rl_r.at[t])
            encode(t, 2, total_of(ahead, t) + decode(rl.at[t]))
            onward(t).start()

        def near_rows(t):
            multiply(1, t)
            multiply(3, t)

        run(0, 3, (near_rows, 0))
        run(3, 5, (near_rows, 0), (both, 3))
        y_relay(7)
        run(5, 8, (near_rows, 0), (both, 3))
        run(5, 8, (both, 0))

    with phase("A_far67"):
        spread.middle(False)
        top = jnp.max(targets[...].astype(F32), axis=1, keepdims=True)
        part = jnp.zeros((128, 256), F32)
        for k in range(8):
            part = part + jnp.exp(targets[:, k * 256 : k * 256 + 256].astype(F32) - top)
        tst[...] = stack_rows(
            jnp.zeros((1, 128), F32),
            jnp.zeros((1, 128), F32),
            row_tile(top)[0:1],
            row_tile(jnp.sum(part, axis=1, keepdims=True))[0:1],
        )
        for k in range(6, 8):
            y_far(k)
            normalise(k)

    def finish(t):
        own = total_of(0, t)
        for k in range(2):
            arrived(fin.at[t, k], fin_r.at[t, k], at.partner(), fin_r.at[t, k])
        lg[t] = own + decode(fin.at[t, 0]) + decode(fin.at[t, 1])

    with phase("F_fin"):
        own_rows = (lambda t: multiply(0, t)), 0
        run(0, 3, own_rows)
        run(3, 8, own_rows, (finish, 3))
        run(5, 8, (finish, 0))

    def tell_all(tile, send_sem, recv_sem):
        @pl.loop(1, 32)
        def _(k):
            remote(
                tile.at[v], tile.at[v], send_sem, recv_sem.at[0], (g, (v + k) % 32)
            ).start()

    def hear_all(tile, recv_sem):
        arrived(tile.at[0:31], recv_sem.at[0], up_y, recv_sem.at[0])

    with phase("B_stat"):
        top = lg[0]
        for t in range(1, 8):
            top = jnp.maximum(top, lg[t])
        top = jnp.max(top, axis=1, keepdims=True)
        part = jnp.zeros((128, 256), F32)
        for t in range(8):
            part = part + jnp.exp(lg[t] - top)
        stat_v[v] = stack_rows(
            row_tile(top)[0:1],
            row_tile(jnp.sum(part, axis=1, keepdims=True))[0:1],
            tst[2:3],
            tst[3:4],
        )
        tell_all(stat_v, group_sems.at[5], sv_r)

    with phase("B_statv"):
        hear_all(stat_v, sv_r)
        wide = lambda row: jnp.concatenate([column_tile(row)] * 2, axis=1)
        tops, scales = [], []
        for k in (0, 2):
            top = jnp.max(stat_v[:, k, :], axis=0, keepdims=True)
            part = stat_v[:, k + 1, :] * jnp.exp(stat_v[:, k, :] - top)
            tops.append(wide(top))
            scales.append(wide(1.0 / jnp.sum(part, axis=0, keepdims=True)))
        count = jnp.zeros((1, 128), F32)
        for i in range(8):
            count = count + rf[i, 1:2]
        count = jnp.sum(count, axis=1, keepdims=True)
        scale = wide(1048576.0 * live / count)

    gather = Gather(at, gbuf, Group(group_sems.at[1]), g_near, g_far, g_pair)
    with phase("B_G"):
        acc = jnp.zeros((128, 256), F32)
        for t in range(8):
            draft = jnp.exp(lg[t] - tops[0]) * scales[0]
            target = (
                jnp.exp(targets[:, t * 256 : t * 256 + 256].astype(F32) - tops[1]) * scales[1]
            )
            value = (scale * (draft - target)).astype(BF16)
            for k in range(8):
                gbuf[g, k % 2, k // 2 * 16 : k // 2 * 16 + 16, t * 256 : t * 256 + 256] = value[
                    k * 16 : k * 16 + 16
                ]
            acc = acc + value.astype(F32) * lg[t]
        gather.start()
        dot_v[v] = row_tile(jnp.sum(acc, axis=1, keepdims=True))
        tell_all(dot_v, group_sems.at[6], dv_r)

    units = (((0, 0), (0, 1)), ((3, 0), (1, 1)), ((3, 1), (1, 0)), ((2, 0), (2, 1)))

    def block_of(step):
        return (x + step) % NX

    def backward(k):
        for step, half in units[k]:
            gather.paired(step, half)

        @pl.loop(0, 4)
        def _(n):
            columns = pl.ds(pl.multiple_of(n * 256, 256), 256)
            rows = jnp.concatenate(
                [
                    gbuf[pl.ds(2 * block_of(step), 2), half].reshape(128, 2048)
                    for step, half in units[k]
                ],
                axis=0,
            )
            part = jnp.dot(rows, weight[:, columns], preferred_element_type=F32)
            for p in range(2):
                for which in range(2):
                    for dest in range(NY):
                        row = p * 128 + which * 64 + dest * 16
                        pf[k, dest, p, which, :, columns] = part[row : row + 16]

        way = 1 if k % 2 == 0 else 3
        ysb[k, 0] = pf[k, (y + 2) % NY].astype(BF16)
        send_part(ysb.at[k, 0], yrl.at[k], yrl_r.at[k], at.at_y((y + way) % NY))
        ysb[k, 1] = pf[k, (y + 4 - way) % NY].astype(BF16)
        send_part(ysb.at[k, 1], yfin.at[k, 0], yfin_r.at[k, 0], at.at_y((y + 4 - way) % NY))

    def y_second(k):
        way = 1 if k % 2 == 0 else 3
        arrived(yrl.at[k], yrl_r.at[k], up_y, yrl_r.at[k])
        ysb[k, 2] = (pf[k, (y + way) % NY] + yrl[k].astype(F32)).astype(BF16)
        send_part(ysb.at[k, 2], yfin.at[k, 1], yfin_r.at[k, 1], at.at_y((y + way) % NY))

    def z_send(k, dest):
        return remote(
            qs.at[k, dest], zrs.at[k, z], zs_s.at[k], zs_r.at[k], at.at_z(dest)
        )

    far_first = (4, 3, 5, 2, 6, 1, 7)

    def y_third(k):
        for j in range(2):
            arrived(yfin.at[k, j], yfin_r.at[k, j], up_y, yfin_r.at[k, j])
        value = pf[k, y] + yfin[k, 0].astype(F32) + yfin[k, 1].astype(F32)
        for owner in range(NZ):
            part = value[:, :, :, 128 * owner : 128 * owner + 128]
            qf[k, owner] = part
            qs[k, owner] = part.astype(BF16)
        for shift in far_first:
            z_send(k, (z + shift) % NZ).start()

    own_columns = pl.ds(pl.multiple_of(z * 128, 128), 128)

    def piece_of(k, owner):
        columns = pl.ds(pl.multiple_of(owner * 128, 128), 128)
        return grad_out.at[k, y, :, :, :, columns]

    def seven(k):
        return grad_out.at[k, y, :, :, :, 0:896]

    def z_fourth(k):
        total = qf[k, z]
        arrived(zrs.at[k, 0:7], zs_r.at[k], up_y, zs_r.at[k])
        for j in range(1, NZ):
            total = total + zrs[k, (z + j) % NZ].astype(F32)
        lanes = pl.ds(pl.multiple_of((z % 2) * 128, 128), 128)
        for p, (step, half) in enumerate(units[k]):
            rows = pl.ds(pl.multiple_of(y * 32 + half * 16, 16), 16)
            for which in range(2):
                i = 2 * block_of(step) + which
                values = xall[z // 2, i, rows, lanes].astype(F32)
                grad = cols[i, rows, :] * gain[:, own_columns] * total[p, which]
                grad = grad - values * scols[i, rows, :]
                grad_out[k, y, p, which, :, own_columns] = grad.astype(BF16)
        mine = piece_of(k, z)
        for shift in far_first:
            remote(mine, mine, az_s.at[k], a_z.at[k], at.at_z((z + shift) % NZ)).start()

    def across(k):
        arrived(seven(k), a_z.at[k], up_y, a_z.at[k])
        for turn in range(2):
            for side, device in ((0, up_y), (1, down_y)):
                p = side if turn == 0 else 1 - side
                mine = grad_out.at[k, y, p]
                send_grad(mine, mine, a_y.at[side, k, p], device)

    def across_near(k, side, p):
        half = grad_out.at[k, (y + (3 if side == 0 else 1)) % NY, p]
        arrived(half, a_y.at[side, k, p], up_y, a_y.at[side, k, p])
        return half

    def across_relay(k):
        for side in range(2):
            half = across_near(k, side, side)
            send_grad(half, half, a_y2.at[side, k], up_y if side == 0 else down_y)

    grad_to_hbm = pltpu.make_async_copy(grad_out.at[3], grad_hbm, local_sems.at[2])
    feat_to_hbm = pltpu.make_async_copy(feat_out.at[3], feat_hbm, local_sems.at[3])
    share_to_hbm = pltpu.make_async_copy(share_out, share_hbm, local_sems.at[10])
    acc_to_hbm = pltpu.make_async_copy(joined, joined_hbm, local_sems.at[4])

    def fold(k):
        @pl.loop(0, 4)
        def _(n):
            columns = pl.ds(pl.multiple_of(n * 256, 256), 256)
            part = lax.dot_general(
                grad_out[k, :, :, :, :, columns].reshape(256, 256),
                feat_out[k].reshape(256, 768),
                (((0,), (0,)), ((), ())),
                preferred_element_type=F32,
            )
            if k == 0:
                joined[columns, :] = part
            else:
                joined[columns, :] += part

    def across_far(k):
        for side in range(2):
            across_near(k, side, 1 - side)
        for side in range(2):
            half = grad_out.at[k, (y + 2) % NY, side]
            arrived(half, a_y2.at[side, k], up_y, a_y2.at[side, k])

    with phase("G_bw0"):
        backward(0)
    with phase("G_feat"):
        spread.last()
        for step in (0, 1, 3):
            for half in range(2):
                spread.paired(step, half)
    with phase("G_mid"):
        gather.middle(True)
    with phase("G_ys0"):
        y_second(0)
    with phase("G_dot"):
        hear_all(dot_v, dv_r)
        dot = jnp.sum(dot_v[:, 0, :], axis=0, keepdims=True)
        factor = rf[g][0:1]
        srow[g] = jnp.broadcast_to(factor * factor * dot / (1024.0 * 8), (8, 128))
        pulls = Group(group_sems.at[4])
        for k in range(1, 8):
            pulls(srow.at[g], srow.at[g], sd_r.at[0], at.dp((g + k) % 8))
    with phase("G_bw1"):
        backward(1)
    with phase("G_yt0"):
        y_third(0)
    with phase("G_mid2"):
        gather.middle(False)
    with phase("G_ys1"):
        y_second(1)
    with phase("G_bw2"):
        backward(2)
    with phase("G_s"):
        arrived(srow.at[0:7], sd_r.at[0], up_y, sd_r.at[0])
        for i in range(8):
            scols[i] = column_tile(srow[i, 0:1])
    with phase("G_z0"):
        z_fourth(0)
    with phase("G_last"):
        gather.last()
    with phase("G_yt1"):
        y_third(1)
    with phase("G_bw3"):
        backward(3)
    with phase("G_ys2"):
        y_second(2)
    with phase("H_ax0"):
        across(0)
    with phase("H_feat"):
        spread.paired(2, 0)
        spread.paired(2, 1)
        for k in range(4):
            for p, (step, half) in enumerate(units[k]):
                for which in range(2):
                    for dest in range(NY):
                        row = dest % 2 * 32 + half * 16
                        feat_out[k, dest, p, which] = fall[
                            2 * block_of(step) + which, dest // 2, row : row + 16, :
                        ]
        feat_to_hbm.start()
    with phase("H_z1"):
        z_fourth(1)
    with phase("G_ys3"):
        y_second(3)
    with phase("G_yt2"):
        y_third(2)
    with phase("H_ax1"):
        across(1)
    with phase("G_yt3"):
        y_third(3)
    with phase("H_ar0"):
        across_relay(0)
    with phase("H_z2"):
        z_fourth(2)
    with phase("H_far0"):
        across_far(0)
    with phase("H_ar1"):
        across_relay(1)
    with phase("H_z3"):
        z_fourth(3)
    with phase("H_fold0"):
        fold(0)
    with phase("H_ax2"):
        across(2)
    with phase("H_far1"):
        across_far(1)
    with phase("H_ax3"):
        across(3)
    with phase("H_fold1"):
        fold(1)
    with phase("H_ar2"):
        across_relay(2)
    with phase("H_ar3"):
        across_relay(3)
    with phase("H_far2"):
        across_far(2)
    with phase("H_fold2"):
        fold(2)
        acc_to_hbm.start()
    with phase("H_far"):
        across_far(3)
        grad_to_hbm.start()
        away = (z // 2 + NX - x) % NX
        odd, side = away % 2, away // 2
        for half in range(2):
            k = odd * (1 + (half + side + 1) % 2) + (1 - odd) * 3 * side
            p = odd * (1 - side) + (1 - odd) * half
            share_out[16 * half : 16 * half + 16, :] = grad_out[k, y, p, z % 2]
        share_to_hbm.start()
        share_to_hbm.wait()
        grad_to_hbm.wait()
        feat_to_hbm.wait()
        acc_to_hbm.wait()

    with phase("H_drain"):
        there = at.partner()
        for step in range(NX):
            remote(
                pr.at[step], pr.at[step], pair_s.at[step], pair_r.at[step, 0], there
            ).wait_send()
        for k in range(3):
            remote(rl, rl, sb_s.at[k], rl_r.at[0], there).wait_send()
        for k, like in enumerate(
            (
                fall.at[0:7], gbuf.at[0:7], stat.at[0:3], rf.at[0:7],
                srow.at[0:7], stat_v.at[0:31], dot_v.at[0:31],
                zbuf.at[0:7], xall.at[0:3], ysb, grad_out.at[0:3], zbuf.at[0:7],
            )
        ):
            Group(group_sems.at[k]).drain(like, there)
        for k in range(4):
            remote(
                qs.at[k, 0:7], zrs.at[k, 0:7], zs_s.at[k], zs_r.at[k], there
            ).wait_send()
            remote(seven(k), seven(k), az_s.at[k], a_z.at[k], there).wait_send()


VMEM = pl.BlockSpec(memory_space=pltpu.VMEM)
HBM = pl.BlockSpec(memory_space=pl.ANY)
LIMIT = 60 * 1024 * 1024


def call(*operands):
    return pl.pallas_call(
        kernel,
        out_shape=(
            jax.ShapeDtypeStruct((32, 1024), BF16),
            jax.ShapeDtypeStruct((1024, 768), F32),
            jax.ShapeDtypeStruct((NY, 2, 2, 16, 1024), BF16),
            jax.ShapeDtypeStruct((NY, 2, 2, 16, 768), BF16),
        ),
        in_specs=[HBM] * 7,
        out_specs=[HBM] * 4,
        scratch_shapes=[
            pltpu.VMEM((128, 256), BF16),
            pltpu.VMEM((1, 128), jnp.int32),
            pltpu.VMEM((1, 128), jnp.int32),
            pltpu.VMEM((128, 768), BF16),
            pltpu.VMEM((8, 8, 128), F32),
            pltpu.VMEM((32, 1024), BF16),
            pltpu.VMEM((1024, 768), F32),
            pltpu.VMEM((4, NY, 2, 2, 16, 1024), BF16),
            pltpu.VMEM((4, NY, 2, 2, 16, 768), BF16),
            pltpu.VMEM((8, 2, 64, 768), BF16),
            pltpu.VMEM((2048, 1024), BF16),
            pltpu.VMEM((128, 2048), BF16),
            pltpu.VMEM((NZ, 128, 256), BF16),
            pltpu.VMEM((NY, 8, 128, 256), BF16),
            pltpu.VMEM((1024, 1024), BF16),
            pltpu.VMEM((NY, 8, 128), F32),
            pltpu.VMEM((8, 128, 128), F32),
            pltpu.VMEM((8, 128, 128), F32),
            pltpu.VMEM((8, 8, 128), F32),
            pltpu.VMEM((8, 8, 128), F32),
            pltpu.VMEM((1, 1024), F32),
            pltpu.VMEM((NX, 8, 2, 128, 256), F32),
            pltpu.VMEM((NX, 8, 128, 256), F32),
            pltpu.VMEM((8, 3, 272, 128), BF16),
            pltpu.VMEM((8, 272, 128), BF16),
            pltpu.VMEM((8, 2, 272, 128), BF16),
            pltpu.VMEM((8, 128, 256), F32),
            pltpu.VMEM((8, 128), F32),
            pltpu.VMEM((32, 8, 128), F32),
            pltpu.VMEM((32, 8, 128), F32),
            pltpu.VMEM((8, 2, 64, 2048), BF16),
            pltpu.VMEM((4, NY, 2, 2, 16, 1024), F32),
            pltpu.VMEM((4, 3, 2, 2, 16, 1024), BF16),
            pltpu.VMEM((4, 2, 2, 16, 1024), BF16),
            pltpu.VMEM((4, 2, 2, 2, 16, 1024), BF16),
            pltpu.VMEM((4, NZ, 2, 2, 16, 128), F32),
            pltpu.VMEM((4, NZ, 2, 2, 16, 128), BF16),
            pltpu.VMEM((4, NZ, 2, 2, 16, 128), BF16),
            DMA((11,)),
            DMA((12,)),
            DMA((2, NZ)),
            DMA((1,)),
            DMA((8,)),
            DMA((2, 8)),
            DMA((8,)),
            DMA((1,)),
            DMA((1,)),
            DMA((2, 2)),
            DMA((2,)),
            DMA((4, 2)),
            DMA((NX,)),
            DMA((NX, 8)),
            DMA((3,)),
            DMA((8,)),
            DMA((8, 2)),
            DMA((1,)),
            DMA((1,)),
            DMA((1,)),
            DMA((2, 2)),
            DMA((2,)),
            DMA((4, 2)),
            DMA((4,)),
            DMA((4, 2)),
            DMA((4,)),
            DMA((4,)),
            DMA((4,)),
            DMA((4,)),
            DMA((2, 4, 2)),
            DMA((2, 4)),
        ],
        compiler_params=pltpu.CompilerParams(
            collective_id=0, has_side_effects=True, vmem_limit_bytes=LIMIT
        ),
    )(*operands)


def body(hidden, norm_gain, head_weight, target_logits, valid_rows, parents, features):
    share, joined, grad, parent_features = call(
        hidden,
        valid_rows.reshape(1, 128),
        parents.reshape(1, 128),
        features,
        norm_gain.reshape(8, 8, 128),
        head_weight,
        target_logits,
    )
    grad_joining = joined + lax.dot_general(
        *lax.optimization_barrier(
            (grad.reshape(256, 1024), parent_features.reshape(256, 768))
        ),
        (((0,), (0,)), ((), ())),
        preferred_element_type=F32,
    )
    return (share, grad_joining)


def solution(mesh):
    placed = (
        P("dp", "vocab"),
        P(),
        P("vocab", "dp"),
        P("dp", "vocab"),
        P("dp"),
        P("dp"),
        P("dp", "vocab"),
    )
    return jax.shard_map(
        body,
        mesh=mesh,
        in_specs=placed,
        out_specs=(P("vocab", "dp"), P("dp", "vocab")),
        check_vma=False,
    )
```

```python
import contextlib

import jax
import jax.numpy as jnp
from jax import lax
from jax.experimental import pallas as pl
from jax.experimental.pallas import tpu as pltpu
from jax.sharding import PartitionSpec as P

TREE = 64
NX, NC, NY, NZ = 4, 2, 4, 8
F32, BF16 = jnp.float32, jnp.bfloat16
DMA = pltpu.SemaphoreType.DMA


def remote(src, dst, send_sem, recv_sem, device):
    return pltpu.make_async_remote_copy(
        src_ref=src,
        dst_ref=dst,
        send_sem=send_sem,
        recv_sem=recv_sem,
        device_id=device,
        device_id_type=pl.DeviceIdType.MESH,
    )


def phase(name):
    return contextlib.nullcontext()


class Place:
    def __init__(self):
        self.g = lax.axis_index("dp")
        self.v = lax.axis_index("vocab")
        self.x, self.c = self.g // NC, self.g % NC
        self.z, self.y = self.v // NY, self.v % NY

    def dp(self, i):
        return (i, self.v)

    def at_x(self, x):
        return (x * NC + self.c, self.v)

    def partner(self):
        return (self.x * NC + 1 - self.c, self.v)

    def at_y(self, y):
        return (self.g, self.z * NY + y)

    def at_z(self, z):
        return (self.g, z * NY + self.y)


class Group:
    def __init__(self, sem):
        self.sem = sem

    def __call__(self, src, dst, recv_sem, device):
        remote(src, dst, self.sem, recv_sem, device).start()

    def drain(self, like, device):
        remote(like, like, self.sem, self.sem, device).wait_send()


def arrived(dst, recv_sem, device, any_sem):
    remote(dst, dst, any_sem, recv_sem, device).wait_recv()


class Gather:
    def __init__(self, at, buf, send, near, far, pair):
        self.at, self.buf, self.send = at, buf, send
        self.near, self.far, self.pair = near, far, pair

    def slot(self, step, core):
        return ((self.at.x + step) % NX) * NC + core

    def start(self):
        at, buf = self.at, self.buf
        up, down = at.at_x((at.x + 1) % NX), at.at_x((at.x + 3) % NX)
        for k in range(2):
            for side, half, device in ((0, k, up), (1, 1 - k, down)):
                mine = buf.at[at.g, half]
                self.send(mine, mine, self.near.at[side, half], device)
            mine = buf.at[at.g, k]
            self.send(mine, mine, self.pair.at[0, k], at.partner())

    def middle(self, first):
        at, buf = self.at, self.buf
        for side, step in ((0, 3), (1, 1)):
            half = side if first else 1 - side
            block = buf.at[self.slot(step, at.c), half]
            arrived(block, self.near.at[side, half], at.partner(), self.near.at[side, half])
            if first:
                onward = at.at_x((at.x + (1 if side == 0 else 3)) % NX)
                self.send(block, block, self.far.at[half], onward)
            self.send(block, block, self.pair.at[step, half], at.partner())

    def last(self):
        at, buf = self.at, self.buf
        for half in range(2):
            block = buf.at[self.slot(2, at.c), half]
            arrived(block, self.far.at[half], at.partner(), self.far.at[half])
            self.send(block, block, self.pair.at[2, half], at.partner())

    def paired(self, step, half):
        at = self.at
        block = self.buf.at[self.slot(step, 1 - at.c), half]
        arrived(block, self.pair.at[step, half], at.partner(), self.pair.at[step, half])


def row_tile(column):
    return jnp.transpose(jnp.broadcast_to(column, (128, 128)))[0:8]


def column_tile(row):
    return jnp.transpose(jnp.broadcast_to(row, (128, 128)))


def stack_rows(*rows):
    index = lax.broadcasted_iota(jnp.int32, (8, 128), 0)
    tile = jnp.zeros((8, 128), F32)
    for k, row in enumerate(rows):
        tile = jnp.where(index == k, row, tile)
    return tile


def kernel(
    hid_hbm, valid_hbm, parents_hbm, feat_hbm_in, gains_hbm, weight_hbm, targets_hbm,
    share_hbm, joined_hbm, grad_hbm, feat_hbm,
    hid, valid, parents, feat, gains, share_out,
    joined, grad_out, feat_out, fall,
    weight, targets, zbuf, xall, normed, stat, cols, scols, rf, srow, gain,
    pk, pr, sb, rl, fin, lg, tst, stat_v, dot_v, gbuf, pf, ysb, yrl, yfin,
    qf, qs, zrs,
    local_sems, group_sems, zr, xs, xr, yr, y2, sr, fr,
    f_near, f_far, f_pair,
    pair_s, pair_r, sb_s, rl_r, fin_r,
    sv_r, dv_r, sd_r, g_near, g_far, g_pair,
    yrl_r, yfin_r, zs_s, zs_r, az_s, a_z, a_y, a_y2,
):
    at = Place()
    x, c, y, z, g, v = at.x, at.c, at.y, at.z, at.g, at.v
    up_z, down_z = at.at_z((z + 1) % NZ), at.at_z((z + NZ - 1) % NZ)
    up_y, down_y = at.at_y((y + 1) % NY), at.at_y((y + 3) % NY)

    loads = [
        pltpu.make_async_copy(src, dst, local_sems.at[5 + k])
        for k, (src, dst) in enumerate(
            (
                (hid_hbm, hid),
                (parents_hbm, parents),
                (feat_hbm_in, feat),
                (valid_hbm, valid),
                (gains_hbm, gains),
            )
        )
    ]
    for load in loads:
        load.start()
    load_weight = pltpu.make_async_copy(weight_hbm, weight, local_sems.at[0])
    load_targets = pltpu.make_async_copy(targets_hbm, targets, local_sems.at[1])
    load_weight.start()
    load_targets.start()

    with phase("A_feat"):
        barrier = pltpu.get_barrier_semaphore()

        @pl.loop(1, 32)
        def _(k):
            pl.semaphore_signal(
                barrier,
                inc=1,
                device_id=(g, (v + k) % 32),
                device_id_type=pl.DeviceIdType.MESH,
            )

        @pl.loop(1, 8)
        def _(k):
            pl.semaphore_signal(
                barrier,
                inc=1,
                device_id=((g + k) % 8, v),
                device_id_type=pl.DeviceIdType.MESH,
            )

    with phase("A_load"):
        for load in loads:
            load.wait()
    with phase("A_own"):
        live = (valid[...] == 1).astype(F32)
        row = lax.broadcasted_iota(jnp.int32, (128, 128), 0)
        lane = lax.broadcasted_iota(jnp.int32, (128, 128), 1)
        wanted = column_tile(parents[...].astype(F32)).astype(jnp.int32) + row // TREE * TREE
        pick = (lane == wanted).astype(BF16)
        chosen = jnp.dot(pick, feat[...], preferred_element_type=F32).astype(BF16)
        fall[g, 0] = chosen[:64]
        fall[g, 1] = chosen[64:]
        own_gain = gains[g]
        gain[...] = jnp.concatenate([own_gain[k : k + 1] for k in range(8)], axis=1)

    with phase("A_greet"):
        pl.semaphore_wait(barrier, 38)
    send_z, send_y = Group(group_sems.at[7]), Group(group_sems.at[8])
    send_part, send_grad = Group(group_sems.at[9]), Group(group_sems.at[10])
    send_x = Group(group_sems.at[11])
    spread = Gather(at, fall, Group(group_sems.at[0]), f_near, f_far, f_pair)

    def to_slice(src, j):
        @pl.when(j != g)
        def _():
            send_x(src, xall.at[y, g], xr.at[g], at.dp(j))

        @pl.when(j == g)
        def _():
            pltpu.make_async_copy(src, xall.at[y, g], xs.at[0]).start()

    def piece(ref, q):
        return ref.at[64 * q : 64 * q + 64]

    with phase("A_z"):
        for q in range(2):
            send_z(piece(hid, q), piece(zbuf.at[z], q), zr.at[q, z], up_z)
            send_z(piece(hid, q), piece(zbuf.at[z], q), zr.at[q, z], down_z)
        to_slice(hid, z)
        spread.start()
        for step in range(1, 5):
            low, high = (z + NZ - step) % NZ, (z + step) % NZ
            for q in range(2):
                block = piece(zbuf.at[low], q)
                arrived(block, zr.at[q, low], up_z, zr.at[q, low])
                if step < 4:
                    send_z(block, block, zr.at[q, low], up_z)
                    block = piece(zbuf.at[high], q)
                    arrived(block, zr.at[q, high], up_z, zr.at[q, high])
                    if step < 3:
                        send_z(block, block, zr.at[q, high], down_z)
            to_slice(zbuf.at[low], low)
            if step < 4:
                to_slice(zbuf.at[high], high)

    with phase("A_stat"):
        small = Group(group_sems.at[2])
        squares = jnp.square(hid[...].astype(F32))
        for k in range(1, NZ):
            squares = squares + jnp.square(zbuf[(z + k) % NZ].astype(F32))
        stat[y] = row_tile(jnp.sum(squares, axis=1, keepdims=True))
        for k in range(1, NY):
            small(stat.at[y], stat.at[y], sr.at[0], at.at_y((y + k) % NY))

    turns = (2, 1, 3, 0)

    def group(k):
        return 2 * ((x + turns[k // 2]) % NX) + k % 2

    def y_send(k):
        block = xall.at[y, group(k)]
        sem = xr.at[group(k)]
        if k < 6:
            arrived(block, sem, up_y, sem)
        else:

            @pl.when(c != k % 2)
            def _():
                arrived(block, sem, up_y, sem)

            @pl.when(c == k % 2)
            def _():
                pltpu.make_async_copy(hid, block, xs.at[0]).wait()

        send_y(block, block, yr.at[0, k], up_y)
        send_y(block, block, yr.at[1, k], down_y)

    def y_relay(k):
        for side, step in ((0, 3), (1, 1)):
            block = xall.at[(y + step) % NY, group(k)]
            arrived(block, yr.at[side, k], up_y, yr.at[side, k])
            if k % 2 == side:
                send_y(block, block, y2.at[k], up_y if side == 0 else down_y)
        if k + 3 < 8:
            y_send(k + 3)

    def y_far(k):
        block = xall.at[(y + 2) % NY, group(k)]
        arrived(block, y2.at[k], up_y, y2.at[k])

    def normalise(k):
        i = group(k)
        scale = cols[i]
        scale = jnp.concatenate([scale, scale], axis=1)
        rows = pl.ds(pl.multiple_of(i * 128, 128), 128)
        for part in range(NY):
            columns = slice(part * 256, part * 256 + 256)
            values = xall[part, i].astype(F32)
            normed[rows, columns] = (values * scale * gain[:, columns]).astype(BF16)

    def pair_copy(step, t):
        return remote(
            pk.at[step, t, 1 - c], pr.at[step, t],
            pair_s.at[step], pair_r.at[step, t], at.partner(),
        )

    def multiply(step, t):
        rows = pl.ds(pl.multiple_of(((x + step) % NX) * 256, 256), 256)
        tile = pl.ds(pl.multiple_of(t * 256, 256), 256)
        part = lax.dot_general(
            normed[rows, :],
            weight[tile, :],
            (((1,), (1,)), ((), ())),
            preferred_element_type=F32,
        )
        pk[step, t, 0] = part[:128]
        pk[step, t, 1] = part[128:]
        pair_copy(step, t).start()

    def total_of(step, t):
        arrived(pr.at[step, t], pair_r.at[step, t], at.partner(), pair_r.at[step, t])
        return pk[step, t, c] + pr[step, t]

    def ways(t):
        way = 1 + 2 * (t % 2)
        return way, 4 - way

    def first_hop(t):
        ahead, _ = ways(t)
        return remote(sb.at[t, 0], rl.at[t], sb_s.at[0], rl_r.at[t], at.at_x((x + ahead) % NX))

    def direct(t):
        _, back = ways(t)
        return remote(
            sb.at[t, 1], fin.at[t, 0], sb_s.at[1], fin_r.at[t, 0], at.at_x((x + back) % NX)
        )

    def onward(t):
        ahead, _ = ways(t)
        return remote(
            sb.at[t, 2], fin.at[t, 1], sb_s.at[2], fin_r.at[t, 1], at.at_x((x + ahead) % NX)
        )

    def encode(t, k, value):
        left, right = value[:, :128], value[:, 128:]
        top = jnp.max(jnp.maximum(jnp.abs(left), jnp.abs(right)), axis=0, keepdims=True)
        step = (120.0 / jnp.maximum(top, 1e-30)).astype(BF16)
        sb[t, k, 256:] = jnp.broadcast_to(step, (16, 128))
        step = sb[t, k, 256:].astype(F32)[0:1]
        sb[t, k, :128] = jnp.exp2(left * step).astype(BF16)
        sb[t, k, 128:256] = jnp.exp2(right * step).astype(BF16)

    def decode(block):
        size = 1.0 / block[256:].astype(F32)[0:1]
        return jnp.concatenate(
            [
                jnp.log2(block[:128].astype(F32)) * size,
                jnp.log2(block[128:256].astype(F32)) * size,
            ],
            axis=1,
        )

    with phase("A_ysend"):
        for k in range(3):
            y_send(k)

    with phase("A_rf"):
        arrived(stat.at[0:3], sr.at[0], up_y, sr.at[0])
        total = stat[y]
        for k in range(1, NY):
            total = total + stat[(y + k) % NY]
        factor = lax.rsqrt(total / (1024.0 * 8) + 1e-05)
        rf[g] = stack_rows(factor[0:1], live)
        factors = Group(group_sems.at[3])
        for k in range(1, 8):
            factors(rf.at[g], rf.at[g], fr.at[0], at.dp((g + k) % 8))

    with phase("A_y0123"):
        y_relay(0)
        y_relay(1)
        spread.middle(True)
        y_relay(2)
        arrived(rf.at[0:7], fr.at[0], up_y, fr.at[0])
        for i in range(8):
            cols[i] = column_tile(rf[i, 0:1])
        y_relay(3)
        load_weight.wait()
        load_targets.wait()
    with phase("A_far01"):
        y_far(0)
        y_far(1)
        normalise(0)
        normalise(1)
    def run(low, high, *stages):
        @pl.loop(low, high)
        def _(t):
            for stage, lag in stages:
                stage(t - lag)

    def hop(t):
        encode(t, 0, total_of(2, t))
        first_hop(t).start()

    with phase("F_hop"):
        far_rows = (lambda t: multiply(2, t)), 0
        run(0, 3, far_rows)
        run(3, 6, far_rows, (hop, 3))
        y_relay(4)
        run(6, 8, far_rows, (hop, 3))
        y_relay(5)
        run(5, 8, (hop, 0))
    with phase("A_y6"):
        y_relay(6)
    with phase("A_far2345"):
        for k in range(2, 6):
            y_far(k)
            normalise(k)
    with phase("F_both"):

        def both(t):
            ahead, back = ways(t)
            encode(t, 1, total_of(back, t))
            direct(t).start()
            arrived(rl.at[t], rl_r.at[t], at.partner(), rl_r.at[t])
            encode(t, 2, total_of(ahead, t) + decode(rl.at[t]))
            onward(t).start()

        def near_rows(t):
            multiply(1, t)
            multiply(3, t)

        run(0, 3, (near_rows, 0))
        run(3, 5, (near_rows, 0), (both, 3))
        y_relay(7)
        run(5, 8, (near_rows, 0), (both, 3))
        run(5, 8, (both, 0))

    with phase("A_far67"):
        spread.middle(False)
        top = jnp.max(targets[...].astype(F32), axis=1, keepdims=True)
        part = jnp.zeros((128, 256), F32)
        for k in range(8):
            part = part + jnp.exp(targets[:, k * 256 : k * 256 + 256].astype(F32) - top)
        tst[...] = stack_rows(
            jnp.zeros((1, 128), F32),
            jnp.zeros((1, 128), F32),
            row_tile(top)[0:1],
            row_tile(jnp.sum(part, axis=1, keepdims=True))[0:1],
        )
        for k in range(6, 8):
            y_far(k)
            normalise(k)

    def finish(t):
        own = total_of(0, t)
        for k in range(2):
            arrived(fin.at[t, k], fin_r.at[t, k], at.partner(), fin_r.at[t, k])
        lg[t] = own + decode(fin.at[t, 0]) + decode(fin.at[t, 1])

    with phase("F_fin"):
        own_rows = (lambda t: multiply(0, t)), 0
        run(0, 3, own_rows)
        run(3, 8, own_rows, (finish, 3))
        run(5, 8, (finish, 0))

    def tell_all(tile, send_sem, recv_sem):
        @pl.loop(1, 32)
        def _(k):
            remote(
                tile.at[v], tile.at[v], send_sem, recv_sem.at[0], (g, (v + k) % 32)
            ).start()

    def hear_all(tile, recv_sem):
        arrived(tile.at[0:31], recv_sem.at[0], up_y, recv_sem.at[0])

    with phase("B_stat"):
        top = lg[0]
        for t in range(1, 8):
            top = jnp.maximum(top, lg[t])
        top = jnp.max(top, axis=1, keepdims=True)
        part = jnp.zeros((128, 256), F32)
        for t in range(8):
            part = part + jnp.exp(lg[t] - top)
        stat_v[v] = stack_rows(
            row_tile(top)[0:1],
            row_tile(jnp.sum(part, axis=1, keepdims=True))[0:1],
            tst[2:3],
            tst[3:4],
        )
        tell_all(stat_v, group_sems.at[5], sv_r)

    with phase("B_statv"):
        hear_all(stat_v, sv_r)
        wide = lambda row: jnp.concatenate([column_tile(row)] * 2, axis=1)
        tops, scales = [], []
        for k in (0, 2):
            top = jnp.max(stat_v[:, k, :], axis=0, keepdims=True)
            part = stat_v[:, k + 1, :] * jnp.exp(stat_v[:, k, :] - top)
            tops.append(wide(top))
            scales.append(wide(1.0 / jnp.sum(part, axis=0, keepdims=True)))
        count = jnp.zeros((1, 128), F32)
        for i in range(8):
            count = count + rf[i, 1:2]
        count = jnp.sum(count, axis=1, keepdims=True)
        scale = wide(1048576.0 * live / count)

    gather = Gather(at, gbuf, Group(group_sems.at[1]), g_near, g_far, g_pair)
    with phase("B_G"):
        acc = jnp.zeros((128, 256), F32)
        for t in range(8):
            draft = jnp.exp(lg[t] - tops[0]) * scales[0]
            target = (
                jnp.exp(targets[:, t * 256 : t * 256 + 256].astype(F32) - tops[1]) * scales[1]
            )
            value = (scale * (draft - target)).astype(BF16)
            for k in range(8):
                gbuf[g, k % 2, k // 2 * 16 : k // 2 * 16 + 16, t * 256 : t * 256 + 256] = value[
                    k * 16 : k * 16 + 16
                ]
            acc = acc + value.astype(F32) * lg[t]
        gather.start()
        dot_v[v] = row_tile(jnp.sum(acc, axis=1, keepdims=True))
        tell_all(dot_v, group_sems.at[6], dv_r)

    units = (((0, 0), (0, 1)), ((3, 0), (1, 1)), ((3, 1), (1, 0)), ((2, 0), (2, 1)))

    def block_of(step):
        return (x + step) % NX

    def backward(k):
        for step, half in units[k]:
            gather.paired(step, half)

        @pl.loop(0, 4)
        def _(n):
            columns = pl.ds(pl.multiple_of(n * 256, 256), 256)
            rows = jnp.concatenate(
                [
                    gbuf[pl.ds(2 * block_of(step), 2), half].reshape(128, 2048)
                    for step, half in units[k]
                ],
                axis=0,
            )
            part = jnp.dot(rows, weight[:, columns], preferred_element_type=F32)
            for p in range(2):
                for which in range(2):
                    for dest in range(NY):
                        row = p * 128 + which * 64 + dest * 16
                        pf[k, dest, p, which, :, columns] = part[row : row + 16]

        way = 1 if k % 2 == 0 else 3
        ysb[k, 0] = pf[k, (y + 2) % NY].astype(BF16)
        send_part(ysb.at[k, 0], yrl.at[k], yrl_r.at[k], at.at_y((y + way) % NY))
        ysb[k, 1] = pf[k, (y + 4 - way) % NY].astype(BF16)
        send_part(ysb.at[k, 1], yfin.at[k, 0], yfin_r.at[k, 0], at.at_y((y + 4 - way) % NY))

    def y_second(k):
        way = 1 if k % 2 == 0 else 3
        arrived(yrl.at[k], yrl_r.at[k], up_y, yrl_r.at[k])
        ysb[k, 2] = (pf[k, (y + way) % NY] + yrl[k].astype(F32)).astype(BF16)
        send_part(ysb.at[k, 2], yfin.at[k, 1], yfin_r.at[k, 1], at.at_y((y + way) % NY))

    def z_send(k, dest):
        return remote(
            qs.at[k, dest], zrs.at[k, z], zs_s.at[k], zs_r.at[k], at.at_z(dest)
        )

    far_first = (4, 3, 5, 2, 6, 1, 7)

    def y_third(k):
        for j in range(2):
            arrived(yfin.at[k, j], yfin_r.at[k, j], up_y, yfin_r.at[k, j])
        value = pf[k, y] + yfin[k, 0].astype(F32) + yfin[k, 1].astype(F32)
        for owner in range(NZ):
            part = value[:, :, :, 128 * owner : 128 * owner + 128]
            qf[k, owner] = part
            qs[k, owner] = part.astype(BF16)
        for shift in far_first:
            z_send(k, (z + shift) % NZ).start()

    own_columns = pl.ds(pl.multiple_of(z * 128, 128), 128)

    def piece_of(k, owner):
        columns = pl.ds(pl.multiple_of(owner * 128, 128), 128)
        return grad_out.at[k, y, :, :, :, columns]

    def seven(k):
        return grad_out.at[k, y, :, :, :, 0:896]

    def z_fourth(k):
        total = qf[k, z]
        arrived(zrs.at[k, 0:7], zs_r.at[k], up_y, zs_r.at[k])
        for j in range(1, NZ):
            total = total + zrs[k, (z + j) % NZ].astype(F32)
        lanes = pl.ds(pl.multiple_of((z % 2) * 128, 128), 128)
        for p, (step, half) in enumerate(units[k]):
            rows = pl.ds(pl.multiple_of(y * 32 + half * 16, 16), 16)
            for which in range(2):
                i = 2 * block_of(step) + which
                values = xall[z // 2, i, rows, lanes].astype(F32)
                grad = cols[i, rows, :] * gain[:, own_columns] * total[p, which]
                grad = grad - values * scols[i, rows, :]
                grad_out[k, y, p, which, :, own_columns] = grad.astype(BF16)
        mine = piece_of(k, z)
        for shift in far_first:
            remote(mine, mine, az_s.at[k], a_z.at[k], at.at_z((z + shift) % NZ)).start()

    def across(k):
        arrived(seven(k), a_z.at[k], up_y, a_z.at[k])
        for turn in range(2):
            for side, device in ((0, up_y), (1, down_y)):
                p = side if turn == 0 else 1 - side
                mine = grad_out.at[k, y, p]
                send_grad(mine, mine, a_y.at[side, k, p], device)

    def across_near(k, side, p):
        half = grad_out.at[k, (y + (3 if side == 0 else 1)) % NY, p]
        arrived(half, a_y.at[side, k, p], up_y, a_y.at[side, k, p])
        return half

    def across_relay(k):
        for side in range(2):
            half = across_near(k, side, side)
            send_grad(half, half, a_y2.at[side, k], up_y if side == 0 else down_y)

    grad_to_hbm = pltpu.make_async_copy(grad_out.at[3], grad_hbm, local_sems.at[2])
    feat_to_hbm = pltpu.make_async_copy(feat_out.at[3], feat_hbm, local_sems.at[3])
    share_to_hbm = pltpu.make_async_copy(share_out, share_hbm, local_sems.at[10])
    acc_to_hbm = pltpu.make_async_copy(joined, joined_hbm, local_sems.at[4])

    def fold(k):
        @pl.loop(0, 4)
        def _(n):
            columns = pl.ds(pl.multiple_of(n * 256, 256), 256)
            part = lax.dot_general(
                grad_out[k, :, :, :, :, columns].reshape(256, 256),
                feat_out[k].reshape(256, 768),
                (((0,), (0,)), ((), ())),
                preferred_element_type=F32,
            )
            if k == 0:
                joined[columns, :] = part
            else:
                joined[columns, :] += part

    def across_far(k):
        for side in range(2):
            across_near(k, side, 1 - side)
        for side in range(2):
            half = grad_out.at[k, (y + 2) % NY, side]
            arrived(half, a_y2.at[side, k], up_y, a_y2.at[side, k])

    with phase("G_bw0"):
        backward(0)
    with phase("G_feat"):
        spread.last()
        for step in (0, 1, 3):
            for half in range(2):
                spread.paired(step, half)
    with phase("G_mid"):
        gather.middle(True)
    with phase("G_ys0"):
        y_second(0)
    with phase("G_dot"):
        hear_all(dot_v, dv_r)
        dot = jnp.sum(dot_v[:, 0, :], axis=0, keepdims=True)
        factor = rf[g][0:1]
        srow[g] = jnp.broadcast_to(factor * factor * dot / (1024.0 * 8), (8, 128))
        pulls = Group(group_sems.at[4])
        for k in range(1, 8):
            pulls(srow.at[g], srow.at[g], sd_r.at[0], at.dp((g + k) % 8))
    with phase("G_bw1"):
        backward(1)
    with phase("G_yt0"):
        y_third(0)
    with phase("G_mid2"):
        gather.middle(False)
    with phase("G_ys1"):
        y_second(1)
    with phase("G_bw2"):
        backward(2)
    with phase("G_s"):
        arrived(srow.at[0:7], sd_r.at[0], up_y, sd_r.at[0])
        for i in range(8):
            scols[i] = column_tile(srow[i, 0:1])
    with phase("G_z0"):
        z_fourth(0)
    with phase("G_last"):
        gather.last()
    with phase("G_yt1"):
        y_third(1)
    with phase("G_bw3"):
        backward(3)
    with phase("G_ys2"):
        y_second(2)
    with phase("H_feat"):
        spread.paired(2, 0)
        spread.paired(2, 1)
        for k in range(4):
            for p, (step, half) in enumerate(units[k]):
                for which in range(2):
                    for dest in range(NY):
                        row = dest % 2 * 32 + half * 16
                        feat_out[k, dest, p, which] = fall[
                            2 * block_of(step) + which, dest // 2, row : row + 16, :
                        ]
        feat_to_hbm.start()
    with phase("G_ys3"):
        y_second(3)
    with phase("H_ax0"):
        across(0)
    with phase("H_z1"):
        z_fourth(1)
    with phase("G_yt2"):
        y_third(2)
    with phase("H_ax1"):
        across(1)
    with phase("G_yt3"):
        y_third(3)
    with phase("H_ar0"):
        across_relay(0)
    with phase("H_z2"):
        z_fourth(2)
    with phase("H_far0"):
        across_far(0)
    with phase("H_ar1"):
        across_relay(1)
    with phase("H_z3"):
        z_fourth(3)
    with phase("H_fold0"):
        fold(0)
    with phase("H_ax2"):
        across(2)
    with phase("H_far1"):
        across_far(1)
    with phase("H_ax3"):
        across(3)
    with phase("H_fold1"):
        fold(1)
    with phase("H_ar2"):
        across_relay(2)
    with phase("H_ar3"):
        across_relay(3)
    with phase("H_far2"):
        across_far(2)
    with phase("H_fold2"):
        fold(2)
        acc_to_hbm.start()
    with phase("H_far"):
        across_far(3)
        grad_to_hbm.start()
        away = (z // 2 + NX - x) % NX
        odd, side = away % 2, away // 2
        for half in range(2):
            k = odd * (1 + (half + side + 1) % 2) + (1 - odd) * 3 * side
            p = odd * (1 - side) + (1 - odd) * half
            share_out[16 * half : 16 * half + 16, :] = grad_out[k, y, p, z % 2]
        share_to_hbm.start()
        share_to_hbm.wait()
        grad_to_hbm.wait()
        feat_to_hbm.wait()
        acc_to_hbm.wait()

    with phase("H_drain"):
        there = at.partner()
        for step in range(NX):
            remote(
                pr.at[step], pr.at[step], pair_s.at[step], pair_r.at[step, 0], there
            ).wait_send()
        for k in range(3):
            remote(rl, rl, sb_s.at[k], rl_r.at[0], there).wait_send()
        for k, like in enumerate(
            (
                fall.at[0:7], gbuf.at[0:7], stat.at[0:3], rf.at[0:7],
                srow.at[0:7], stat_v.at[0:31], dot_v.at[0:31],
                zbuf.at[0:7], xall.at[0:3], ysb, grad_out.at[0:3], zbuf.at[0:7],
            )
        ):
            Group(group_sems.at[k]).drain(like, there)
        for k in range(4):
            remote(
                qs.at[k, 0:7], zrs.at[k, 0:7], zs_s.at[k], zs_r.at[k], there
            ).wait_send()
            remote(seven(k), seven(k), az_s.at[k], a_z.at[k], there).wait_send()


VMEM = pl.BlockSpec(memory_space=pltpu.VMEM)
HBM = pl.BlockSpec(memory_space=pl.ANY)
LIMIT = 60 * 1024 * 1024


def call(*operands):
    return pl.pallas_call(
        kernel,
        out_shape=(
            jax.ShapeDtypeStruct((32, 1024), BF16),
            jax.ShapeDtypeStruct((1024, 768), F32),
            jax.ShapeDtypeStruct((NY, 2, 2, 16, 1024), BF16),
            jax.ShapeDtypeStruct((NY, 2, 2, 16, 768), BF16),
        ),
        in_specs=[HBM] * 7,
        out_specs=[HBM] * 4,
        scratch_shapes=[
            pltpu.VMEM((128, 256), BF16),
            pltpu.VMEM((1, 128), jnp.int32),
            pltpu.VMEM((1, 128), jnp.int32),
            pltpu.VMEM((128, 768), BF16),
            pltpu.VMEM((8, 8, 128), F32),
            pltpu.VMEM((32, 1024), BF16),
            pltpu.VMEM((1024, 768), F32),
            pltpu.VMEM((4, NY, 2, 2, 16, 1024), BF16),
            pltpu.VMEM((4, NY, 2, 2, 16, 768), BF16),
            pltpu.VMEM((8, 2, 64, 768), BF16),
            pltpu.VMEM((2048, 1024), BF16),
            pltpu.VMEM((128, 2048), BF16),
            pltpu.VMEM((NZ, 128, 256), BF16),
            pltpu.VMEM((NY, 8, 128, 256), BF16),
            pltpu.VMEM((1024, 1024), BF16),
            pltpu.VMEM((NY, 8, 128), F32),
            pltpu.VMEM((8, 128, 128), F32),
            pltpu.VMEM((8, 128, 128), F32),
            pltpu.VMEM((8, 8, 128), F32),
            pltpu.VMEM((8, 8, 128), F32),
            pltpu.VMEM((1, 1024), F32),
            pltpu.VMEM((NX, 8, 2, 128, 256), F32),
            pltpu.VMEM((NX, 8, 128, 256), F32),
            pltpu.VMEM((8, 3, 272, 128), BF16),
            pltpu.VMEM((8, 272, 128), BF16),
            pltpu.VMEM((8, 2, 272, 128), BF16),
            pltpu.VMEM((8, 128, 256), F32),
            pltpu.VMEM((8, 128), F32),
            pltpu.VMEM((32, 8, 128), F32),
            pltpu.VMEM((32, 8, 128), F32),
            pltpu.VMEM((8, 2, 64, 2048), BF16),
            pltpu.VMEM((4, NY, 2, 2, 16, 1024), F32),
            pltpu.VMEM((4, 3, 2, 2, 16, 1024), BF16),
            pltpu.VMEM((4, 2, 2, 16, 1024), BF16),
            pltpu.VMEM((4, 2, 2, 2, 16, 1024), BF16),
            pltpu.VMEM((4, NZ, 2, 2, 16, 128), F32),
            pltpu.VMEM((4, NZ, 2, 2, 16, 128), BF16),
            pltpu.VMEM((4, NZ, 2, 2, 16, 128), BF16),
            DMA((11,)),
            DMA((12,)),
            DMA((2, NZ)),
            DMA((1,)),
            DMA((8,)),
            DMA((2, 8)),
            DMA((8,)),
            DMA((1,)),
            DMA((1,)),
            DMA((2, 2)),
            DMA((2,)),
            DMA((4, 2)),
            DMA((NX,)),
            DMA((NX, 8)),
            DMA((3,)),
            DMA((8,)),
            DMA((8, 2)),
            DMA((1,)),
            DMA((1,)),
            DMA((1,)),
            DMA((2, 2)),
            DMA((2,)),
            DMA((4, 2)),
            DMA((4,)),
            DMA((4, 2)),
            DMA((4,)),
            DMA((4,)),
            DMA((4,)),
            DMA((4,)),
            DMA((2, 4, 2)),
            DMA((2, 4)),
        ],
        compiler_params=pltpu.CompilerParams(
            collective_id=0, has_side_effects=True, vmem_limit_bytes=LIMIT
        ),
    )(*operands)


def body(hidden, norm_gain, head_weight, target_logits, valid_rows, parents, features):
    share, joined, grad, parent_features = call(
        hidden,
        valid_rows.reshape(1, 128),
        parents.reshape(1, 128),
        features,
        norm_gain.reshape(8, 8, 128),
        head_weight,
        target_logits,
    )
    grad_joining = joined + lax.dot_general(
        *lax.optimization_barrier(
            (grad.reshape(256, 1024), parent_features.reshape(256, 768))
        ),
        (((0,), (0,)), ((), ())),
        preferred_element_type=F32,
    )
    return (share, grad_joining)


def solution(mesh):
    placed = (
        P("dp", "vocab"),
        P(),
        P("vocab", "dp"),
        P("dp", "vocab"),
        P("dp"),
        P("dp"),
        P("dp", "vocab"),
    )
    return jax.shard_map(
        body,
        mesh=mesh,
        in_specs=placed,
        out_specs=(P("vocab", "dp"), P("dp", "vocab")),
        check_vma=False,
    )
```
